128 devices in a mesh: ctx: 32 (over y, x, core), head: 4 (over z).
Axes of the slice: x: 4, y: 4, z: 4, core: 2. Of those that a mesh axis runs over, the one named last changes fastest.
Arguments:
- tokens: bfloat16 [4096, 4096], P('ctx'), may hold values from -8 to 8
- w_query: bfloat16 [4096, 4096], P(None, 'head'), may hold values from -1 to 1
- w_key: bfloat16 [4096, 1024], P(None, 'head'), may hold values from -1 to 1
- w_value: bfloat16 [4096, 1024], P(None, 'head'), may hold values from -0.09375 to 0.09375
- w_out: bfloat16 [4096, 4096], P('head'), may hold values from -0.09375 to 0.09375
- doc_ids: int32 [4096], P('ctx'), may hold values from 0 to 31, never falling along the last dimension, each value on 1 to 2176 neighbouring positions
Outputs:
- mixed: bfloat16 [4096, 4096], P('ctx', 'head')
The draws below stay inside these ranges and needn't reach their ends.
Inputs may be any that keep to these rules, and one draw needn't show every extreme that they name: doc_ids never fall along the context; each document has 1 to 2176 tokens and one has exactly 2176.
All inputs are finite; a program needn't handle non-finite values.
Results may differ from the reference program's by a relative error of at most 0.011.
Values may be sent and summed in bfloat16 or wider, within the bound.
No kernel may reach another device: no remote copies, remote signals or barrier semaphores. Data moves between devices by JAX's collectives and lax.ppermute only.
A program may use at most 128 MiB of HBM per device.

```python
import math
import jax
import jax.numpy as jnp
import numpy as np
from jax import lax

D = 4096
QH = 32
KVH = 8
HD = 128
TOKENS = 4096
DOC_MOST = 2176
DOCS = 32
N_HEAD = 4


def drawn_weight(key, head_count, salt_value):
    entries = jax.random.truncated_normal(jax.random.fold_in(key, salt_value), -6.0, 6.0, (D, head_count * HD), jnp.float32) * D ** (-0.5)
    return entries.astype(jnp.bfloat16)


def draw_w_query(key, part):
    return drawn_weight(key, QH, 11)


def draw_w_key(key, part):
    return drawn_weight(key, KVH, 12)


def draw_tokens(key, part):
    values_drawn = jax.random.truncated_normal(jax.random.fold_in(key, 13), -6.0, 6.0, (TOKENS, D), jnp.float32)
    return values_drawn.astype(jnp.bfloat16)


def level_of(key, extent, shards, smallest, top_value):
    factor_of = 1.0
    for position, parts in shards:
        draws = jax.random.uniform(jax.random.fold_in(jax.random.fold_in(key, 6), position), (parts,), jnp.float32, smallest / len(shards), top_value / len(shards))
        factor_of = factor_of * jnp.repeat(jnp.exp(draws), extent[position] // parts).reshape((-1,) + (1,) * (len(extent) - 1 - position))
    return factor_of


def profile(amount, total, most, skew):
    loads = [(1 << 20) // math.isqrt(rank ** skew) + 1 for rank in range(2, amount + 1)]
    surplus, given = total - most - (amount - 1), [1] * (amount - 1)
    while surplus > 0:
        free = [i for i in range(amount - 1) if given[i] < most]
        whole, left = sum([loads[i] for i in free]), surplus
        for i in free:
            addition = min(most - given[i], max(1, left * loads[i] // whole), surplus)
            given[i] = given[i] + addition
            surplus = surplus - addition
    return np.array([most] + given)


def uneven_parts(key, count, total, bound, skew):
    if count == 2:
        one = jax.random.randint(key, (), max(1, total - bound), min(bound, total - 1) + 1)
        return jnp.stack([one, total - one])
    lengths = jnp.asarray(profile(count, total, bound, skew), jnp.int32)
    twos = (count - 1) // 2
    giver, taker = lengths[1:1 + 2 * twos:2], lengths[2:2 + 2 * twos:2]
    room = jnp.minimum(giver - 1, bound - taker)
    shifted = jax.random.randint(jax.random.fold_in(key, 1), (twos,), 0, 1 << 20) % (room + 1)
    lengths = lengths.at[1:1 + 2 * twos:2].set(giver - shifted).at[2:2 + 2 * twos:2].set(taker + shifted)
    return lengths[jax.random.permutation(jax.random.fold_in(key, 2), count)]


def scatter_about(own_key, extent, deviation, limit, pieces=(), kind=jnp.bfloat16):
    values = jax.random.normal(own_key, extent, jnp.float32) * deviation
    if len(pieces) > 0:
        values = level_of(own_key, extent, pieces, -0.22, 0.18) * values
    return jnp.clip(values, min=-limit, max=limit).astype(kind)


def setup_inputs(seed: int = 0) -> dict:
    key_of = jax.random.split(jax.random.key(seed), 7)
    return {
        "tokens": draw_tokens(jax.random.fold_in(key_of[6], 71), 0),
        "w_query": draw_w_query(jax.random.fold_in(key_of[6], 71), 0),
        "w_key": draw_w_key(jax.random.fold_in(key_of[6], 71), 0),
        "w_value": scatter_about(key_of[3], (D, KVH * HD), D ** -0.5, 0.09375, ((1, 4),)),
        "w_out": scatter_about(key_of[4], (QH * HD, D), (QH * HD) ** -0.5, 0.09375, ((0, 4),)),
        "doc_ids": jnp.searchsorted(jnp.cumsum(uneven_parts(key_of[5], DOCS, TOKENS, DOC_MOST, 2)), jnp.arange(TOKENS), side="right").astype(jnp.int32),
    }


def rotate(vectors, places):
    half_dim = vectors.shape[-1] // 2
    freqs = 500000.0 ** (-2.0 * jnp.arange(half_dim, dtype=jnp.float32) / vectors.shape[-1])
    angles = places.astype(jnp.float32)[:, None] * freqs[None, :]
    cosine = jnp.cos(angles)[:, None, :]
    sine = jnp.sin(angles)[:, None, :]
    first_half = vectors[..., :half_dim]
    second_half = vectors[..., half_dim:]
    return jnp.concatenate([first_half * cosine - second_half * sine, second_half * cosine + first_half * sine], axis=-1)

def reference(tokens, w_query, w_key, w_value, w_out, doc_ids):
    count = tokens.shape[0]
    places = jnp.arange(count, dtype=jnp.int32)
    queries = rotate(jnp.dot(tokens, w_query, preferred_element_type=jnp.float32).reshape(count, QH, HD), places).astype(jnp.bfloat16)
    keys_all = rotate(jnp.dot(tokens, w_key, preferred_element_type=jnp.float32).reshape(count, KVH, HD), places).astype(jnp.bfloat16)
    values_all = jnp.dot(tokens, w_value, preferred_element_type=jnp.float32).astype(jnp.bfloat16).reshape(count, KVH, HD)
    group_size = QH // KVH
    queries = queries.reshape(count, KVH, group_size, HD)
    block_rows = math.gcd(512, count)
    window = DOC_MOST + block_rows
    keys_pad = jnp.concatenate([jnp.zeros((DOC_MOST, KVH, HD), jnp.bfloat16), keys_all], axis=0)
    values_pad = jnp.concatenate([jnp.zeros((DOC_MOST, KVH, HD), jnp.bfloat16), values_all], axis=0)
    docs_pad = jnp.concatenate([jnp.full((DOC_MOST,), -1, jnp.int32), doc_ids], axis=0)
    score_scale = 1.0 / math.sqrt(HD)

    def one_block(block):
        q_start = (block * block_rows).astype(jnp.int32)
        q_block = lax.dynamic_slice_in_dim(queries, q_start, block_rows, 0).astype(jnp.float32)
        q_docs = lax.dynamic_slice_in_dim(doc_ids, q_start, block_rows, 0)
        q_index = q_start + jnp.arange(block_rows, dtype=jnp.int32)
        k_block = lax.dynamic_slice_in_dim(keys_pad, q_start, window, 0).astype(jnp.float32)
        v_block = lax.dynamic_slice_in_dim(values_pad, q_start, window, 0).astype(jnp.float32)
        k_docs = lax.dynamic_slice_in_dim(docs_pad, q_start, window, 0)
        k_index = q_start - DOC_MOST + jnp.arange(window, dtype=jnp.int32)
        allowed = (k_docs[None, :] == q_docs[:, None]) & (k_index[None, :] <= q_index[:, None])
        scores = jnp.einsum('tjgd,njd->jgtn', q_block, k_block) * score_scale
        scores = jnp.where(allowed, scores, -1e+30)
        top = lax.optimization_barrier(jnp.max(scores, axis=-1, keepdims=True))
        weights = jnp.exp(scores - top) * allowed.astype(jnp.float32)
        total = lax.optimization_barrier(jnp.sum(weights, axis=-1))
        summed = jnp.einsum('jgtn,njd->jgtd', weights.astype(jnp.bfloat16).astype(jnp.float32), v_block)
        result = summed / total[..., None]
        return jnp.transpose(result, (2, 0, 1, 3)).reshape(block_rows, QH * HD).astype(jnp.bfloat16)
    attended = lax.map(one_block, jnp.arange(count // block_rows, dtype=jnp.int32)).reshape(count, QH * HD)
    group_cols = QH * HD // N_HEAD
    mixed = jnp.zeros((count, D), jnp.float32)
    for group in range(N_HEAD):
        partial_value = jnp.dot(attended[:, group * group_cols:(group + 1) * group_cols], w_out[group * group_cols:(group + 1) * group_cols], preferred_element_type=jnp.float32).astype(jnp.bfloat16)
        partial_value = lax.optimization_barrier(partial_value)
        mixed = mixed + partial_value.astype(jnp.float32)
    return mixed.astype(jnp.bfloat16)
```

```python
import math

import jax
import jax.numpy as jnp
import numpy as np
from jax import lax
from jax.experimental import pallas as pl
from jax.experimental.pallas import tpu as pltpu
from jax.sharding import PartitionSpec as P

HD = 128
ROWS = 128
UNIT = 264
F32 = jnp.float32
BF16 = jnp.bfloat16
MIB = 1 << 20
SCALE = math.log2(math.e) / math.sqrt(HD)


def rope_table(count):
    half = HD // 2
    freqs = 500000.0 ** (-2.0 * np.arange(half, dtype=np.float64) / HD)
    angles = np.arange(count, dtype=np.float64)[:, None] * freqs[None, :]
    return np.concatenate([np.cos(angles), np.sin(angles)], axis=1).astype(np.float32)


def rotation(table):
    half = HD // 2
    cosine, sine = table[:, :half], table[:, half:]
    cosine = jnp.concatenate([cosine, cosine], axis=1)
    sine = jnp.concatenate([-sine, sine], axis=1)
    return lambda t: t * cosine + pltpu.roll(t, half, 1) * sine


SMEM = pl.BlockSpec(memory_space=pltpu.SMEM)
VMEM = pl.BlockSpec(memory_space=pltpu.VMEM)
HBM = pl.BlockSpec(memory_space=pltpu.HBM)


def like(*dims, dtype=BF16):
    return jax.ShapeDtypeStruct(dims, dtype)


def call(body, name, out, ins, outs, scratch=(), limit=4, flops=0, moved=1, exps=0):
    return pl.pallas_call(
        body,
        out_shape=out,
        in_specs=ins,
        out_specs=outs,
        scratch_shapes=list(scratch),
        name=name,
        cost_estimate=pl.CostEstimate(
            flops=flops, bytes_accessed=moved * MIB, transcendentals=exps
        ),
        compiler_params=pltpu.CompilerParams(vmem_limit_bytes=limit * MIB),
    )


def core_index():
    return lax.rem(lax.axis_index("ctx"), 2)


def table_rows(table):
    return table.at[pl.ds(pl.multiple_of(lax.axis_index("ctx") * ROWS, ROWS), ROWS), :]


def started(copies):
    for copy in copies:
        copy.start()
    return copies


KV_PARTS = 4


def kv_body(tok, wk, wv, docs, table, mine, send, tok_s, wk_s, wv_s, docs_s, table_s, acc, sems):
    part = tok.shape[1] // KV_PARTS
    copies = []
    for i in range(KV_PARTS):
        cut = pl.ds(i * part, part)
        copies.append(
            started([
                pltpu.make_async_copy(tok.at[:, cut], tok_s.at[:, cut], sems.at[3 * i]),
                pltpu.make_async_copy(wk.at[cut, :], wk_s.at[cut, :], sems.at[3 * i + 1]),
                pltpu.make_async_copy(wv.at[cut, :], wv_s.at[cut, :], sems.at[3 * i + 2]),
            ])
        )
    small = started([
        pltpu.make_async_copy(docs, docs_s, sems.at[3 * KV_PARTS]),
        pltpu.make_async_copy(table_rows(table), table_s, sems.at[3 * KV_PARTS + 1]),
    ])
    for i, group in enumerate(copies):
        for copy in group:
            copy.wait()
        cut = slice(i * part, (i + 1) * part)
        keys = jnp.dot(tok_s[:, cut], wk_s[cut, :], preferred_element_type=F32)
        values = jnp.dot(tok_s[:, cut], wv_s[cut, :], preferred_element_type=F32)
        if i == 0:
            acc[:, : 2 * HD] = keys
            acc[:, 2 * HD :] = values
        else:
            acc[:, : 2 * HD] += keys
            acc[:, 2 * HD :] += values
    for copy in small:
        copy.wait()
    first = core_index() == 0
    rot = rotation(table_s[...])
    keys = [rot(acc[:, h * HD : (h + 1) * HD]).astype(BF16) for h in (0, 1)]
    values = [acc[:, (2 + h) * HD : (3 + h) * HD].astype(BF16) for h in (0, 1)]
    tags = jnp.broadcast_to((docs_s[...] + 1).astype(F32), (8, ROWS)).astype(BF16)
    for out, kept in ((mine, first), (send, jnp.logical_not(first))):
        out[:ROWS, :HD] = jnp.where(kept, keys[0], keys[1])
        out[:ROWS, HD:] = jnp.where(kept, values[0], values[1])
        out[ROWS:, :HD] = tags
        out[ROWS:, HD:] = tags


def project_kv(tokens, w_key, w_value, docs, table):
    depth = tokens.shape[1]
    half = like(ROWS + 8, 2 * HD)
    return call(
        kv_body, "project_kv", (half, half), [HBM] * 5, (VMEM, VMEM),
        [
            pltpu.VMEM((ROWS, depth), BF16),
            pltpu.VMEM((depth, 2 * HD), BF16),
            pltpu.VMEM((depth, 2 * HD), BF16),
            pltpu.VMEM((1, ROWS), jnp.int32),
            pltpu.VMEM((ROWS, HD), F32),
            pltpu.VMEM((ROWS, 4 * HD), F32),
            pltpu.SemaphoreType.DMA((3 * KV_PARTS + 2,)),
        ],
        limit=8, flops=2 * ROWS * depth * 4 * HD, moved=5,
    )(tokens, w_key, w_value, docs, table)


def merge_body(mine, came, unit):
    first = core_index() == 0
    a, b = mine[...], came[...]
    unit[:ROWS, :] = jnp.where(first, a[:ROWS], b[:ROWS])
    unit[ROWS : 2 * ROWS, :] = jnp.where(first, b[:ROWS], a[:ROWS])
    unit[2 * ROWS :, :HD] = jnp.where(first, a[ROWS:, :HD], b[ROWS:, :HD])
    unit[2 * ROWS :, HD:] = jnp.where(first, b[ROWS:, :HD], a[ROWS:, :HD])


def merge(mine, came):
    return call(merge_body, "merge", like(UNIT, 2 * HD), [VMEM] * 2, VMEM, limit=1)(mine, came)


Q_PARTS = 2


def q_body(tok, wq, table, mine, send, tok_s, wq_s, table_s, sems):
    half = wq.shape[1] // 2
    part = wq.shape[0] // Q_PARTS
    core = core_index()
    small = started([
        pltpu.make_async_copy(tok, tok_s, sems.at[0]),
        pltpu.make_async_copy(table_rows(table), table_s, sems.at[1]),
    ])
    copies = []
    for side, at in ((0, 1 - core), (1, core)):
        cols = pl.ds(pl.multiple_of(at * half, half), half)
        for i in range(Q_PARTS):
            rows = pl.ds(i * part, part)
            copies += started([
                pltpu.make_async_copy(
                    wq.at[rows, cols], wq_s.at[side, rows, :], sems.at[2 + side * Q_PARTS + i]
                )
            ])
    for copy in small:
        copy.wait()
    rot = rotation(table_s[...])
    for side, out in ((0, send), (1, mine)):
        got = None
        for i in range(Q_PARTS):
            copies[side * Q_PARTS + i].wait()
            rows = slice(i * part, (i + 1) * part)
            more = jnp.dot(tok_s[:, rows], wq_s[side, rows, :], preferred_element_type=F32)
            got = more if got is None else got + more
        for h in range(half // HD):
            cols = slice(h * HD, (h + 1) * HD)
            out[:, cols] = rot(got[:, cols]).astype(BF16)


def project_q(tokens, w_query, table):
    depth, width = w_query.shape
    half = like(ROWS, width // 2)
    return call(
        q_body, "project_q", (half, half), [HBM] * 3, (VMEM, VMEM),
        [
            pltpu.VMEM((ROWS, depth), BF16),
            pltpu.VMEM((2, depth, width // 2), BF16),
            pltpu.VMEM((ROWS, HD), F32),
            pltpu.SemaphoreType.DMA((2 + 2 * Q_PARTS,)),
        ],
        limit=12, flops=2 * ROWS * depth * width, moved=9,
    )(tokens, w_query, table)


def bundle_body(unit, r1, r2, r3, out_a, out_b, out_c, slots):
    place = lax.axis_index("ctx")
    odd = lax.rem(place, 2)
    column = lax.rem(lax.div(place, 2), 4)
    for i, src in enumerate((unit, r1, r2, r3, unit)):
        slots[i] = src[...]

    def fill(out, count, late):
        skip = jnp.where((odd == 1) & (column >= late), 1, 0)
        for i in range(count):
            out[i * UNIT : (i + 1) * UNIT, :] = slots[skip + i]

    fill(out_a, 4, 3)
    fill(out_b, 2, 2)
    fill(out_c, 2, 1)


def bundle(unit, r1, r2, r3):
    return call(
        bundle_body, "bundle",
        (like(4 * UNIT, 2 * HD), like(2 * UNIT, 2 * HD), like(2 * UNIT, 2 * HD)),
        [VMEM] * 4, (VMEM,) * 3, [pltpu.VMEM((5, UNIT, 2 * HD), BF16)], limit=2,
    )(unit, r1, r2, r3)


COUNT = 2 * ROWS
CONTRACT = (((1,), (1,)), ((), ()))


def add_unit(qs, src, base, q_tag, q_first, state, allow=True):
    m_s, l_s, acc = state
    k_tag = src[pl.ds(base + COUNT, 8), :].astype(F32)

    @pl.when((jnp.max(k_tag) >= q_first) & allow)
    def _():
        bias = jnp.where(k_tag[0:1, :] == q_tag, 0.0, -1e30)
        keys = src[pl.ds(base, COUNT), :HD]
        values = src[pl.ds(base, COUNT), HD:]
        for h in range(qs.shape[0]):
            s = lax.dot_general(qs[h], keys, CONTRACT, preferred_element_type=F32)
            s = s * SCALE + bias
            old = m_s[h]
            top = jnp.maximum(old, jnp.max(s, axis=1, keepdims=True))
            fade = jnp.exp2(old - top)
            w = jnp.exp2(s - jnp.concatenate([top, top], axis=1))
            m_s[h] = top
            l_s[h] = fade * l_s[h] + jnp.sum(w, axis=1, keepdims=True)
            acc[h] = fade * acc[h] + jnp.dot(w.astype(BF16), values, preferred_element_type=F32)


def tags_of(unit):
    tags = unit[COUNT:UNIT, :].astype(F32)
    return tags, jnp.transpose(tags, (1, 0))[:, 0:1], jnp.min(tags)


def spans():
    core = core_index()
    own = pl.ds(pl.multiple_of(core * ROWS, ROWS), ROWS)
    other = pl.ds(pl.multiple_of((1 - core) * ROWS, ROWS), ROWS)
    return own, other


def near_body(qm, qr, unit, r1, r2, r3, qs, m_s, l_s, acc):
    heads = qs.shape[0]
    own, other = spans()
    for h in range(heads):
        qs[h, own, :] = qm[:, h * HD : (h + 1) * HD]
        qs[h, other, :] = qr[:, h * HD : (h + 1) * HD]
    tags, q_tag, q_first = tags_of(unit)
    rows = lax.broadcasted_iota(jnp.int32, (COUNT, COUNT), 0)
    cols = lax.broadcasted_iota(jnp.int32, (COUNT, COUNT), 1)
    bias = jnp.where((tags[0:1, :] == q_tag) & (cols <= rows), 0.0, -1e30)
    keys, values = unit[:COUNT, :HD], unit[:COUNT, HD:]
    for h in range(heads):
        s = lax.dot_general(qs[h], keys, CONTRACT, preferred_element_type=F32)
        s = s * SCALE + bias
        top = jnp.max(s, axis=1, keepdims=True)
        w = jnp.exp2(s - top)
        m_s[h] = jnp.broadcast_to(top, (COUNT, HD))
        l_s[h] = jnp.broadcast_to(jnp.sum(w, axis=1, keepdims=True), (COUNT, HD))
        acc[h] = jnp.dot(w.astype(BF16), values, preferred_element_type=F32)
    for src in (r1, r2, r3):
        add_unit(qs, src, 0, q_tag, q_first, (m_s, l_s, acc))


def attend_near(qm, qr, unit, r1, r2, r3):
    heads = qm.shape[1] // HD
    state = like(heads, COUNT, HD, dtype=F32)
    return call(
        near_body, "attend_near", (like(heads, COUNT, HD), state, state, state),
        [VMEM] * 6, (VMEM,) * 4, limit=4,
        flops=4 * heads * COUNT * 4 * COUNT * HD, exps=heads * COUNT * 4 * COUNT,
    )(qm, qr, unit, r1, r2, r3)


def far_body(qs, m_in, l_in, acc_in, unit, far_a, far_b, far_c, mine, send, m_s, l_s, acc):
    heads = qs.shape[0]
    state = (m_s, l_s, acc)
    for new, old in zip(state, (m_in, l_in, acc_in)):
        new[...] = old[...]
    _, q_tag, q_first = tags_of(unit)
    even = core_index() == 0
    for src, count in ((far_b, 2), (far_c, 2), (far_a, 4)):

        def step(i, carry):
            base = pl.multiple_of(i * UNIT, 8)
            add_unit(qs, src, base, q_tag, q_first, state, even | (i < 3))
            return carry

        lax.fori_loop(0, count, step, 0)
    own, other = spans()
    for h in range(heads):
        cols = slice(h * HD, (h + 1) * HD)
        mine[:, cols] = (acc[h, own, :] / l_s[h, own, :]).astype(BF16)
        send[:, cols] = (acc[h, other, :] / l_s[h, other, :]).astype(BF16)


def attend_far(qs, m_in, l_in, acc_in, unit, far_a, far_b, far_c):
    heads = qs.shape[0]
    half = like(ROWS, heads * HD)
    state = pltpu.VMEM((heads, COUNT, HD), F32)
    return call(
        far_body, "attend_far", (half, half), [VMEM] * 8, (VMEM,) * 2, [state] * 3, limit=6,
        flops=4 * heads * COUNT * 7 * COUNT * HD, exps=heads * COUNT * 7 * COUNT,
    )(qs, m_in, l_in, acc_in, unit, far_a, far_b, far_c)


def project_out(xm, xr, w_out, shift, groups):
    depth = xm.shape[1]
    width = w_out.shape[1] // groups

    def body(xm, xr, w, out):
        core = core_index()
        group = lax.rem(lax.axis_index("head") + shift, groups)
        cols = pl.ds(pl.multiple_of(group * width, width), width)
        own = pl.ds(pl.multiple_of(core * depth, depth), depth)
        other = pl.ds(pl.multiple_of((1 - core) * depth, depth), depth)
        got = jnp.dot(xm[...], w[own, cols], preferred_element_type=F32)
        got += jnp.dot(xr[...], w[other, cols], preferred_element_type=F32)
        out[...] = got.astype(BF16)

    return call(
        body, "project_out", like(ROWS, width), [VMEM] * 3, VMEM, limit=4,
        flops=2 * ROWS * 2 * depth * width, moved=3,
    )(xm, xr, w_out)


def shards(tokens, w_query, w_key, w_value, w_out, doc_ids):
    ranks = lax.axis_size("ctx")
    groups = lax.axis_size("head")
    table = jnp.asarray(rope_table(ranks * ROWS))

    def swap(value):
        return lax.ppermute(value, "ctx", [(r, r ^ 1) for r in range(ranks)])

    def along(value, even, odd):
        moves = []
        for r in range(ranks):
            chip = (odd if r % 2 else even)(r // 2)
            if chip is not None and chip < ranks // 2:
                moves.append((r, 2 * chip + r % 2))
        return lax.ppermute(value, "ctx", moves)

    def ahead(step):
        return lambda chip: chip + step

    def in_row(step):
        return lambda chip: chip // 4 * 4 + (chip + step) % 4

    def nowhere(chip):
        return None

    tokens, w_key, w_value, w_query, table, docs = (
        pltpu.with_memory_space_constraint(a, pltpu.HBM)
        for a in (tokens, w_key, w_value, w_query, table, doc_ids.reshape(1, -1))
    )
    mine, send = project_kv(tokens, w_key, w_value, docs, table)
    unit = merge(mine, swap(send))
    r1 = along(unit, ahead(1), ahead(4))
    r2 = along(unit, ahead(2), ahead(8))
    r3 = along(unit, ahead(3), lambda chip: 15 if chip == 3 else None)
    qm, qs = project_q(tokens, w_query, table)
    r1, r2, r3, qm, qs = lax.optimization_barrier((r1, r2, r3, qm, qs))
    qr = swap(qs)
    out_a, out_b, out_c = bundle(unit, r1, r2, r3)
    far_a = along(out_a, ahead(4), in_row(1))
    far_b = along(out_b, ahead(8), in_row(2))
    far_c = along(out_c, nowhere, in_row(3))
    state = attend_near(qm, qr, unit, r1, r2, r3)
    xm, xs = attend_far(*state, unit, far_a, far_b, far_c)
    xr = swap(xs)
    came = []
    for shift in (2, 1, 3):
        partial = project_out(xm, xr, w_out, shift, groups)
        came.append(
            lax.ppermute(partial, "head", [(g, (g + shift) % groups) for g in range(groups)])
        )
    total = project_out(xm, xr, w_out, 0, groups).astype(F32)
    for partial in came:
        total = total + partial.astype(F32)
    return total.astype(BF16)


def solution(mesh):
    return jax.shard_map(
        shards,
        mesh=mesh,
        in_specs=(
            P("ctx", None),
            P(None, "head"),
            P(None, "head"),
            P(None, "head"),
            P("head", None),
            P("ctx"),
        ),
        out_specs=P("ctx", "head"),
        check_vma=False,
    )
```

```python
import math

import jax
import jax.numpy as jnp
import numpy as np
from jax import lax
from jax.experimental import pallas as pl
from jax.experimental.pallas import tpu as pltpu
from jax.sharding import PartitionSpec as P

HD = 128
ROWS = 128
UNIT = 264
F32 = jnp.float32
BF16 = jnp.bfloat16
MIB = 1 << 20
SCALE = math.log2(math.e) / math.sqrt(HD)


def rope_table(count):
    half = HD // 2
    freqs = 500000.0 ** (-2.0 * np.arange(half, dtype=np.float64) / HD)
    angles = np.arange(count, dtype=np.float64)[:, None] * freqs[None, :]
    return np.concatenate([np.cos(angles), np.sin(angles)], axis=1).astype(np.float32)


def rotation(table):
    half = HD // 2
    cosine, sine = table[:, :half], table[:, half:]
    cosine = jnp.concatenate([cosine, cosine], axis=1)
    sine = jnp.concatenate([-sine, sine], axis=1)
    return lambda t: t * cosine + pltpu.roll(t, half, 1) * sine


SMEM = pl.BlockSpec(memory_space=pltpu.SMEM)
VMEM = pl.BlockSpec(memory_space=pltpu.VMEM)
HBM = pl.BlockSpec(memory_space=pltpu.HBM)


def like(*dims, dtype=BF16):
    return jax.ShapeDtypeStruct(dims, dtype)


def call(body, name, out, ins, outs, scratch=(), limit=4, flops=0, moved=1, exps=0):
    return pl.pallas_call(
        body,
        out_shape=out,
        in_specs=ins,
        out_specs=outs,
        scratch_shapes=list(scratch),
        name=name,
        cost_estimate=pl.CostEstimate(
            flops=flops, bytes_accessed=moved * MIB, transcendentals=exps
        ),
        compiler_params=pltpu.CompilerParams(vmem_limit_bytes=limit * MIB),
    )


def core_index():
    return lax.rem(lax.axis_index("ctx"), 2)


def table_rows(table):
    return table.at[pl.ds(pl.multiple_of(lax.axis_index("ctx") * ROWS, ROWS), ROWS), :]


def started(copies):
    for copy in copies:
        copy.start()
    return copies


KV_PARTS = 4


def kv_body(tok, wk, wv, docs, table, mine, send, tok_s, wk_s, wv_s, docs_s, table_s, acc, sems):
    part = tok.shape[1] // KV_PARTS
    copies = []
    for i in range(KV_PARTS):
        cut = pl.ds(i * part, part)
        copies.append(
            started([
                pltpu.make_async_copy(tok.at[:, cut], tok_s.at[:, cut], sems.at[3 * i]),
                pltpu.make_async_copy(wk.at[cut, :], wk_s.at[cut, :], sems.at[3 * i + 1]),
                pltpu.make_async_copy(wv.at[cut, :], wv_s.at[cut, :], sems.at[3 * i + 2]),
            ])
        )
    small = started([
        pltpu.make_async_copy(docs, docs_s, sems.at[3 * KV_PARTS]),
        pltpu.make_async_copy(table_rows(table), table_s, sems.at[3 * KV_PARTS + 1]),
    ])
    for i, group in enumerate(copies):
        for copy in group:
            copy.wait()
        cut = slice(i * part, (i + 1) * part)
        keys = jnp.dot(tok_s[:, cut], wk_s[cut, :], preferred_element_type=F32)
        values = jnp.dot(tok_s[:, cut], wv_s[cut, :], preferred_element_type=F32)
        if i == 0:
            acc[:, : 2 * HD] = keys
            acc[:, 2 * HD :] = values
        else:
            acc[:, : 2 * HD] += keys
            acc[:, 2 * HD :] += values
    for copy in small:
        copy.wait()
    first = core_index() == 0
    rot = rotation(table_s[...])
    keys = [rot(acc[:, h * HD : (h + 1) * HD]).astype(BF16) for h in (0, 1)]
    values = [acc[:, (2 + h) * HD : (3 + h) * HD].astype(BF16) for h in (0, 1)]
    tags = jnp.broadcast_to((docs_s[...] + 1).astype(F32), (8, ROWS)).astype(BF16)
    for out, kept in ((mine, first), (send, jnp.logical_not(first))):
        out[:ROWS, :HD] = jnp.where(kept, keys[0], keys[1])
        out[:ROWS, HD:] = jnp.where(kept, values[0], values[1])
        out[ROWS:, :HD] = tags
        out[ROWS:, HD:] = tags


def project_kv(tokens, w_key, w_value, docs, table):
    depth = tokens.shape[1]
    half = like(ROWS + 8, 2 * HD)
    return call(
        kv_body, "project_kv", (half, half), [HBM] * 5, (VMEM, VMEM),
        [
            pltpu.VMEM((ROWS, depth), BF16),
            pltpu.VMEM((depth, 2 * HD), BF16),
            pltpu.VMEM((depth, 2 * HD), BF16),
            pltpu.VMEM((1, ROWS), jnp.int32),
            pltpu.VMEM((ROWS, HD), F32),
            pltpu.VMEM((ROWS, 4 * HD), F32),
            pltpu.SemaphoreType.DMA((3 * KV_PARTS + 2,)),
        ],
        limit=8, flops=2 * ROWS * depth * 4 * HD, moved=5,
    )(tokens, w_key, w_value, docs, table)


def merge_body(mine, came, unit):
    first = core_index() == 0
    a, b = mine[...], came[...]
    unit[:ROWS, :] = jnp.where(first, a[:ROWS], b[:ROWS])
    unit[ROWS : 2 * ROWS, :] = jnp.where(first, b[:ROWS], a[:ROWS])
    unit[2 * ROWS :, :HD] = jnp.where(first, a[ROWS:, :HD], b[ROWS:, :HD])
    unit[2 * ROWS :, HD:] = jnp.where(first, b[ROWS:, :HD], a[ROWS:, :HD])


def merge(mine, came):
    return call(merge_body, "merge", like(UNIT, 2 * HD), [VMEM] * 2, VMEM, limit=1)(mine, came)


Q_PARTS = 2


def q_body(tok, wq, table, mine, send, tok_s, wq_s, table_s, sems):
    half = wq.shape[1] // 2
    part = wq.shape[0] // Q_PARTS
    core = core_index()
    small = started([
        pltpu.make_async_copy(tok, tok_s, sems.at[0]),
        pltpu.make_async_copy(table_rows(table), table_s, sems.at[1]),
    ])
    copies = []
    for side, at in ((0, 1 - core), (1, core)):
        cols = pl.ds(pl.multiple_of(at * half, half), half)
        for i in range(Q_PARTS):
            rows = pl.ds(i * part, part)
            copies += started([
                pltpu.make_async_copy(
                    wq.at[rows, cols], wq_s.at[side, rows, :], sems.at[2 + side * Q_PARTS + i]
                )
            ])
    for copy in small:
        copy.wait()
    rot = rotation(table_s[...])
    for side, out in ((0, send), (1, mine)):
        got = None
        for i in range(Q_PARTS):
            copies[side * Q_PARTS + i].wait()
            rows = slice(i * part, (i + 1) * part)
            more = jnp.dot(tok_s[:, rows], wq_s[side, rows, :], preferred_element_type=F32)
            got = more if got is None else got + more
        for h in range(half // HD):
            cols = slice(h * HD, (h + 1) * HD)
            out[:, cols] = (rot(got[:, cols]) * SCALE).astype(BF16)


def project_q(tokens, w_query, table):
    depth, width = w_query.shape
    half = like(ROWS, width // 2)
    return call(
        q_body, "project_q", (half, half), [HBM] * 3, (VMEM, VMEM),
        [
            pltpu.VMEM((ROWS, depth), BF16),
            pltpu.VMEM((2, depth, width // 2), BF16),
            pltpu.VMEM((ROWS, HD), F32),
            pltpu.SemaphoreType.DMA((2 + 2 * Q_PARTS,)),
        ],
        limit=12, flops=2 * ROWS * depth * width, moved=9,
    )(tokens, w_query, table)


NONE = 99
NEAR = ((1, 2, 3), (4, 8, NONE))
FAR_A = ((4, 5, 6), (1, 5, 9))
FAR_B = ((8, 9), (2, 6))
FAR_C = ((7, NONE), (3, 7))


def bundle_body(unit, r1, r2, r3, out_a, out_b, out_c, slots):
    place = lax.axis_index("ctx")
    odd = lax.rem(place, 2) == 1
    column = lax.rem(lax.div(place, 2), 4)
    for i, src in enumerate((unit, r1, r2, r3)):
        slots[i] = src[...]

    def fill(out, even, late):
        skip = jnp.where(column >= late, 1, 0)
        for i, at in enumerate(even):
            out[i * UNIT : (i + 1) * UNIT, :] = slots[jnp.where(odd, skip + i, at)]

    fill(out_a, (0, 1, 2), 3)
    fill(out_b, (0, 1), 2)
    fill(out_c, (3, 3), 1)


def bundle(unit, r1, r2, r3):
    return call(
        bundle_body, "bundle",
        (like(3 * UNIT, 2 * HD), like(2 * UNIT, 2 * HD), like(2 * UNIT, 2 * HD)),
        [VMEM] * 4, (VMEM,) * 3, [pltpu.VMEM((4, UNIT, 2 * HD), BF16)], limit=2,
    )(unit, r1, r2, r3)


COUNT = 2 * ROWS
CONTRACT = (((1,), (1,)), ((), ()))


def tags_of(unit):
    tags = unit[COUNT:UNIT, :].astype(F32)
    return tags, jnp.transpose(tags, (1, 0))[:, 0:1]


def spans():
    core = core_index()
    own = pl.ds(pl.multiple_of(core * ROWS, ROWS), ROWS)
    other = pl.ds(pl.multiple_of((1 - core) * ROWS, ROWS), ROWS)
    return own, other


def with_ones(values):
    return jnp.concatenate([values, jnp.ones((COUNT, HD), BF16)], axis=1)


def add_units(qs, pieces, q_tag, state):
    m_s, l_s, acc = state
    place = lax.axis_index("ctx")
    odd = lax.rem(place, 2) == 1
    chip = lax.div(place, 2)
    for src, distances in pieces:
        for i, (even_step, odd_step) in enumerate(zip(*distances)):
            base = i * UNIT
            valid = chip >= jnp.where(odd, odd_step, even_step)
            k_tag = src[base + COUNT : base + UNIT, :].astype(F32)[0:1, :]
            bias = jnp.where((k_tag == q_tag) & valid, 0.0, -1e30)
            keys = src[base : base + COUNT, :HD]
            values = with_ones(src[base : base + COUNT, HD:])
            for h in range(qs.shape[0]):
                s = lax.dot_general(qs[h], keys, CONTRACT, preferred_element_type=F32) + bias
                old = m_s[h]
                top = jnp.maximum(old, jnp.max(s, axis=1, keepdims=True))
                fade = jnp.exp2(old - top)
                w = jnp.exp2(s - jnp.concatenate([top, top], axis=1)).astype(BF16)
                got = jnp.dot(w, values, preferred_element_type=F32)
                m_s[h] = top
                l_s[h] = fade * l_s[h] + got[:, HD:]
                acc[h] = fade * acc[h] + got[:, :HD]


def near_body(qm, qr, unit, r1, r2, r3, qs, m_s, l_s, acc):
    heads = qs.shape[0]
    own, other = spans()
    for h in range(heads):
        qs[h, own, :] = qm[:, h * HD : (h + 1) * HD]
        qs[h, other, :] = qr[:, h * HD : (h + 1) * HD]
    tags, q_tag = tags_of(unit)
    rows = lax.broadcasted_iota(jnp.int32, (COUNT, COUNT), 0)
    cols = lax.broadcasted_iota(jnp.int32, (COUNT, COUNT), 1)
    bias = jnp.where((tags[0:1, :] == q_tag) & (cols <= rows), 0.0, -1e30)
    keys, values = unit[:COUNT, :HD], with_ones(unit[:COUNT, HD:])
    for h in range(heads):
        s = lax.dot_general(qs[h], keys, CONTRACT, preferred_element_type=F32) + bias
        top = jnp.max(s, axis=1, keepdims=True)
        got = jnp.dot(jnp.exp2(s - top).astype(BF16), values, preferred_element_type=F32)
        m_s[h] = jnp.broadcast_to(top, (COUNT, HD))
        l_s[h] = got[:, HD:]
        acc[h] = got[:, :HD]
    pieces = [
        (src, ((even,), (odd,))) for src, even, odd in zip((r1, r2, r3), NEAR[0], NEAR[1])
    ]
    add_units(qs, pieces, q_tag, (m_s, l_s, acc))


def attend_near(qm, qr, unit, r1, r2, r3):
    heads = qm.shape[1] // HD
    state = like(heads, COUNT, HD, dtype=F32)
    return call(
        near_body, "attend_near", (like(heads, COUNT, HD), state, state, state),
        [VMEM] * 6, (VMEM,) * 4, limit=8,
        flops=4 * heads * COUNT * 4 * COUNT * HD, exps=heads * COUNT * 4 * COUNT,
    )(qm, qr, unit, r1, r2, r3)


def attend_far(side, qs, m_in, l_in, acc_in, unit, far_a, far_b, far_c):
    heads = qs.shape[0]

    def body(q_in, m_in, l_in, acc_in, unit, far_a, far_b, far_c, out, qs, tag_s, m_s, l_s, acc):
        rows = spans()[side]
        state = (m_s, l_s, acc)
        for new, old in zip((qs, *state), (q_in, m_in, l_in, acc_in)):
            for h in range(heads):
                new[h] = old[h, rows, :]
        tag_s[...] = jnp.broadcast_to(tags_of(unit)[1], (COUNT, HD))
        pieces = ((far_b, FAR_B), (far_c, FAR_C), (far_a, FAR_A))
        add_units(qs, pieces, tag_s[rows, :][:, 0:1], state)
        for h in range(heads):
            out[:, h * HD : (h + 1) * HD] = (acc[h] / l_s[h]).astype(BF16)

    state = pltpu.VMEM((heads, ROWS, HD), F32)
    return call(
        body, "attend_far", like(ROWS, heads * HD), [VMEM] * 8, VMEM,
        [pltpu.VMEM((heads, ROWS, HD), BF16), pltpu.VMEM((COUNT, HD), F32), state, state, state],
        limit=8, flops=4 * heads * ROWS * 7 * COUNT * HD, exps=heads * ROWS * 7 * COUNT,
    )(qs, m_in, l_in, acc_in, unit, far_a, far_b, far_c)


def project_out(xm, xr, w_out, groups, parts, dtype):
    depth = xm.shape[1]
    width = w_out.shape[1] // groups
    half = width // 2

    def body(xm, xr, w, *outs):
        core = core_index()
        own = pl.ds(pl.multiple_of(core * depth, depth), depth)
        other = pl.ds(pl.multiple_of((1 - core) * depth, depth), depth)
        for (shift, side), out in zip(parts, outs):
            group = lax.rem(lax.axis_index("head") + shift, groups)
            cols = pl.ds(pl.multiple_of(group * width + side * half, half), half)
            got = jnp.dot(xm[...], w[own, cols], preferred_element_type=F32)
            got += jnp.dot(xr[...], w[other, cols], preferred_element_type=F32)
            out[...] = got.astype(dtype)

    return call(
        body, "project_out", (like(ROWS, half, dtype=dtype),) * len(parts), [VMEM] * 3,
        (VMEM,) * len(parts), limit=4,
        flops=2 * ROWS * 2 * depth * half * len(parts), moved=len(parts),
    )(xm, xr, w_out)


def add_body(a, b, p, q, out_a, out_b):
    out_a[...] = (a[...] + p[...].astype(F32)).astype(BF16)
    out_b[...] = (b[...] + q[...].astype(F32)).astype(BF16)


def add_passing(a, b, p, q):
    out = like(*p.shape)
    return call(add_body, "add_passing", (out, out), [VMEM] * 4, (VMEM,) * 2, limit=2)(a, b, p, q)


def total_body(own_a, own_b, left_a, left_b, right_a, right_b, out):
    half = own_a.shape[1]
    for at, pieces in ((0, (own_a, left_a, right_a)), (half, (own_b, left_b, right_b))):
        total = pieces[0][...] + pieces[1][...].astype(F32) + pieces[2][...].astype(F32)
        out[:, at : at + half] = total.astype(BF16)


def add_total(*pieces):
    rows, half = pieces[0].shape
    return call(total_body, "add_total", like(rows, 2 * half), [VMEM] * 6, VMEM, limit=2)(*pieces)


def shards(tokens, w_query, w_key, w_value, w_out, doc_ids):
    ranks = lax.axis_size("ctx")
    groups = lax.axis_size("head")
    table = jnp.asarray(rope_table(ranks * ROWS))

    def swap(value):
        return lax.ppermute(value, "ctx", [(r, r ^ 1) for r in range(ranks)])

    def along(value, even, odd):
        moves = [(r, 2 * (odd if r % 2 else even)(r // 2) + r % 2) for r in range(ranks)]
        return lax.ppermute(value, "ctx", moves)

    def ahead(step):
        return lambda chip: (chip + step) % (ranks // 2)

    def in_row(step):
        return lambda chip: chip // 4 * 4 + (chip + step) % 4

    tokens, w_key, w_value, w_query, table, docs = (
        pltpu.with_memory_space_constraint(a, pltpu.HBM)
        for a in (tokens, w_key, w_value, w_query, table, doc_ids.reshape(1, -1))
    )
    mine, send = project_kv(tokens, w_key, w_value, docs, table)
    unit = merge(mine, swap(send))
    r1 = along(unit, ahead(1), ahead(4))
    r2 = along(unit, ahead(2), ahead(8))
    r3 = along(unit, ahead(3), ahead(12))
    qm, qs = project_q(tokens, w_query, table)
    r1, r2, r3, qm, qs = lax.optimization_barrier((r1, r2, r3, qm, qs))
    qr = swap(qs)
    out_a, out_b, out_c = bundle(unit, r1, r2, r3)
    far_a = along(out_a, ahead(4), in_row(1))
    far_b = along(out_b, ahead(8), in_row(2))
    far_c = along(out_c, ahead(4), in_row(3))
    state = attend_near(qm, qr, unit, r1, r2, r3)
    far = (*state, unit, far_a, far_b, far_c)
    xr = swap(attend_far(1, *far))
    xm = attend_far(0, *far)

    def shift(value, step):
        return lax.ppermute(value, "head", [(g, (g + step) % groups) for g in range(groups)])

    a2, b2 = project_out(xm, xr, w_out, groups, ((2, 0), (2, 1)), BF16)
    pass_a, pass_b = shift(a2, 1), shift(b2, -1)
    b1, a3 = project_out(xm, xr, w_out, groups, ((1, 1), (3, 0)), BF16)
    left_b, right_a = shift(b1, 1), shift(a3, -1)
    a1, b3, a0, b0 = project_out(xm, xr, w_out, groups, ((1, 0), (3, 1), (0, 0), (0, 1)), F32)
    a1, b3 = add_passing(a1, b3, pass_a, pass_b)
    left_a, right_b = shift(a1, 1), shift(b3, -1)
    return add_total(a0, b0, left_a, left_b, right_a, right_b)


def solution(mesh):
    return jax.shard_map(
        shards,
        mesh=mesh,
        in_specs=(
            P("ctx", None),
            P(None, "head"),
            P(None, "head"),
            P(None, "head"),
            P("head", None),
            P("ctx"),
        ),
        out_specs=P("ctx", "head"),
        check_vma=False,
    )
```

```python
import math

import jax
import jax.numpy as jnp
import numpy as np
from jax import lax
from jax.experimental import pallas as pl
from jax.experimental.pallas import tpu as pltpu
from jax.sharding import PartitionSpec as P

HD = 128
ROWS = 128
UNIT = 264
F32 = jnp.float32
BF16 = jnp.bfloat16
MIB = 1 << 20
SCALE = math.log2(math.e) / math.sqrt(HD)


def rope_table(count):
    half = HD // 2
    freqs = 500000.0 ** (-2.0 * np.arange(half, dtype=np.float64) / HD)
    angles = np.arange(count, dtype=np.float64)[:, None] * freqs[None, :]
    return np.concatenate([np.cos(angles), np.sin(angles)], axis=1).astype(np.float32)


def rotation(table):
    half = HD // 2
    cosine, sine = table[:, :half], table[:, half:]
    cosine = jnp.concatenate([cosine, cosine], axis=1)
    sine = jnp.concatenate([-sine, sine], axis=1)
    return lambda t: t * cosine + pltpu.roll(t, half, 1) * sine


SMEM = pl.BlockSpec(memory_space=pltpu.SMEM)
VMEM = pl.BlockSpec(memory_space=pltpu.VMEM)
HBM = pl.BlockSpec(memory_space=pltpu.HBM)


def like(*dims, dtype=BF16):
    return jax.ShapeDtypeStruct(dims, dtype)


def call(body, name, out, ins, outs, scratch=(), limit=4, flops=0, moved=1, exps=0):
    return pl.pallas_call(
        body,
        out_shape=out,
        in_specs=ins,
        out_specs=outs,
        scratch_shapes=list(scratch),
        name=name,
        cost_estimate=pl.CostEstimate(
            flops=flops, bytes_accessed=moved * MIB, transcendentals=exps
        ),
        compiler_params=pltpu.CompilerParams(vmem_limit_bytes=limit * MIB),
    )


def core_index():
    return lax.rem(lax.axis_index("ctx"), 2)


def table_rows(table):
    return table.at[pl.ds(pl.multiple_of(lax.axis_index("ctx") * ROWS, ROWS), ROWS), :]


def started(copies):
    for copy in copies:
        copy.start()
    return copies


KV_PARTS = 4
CHIP = 2 * ROWS


def halves():
    core = core_index()
    own = pl.ds(pl.multiple_of(core * ROWS, ROWS), ROWS)
    other = pl.ds(pl.multiple_of((1 - core) * ROWS, ROWS), ROWS)
    return own, other


def own_body(tok, wk, wv, docs, table, half, tok_s, w_s, docs_s, table_s, acc, sems):
    part = tok.shape[1] // KV_PARTS
    cols = pl.ds(pl.multiple_of(core_index() * HD, HD), HD)
    copies = []
    for i in range(KV_PARTS):
        cut = pl.ds(i * part, part)
        copies.append(
            started([
                pltpu.make_async_copy(tok.at[:, cut], tok_s.at[:, cut], sems.at[3 * i]),
                pltpu.make_async_copy(
                    wk.at[cut, cols], w_s.at[cut, pl.ds(0, HD)], sems.at[3 * i + 1]
                ),
                pltpu.make_async_copy(
                    wv.at[cut, cols], w_s.at[cut, pl.ds(HD, HD)], sems.at[3 * i + 2]
                ),
            ])
        )
    first = pl.multiple_of(lax.div(lax.axis_index("ctx"), 2) * CHIP, CHIP)
    small = started([
        pltpu.make_async_copy(docs, docs_s, sems.at[3 * KV_PARTS]),
        pltpu.make_async_copy(table.at[pl.ds(first, CHIP), :], table_s, sems.at[3 * KV_PARTS + 1]),
    ])
    for i, group in enumerate(copies):
        for copy in group:
            copy.wait()
        cut = slice(i * part, (i + 1) * part)
        more = jnp.dot(tok_s[:, cut], w_s[cut, :], preferred_element_type=F32)
        if i == 0:
            acc[...] = more
        else:
            acc[...] += more
    for copy in small:
        copy.wait()
    rot = rotation(table_s[halves()[0], :])
    half[:, :HD] = rot(acc[:, :HD]).astype(BF16)
    half[:, HD:] = acc[:, HD:].astype(BF16)


def project_own(tokens, w_key, w_value, docs, table):
    depth = tokens.shape[1]
    return call(
        own_body, "project_own",
        (
            like(ROWS, 2 * HD),
            like(ROWS, depth),
            like(depth, 2 * HD),
            like(1, ROWS, dtype=jnp.int32),
            like(CHIP, HD, dtype=F32),
        ),
        [HBM] * 5, (VMEM,) * 5,
        [pltpu.VMEM((ROWS, 2 * HD), F32), pltpu.SemaphoreType.DMA((3 * KV_PARTS + 2,))],
        limit=6, flops=2 * ROWS * depth * 2 * HD, moved=3,
    )(tokens, w_key, w_value, docs, table)


def unit_body(half, came, w, docs, docs_came, table, unit):
    own, other = halves()
    got = jnp.dot(came[...], w[...], preferred_element_type=F32)
    unit[own, :] = half[...]
    unit[other, :HD] = rotation(table[other, :])(got[:, :HD]).astype(BF16)
    unit[other, HD:] = got[:, HD:].astype(BF16)
    first = core_index() == 0
    a, b = docs[...], docs_came[...]
    tags = jnp.concatenate([jnp.where(first, a, b), jnp.where(first, b, a)], axis=1)
    tags = (tags + 1).astype(F32)
    unit[CHIP:, :] = jnp.broadcast_to(tags, (8, CHIP)).astype(BF16)


def project_unit(half, came, w, docs, docs_came, table):
    return call(
        unit_body, "project_unit", like(UNIT, 2 * HD), [VMEM] * 6, VMEM, limit=2,
        flops=2 * ROWS * w.shape[0] * 2 * HD,
    )(half, came, w, docs, docs_came, table)


Q_PARTS = 4


def q_body(tok, came, wq, table, out, wq_s, sems):
    half = wq.shape[1] // 2
    part = wq.shape[0] // Q_PARTS
    cols = pl.ds(pl.multiple_of(core_index() * half, half), half)
    copies = []
    for i in range(Q_PARTS):
        rows = pl.ds(i * part, part)
        copies += started([
            pltpu.make_async_copy(wq.at[rows, cols], wq_s.at[rows, :], sems.at[i])
        ])
    got = [None, None]
    for i in range(Q_PARTS):
        copies[i].wait()
        rows = slice(i * part, (i + 1) * part)
        for side, src in enumerate((tok, came)):
            more = jnp.dot(src[:, rows], wq_s[rows, :], preferred_element_type=F32)
            got[side] = more if i == 0 else got[side] + more
    for side, span in enumerate(halves()):
        rot = rotation(table[span, :])
        for h in range(half // HD):
            out[h, span, :] = rot(got[side][:, h * HD : (h + 1) * HD]).astype(BF16)


def project_q(tokens, came, w_query, table):
    depth, width = w_query.shape
    return call(
        q_body, "project_q", like(width // 2 // HD, CHIP, HD), [VMEM, VMEM, HBM, VMEM], VMEM,
        [pltpu.VMEM((depth, width // 2), BF16), pltpu.SemaphoreType.DMA((Q_PARTS,))],
        limit=8, flops=2 * CHIP * depth * width // 2, moved=6,
    )(tokens, came, w_query, table)


NONE = 99
NEAR = ((1, 2, 3), (4, 8, NONE))
FAR = ((4, 5, 6, 8, 9, 7, NONE), (1, 5, 9, 2, 6, 3, 7))


def bundle_body(unit, r1, r2, r3, out_a, out_b, out_c, slots):
    place = lax.axis_index("ctx")
    odd = lax.rem(place, 2) == 1
    column = lax.rem(lax.div(place, 2), 4)
    for i, src in enumerate((unit, r1, r2, r3)):
        slots[i] = src[...]

    def fill(out, even, late):
        skip = jnp.where(column >= late, 1, 0)
        for i, at in enumerate(even):
            out[i * UNIT : (i + 1) * UNIT, :] = slots[jnp.where(odd, jnp.minimum(skip + i, 3), at)]

    fill(out_a, (0, 1, 2, 3), 3)
    fill(out_b, (0, 1), 2)
    fill(out_c, (0, 1), 1)


def bundle(unit, r1, r2, r3):
    return call(
        bundle_body, "bundle",
        (like(4 * UNIT, 2 * HD), like(2 * UNIT, 2 * HD), like(2 * UNIT, 2 * HD)),
        [VMEM] * 4, (VMEM,) * 3, [pltpu.VMEM((4, UNIT, 2 * HD), BF16)], limit=2,
    )(unit, r1, r2, r3)


CONTRACT = (((1,), (1,)), ((), ()))


def tags_of(unit):
    tags = unit[CHIP:UNIT, :].astype(F32)
    return tags, jnp.transpose(tags, (1, 0))[:, 0:1]


def with_ones(values):
    return jnp.concatenate([values, jnp.ones((CHIP, HD), BF16)], axis=1)


def add_units(qs, units, steps, q_tag, state):
    m_s, l_s, acc = state
    place = lax.axis_index("ctx")
    odd = lax.rem(place, 2) == 1
    chip = lax.div(place, 2)
    for unit, even_step, odd_step in zip(units, *steps):
        block = unit()
        valid = chip >= jnp.where(odd, odd_step, even_step)
        k_tag = block[CHIP:, :].astype(F32)[0:1, :]
        bias = jnp.where((k_tag == q_tag) & valid, 0.0, -1e30)
        keys = block[:CHIP, :HD]
        values = with_ones(block[:CHIP, HD:])
        for h in range(qs.shape[0]):
            s = lax.dot_general(qs[h], keys, CONTRACT, preferred_element_type=F32)
            s = s * SCALE + bias
            old = m_s[h]
            top = jnp.maximum(old, jnp.max(s, axis=1, keepdims=True))
            fade = jnp.exp2(old - top)
            w = jnp.exp2(s - jnp.concatenate([top, top], axis=1)).astype(BF16)
            got = jnp.dot(w, values, preferred_element_type=F32)
            m_s[h] = top
            l_s[h] = fade * l_s[h] + got[:, HD:]
            acc[h] = fade * acc[h] + got[:, :HD]


def near_body(qs, unit, r1, r2, r3, m_s, l_s, acc):
    tags, q_tag = tags_of(unit)
    rows = lax.broadcasted_iota(jnp.int32, (CHIP, CHIP), 0)
    cols = lax.broadcasted_iota(jnp.int32, (CHIP, CHIP), 1)
    bias = jnp.where((tags[0:1, :] == q_tag) & (cols <= rows), 0.0, -1e30)
    keys, values = unit[:CHIP, :HD], with_ones(unit[:CHIP, HD:])
    for h in range(qs.shape[0]):
        s = lax.dot_general(qs[h], keys, CONTRACT, preferred_element_type=F32)
        s = s * SCALE + bias
        top = jnp.max(s, axis=1, keepdims=True)
        got = jnp.dot(jnp.exp2(s - top).astype(BF16), values, preferred_element_type=F32)
        m_s[h] = jnp.broadcast_to(top, (CHIP, HD))
        l_s[h] = got[:, HD:]
        acc[h] = got[:, :HD]
    units = [lambda src=src: src[...] for src in (r1, r2, r3)]
    add_units(qs, units, NEAR, q_tag, (m_s, l_s, acc))


def attend_near(qs, unit, r1, r2, r3):
    heads = qs.shape[0]
    state = like(heads, CHIP, HD, dtype=F32)
    return call(
        near_body, "attend_near", (state, state, state), [VMEM] * 5, (VMEM,) * 3, limit=8,
        flops=4 * heads * CHIP * 4 * CHIP * HD, exps=heads * CHIP * 4 * CHIP,
    )(qs, unit, r1, r2, r3)


def attend_far(side, qs, m_in, l_in, acc_in, unit, far_a, far_b, far_c):
    heads = qs.shape[0]

    def body(q_in, m_in, l_in, acc_in, unit, far_a, far_b, far_c, out, qs, tag_s, m_s, l_s, acc):
        rows = halves()[side]
        state = (m_s, l_s, acc)
        for new, old in zip((qs, *state), (q_in, m_in, l_in, acc_in)):
            for h in range(heads):
                new[h] = old[h, rows, :]
        tag_s[...] = jnp.broadcast_to(tags_of(unit)[1], (CHIP, HD))
        odd = core_index() == 1

        def at(src, i):
            return lambda: src[i * UNIT : (i + 1) * UNIT, :]

        units = [at(far_a, 0), at(far_a, 1), at(far_a, 2), at(far_b, 0), at(far_b, 1)]
        units.append(lambda: jnp.where(odd, at(far_c, 0)(), at(far_a, 3)()))
        units.append(at(far_c, 1))
        add_units(qs, units, FAR, tag_s[rows, :][:, 0:1], state)
        for h in range(heads):
            out[:, h * HD : (h + 1) * HD] = (acc[h] / l_s[h]).astype(BF16)

    state = pltpu.VMEM((heads, ROWS, HD), F32)
    return call(
        body, "attend_far", like(ROWS, heads * HD), [VMEM] * 8, VMEM,
        [pltpu.VMEM((heads, ROWS, HD), BF16), pltpu.VMEM((CHIP, HD), F32), state, state, state],
        limit=8, flops=4 * heads * ROWS * 7 * CHIP * HD, exps=heads * ROWS * 7 * CHIP,
    )(qs, m_in, l_in, acc_in, unit, far_a, far_b, far_c)


def project_out(xm, xr, w_out, groups, parts, dtype):
    depth = xm.shape[1]
    width = w_out.shape[1] // groups
    half = width // 2

    def body(xm, xr, w, *outs):
        core = core_index()
        own = pl.ds(pl.multiple_of(core * depth, depth), depth)
        other = pl.ds(pl.multiple_of((1 - core) * depth, depth), depth)
        for (shift, side), out in zip(parts, outs):
            group = lax.rem(lax.axis_index("head") + shift, groups)
            cols = pl.ds(pl.multiple_of(group * width + side * half, half), half)
            got = jnp.dot(xm[...], w[own, cols], preferred_element_type=F32)
            got += jnp.dot(xr[...], w[other, cols], preferred_element_type=F32)
            out[...] = got.astype(dtype)

    return call(
        body, "project_out", (like(ROWS, half, dtype=dtype),) * len(parts), [VMEM] * 3,
        (VMEM,) * len(parts), limit=4,
        flops=2 * ROWS * 2 * depth * half * len(parts), moved=len(parts),
    )(xm, xr, w_out)


def add_body(a, b, p, q, out_a, out_b):
    out_a[...] = (a[...] + p[...].astype(F32)).astype(BF16)
    out_b[...] = (b[...] + q[...].astype(F32)).astype(BF16)


def add_passing(a, b, p, q):
    out = like(*p.shape)
    return call(add_body, "add_passing", (out, out), [VMEM] * 4, (VMEM,) * 2, limit=2)(a, b, p, q)


def total_body(own_a, own_b, left_a, left_b, right_a, right_b, out):
    half = own_a.shape[1]
    for at, pieces in ((0, (own_a, left_a, right_a)), (half, (own_b, left_b, right_b))):
        total = pieces[0][...] + pieces[1][...].astype(F32) + pieces[2][...].astype(F32)
        out[:, at : at + half] = total.astype(BF16)


def add_total(*pieces):
    rows, half = pieces[0].shape
    return call(total_body, "add_total", like(rows, 2 * half), [VMEM] * 6, VMEM, limit=2)(*pieces)


def shards(tokens, w_query, w_key, w_value, w_out, doc_ids):
    ranks = lax.axis_size("ctx")
    groups = lax.axis_size("head")
    table = jnp.asarray(rope_table(ranks * ROWS))

    def swap(value):
        return lax.ppermute(value, "ctx", [(r, r ^ 1) for r in range(ranks)])

    def along(value, even, odd):
        moves = [(r, 2 * (odd if r % 2 else even)(r // 2) + r % 2) for r in range(ranks)]
        return lax.ppermute(value, "ctx", moves)

    def ahead(step):
        return lambda chip: (chip + step) % (ranks // 2)

    def in_row(step):
        return lambda chip: chip // 4 * 4 + (chip + step) % 4

    docs = doc_ids.reshape(1, -1)
    came, docs_came = swap(tokens), swap(docs)
    tokens, w_key, w_value, w_query, table, docs = (
        pltpu.with_memory_space_constraint(a, pltpu.HBM)
        for a in (tokens, w_key, w_value, w_query, table, docs)
    )
    half, tokens, w_kv, docs, table = project_own(tokens, w_key, w_value, docs, table)
    unit = project_unit(half, came, w_kv, docs, docs_came, table)
    r1 = along(unit, ahead(1), ahead(4))
    r2 = along(unit, ahead(2), ahead(8))
    r3 = along(unit, ahead(3), ahead(12))
    r1, r2, r3, came = lax.optimization_barrier((r1, r2, r3, came))
    out_a, out_b, out_c = bundle(unit, r1, r2, r3)
    far_a = along(out_a, ahead(4), in_row(1))
    far_b = along(out_b, ahead(8), in_row(2))
    far_c = along(out_c, ahead(12), in_row(3))
    qs = project_q(tokens, came, w_query, table)
    state = attend_near(qs, unit, r1, r2, r3)
    far = (qs, *state, unit, far_a, far_b, far_c)
    xr = swap(attend_far(1, *far))
    xm = attend_far(0, *far)

    def shift(value, step):
        return lax.ppermute(value, "head", [(g, (g + step) % groups) for g in range(groups)])

    a2, b2 = project_out(xm, xr, w_out, groups, ((2, 0), (2, 1)), BF16)
    pass_a, pass_b = shift(a2, 1), shift(b2, -1)
    b1, a3 = project_out(xm, xr, w_out, groups, ((1, 1), (3, 0)), BF16)
    left_b, right_a = shift(b1, 1), shift(a3, -1)
    a1, b3, a0, b0 = project_out(xm, xr, w_out, groups, ((1, 0), (3, 1), (0, 0), (0, 1)), F32)
    a1, b3 = add_passing(a1, b3, pass_a, pass_b)
    left_a, right_b = shift(a1, 1), shift(b3, -1)
    return add_total(a0, b0, left_a, left_b, right_a, right_b)


def solution(mesh):
    return jax.shard_map(
        shards,
        mesh=mesh,
        in_specs=(
            P("ctx", None),
            P(None, "head"),
            P(None, "head"),
            P(None, "head"),
            P("head", None),
            P("ctx"),
        ),
        out_specs=P("ctx", "head"),
        check_vma=False,
    )
```

```python
import math

import jax
import jax.numpy as jnp
import numpy as np
from jax import lax
from jax.experimental import pallas as pl
from jax.experimental.pallas import tpu as pltpu
from jax.sharding import PartitionSpec as P

HD = 128
ROWS = 128
UNIT = 264
F32 = jnp.float32
BF16 = jnp.bfloat16
MIB = 1 << 20
SCALE = math.log2(math.e) / math.sqrt(HD)


def rope_table(count):
    half = HD // 2
    freqs = 500000.0 ** (-2.0 * np.arange(half, dtype=np.float64) / HD)
    angles = np.arange(count, dtype=np.float64)[:, None] * freqs[None, :]
    return np.concatenate([np.cos(angles), np.sin(angles)], axis=1).astype(np.float32)


def rotation(table):
    half = HD // 2
    cosine, sine = table[:, :half], table[:, half:]
    cosine = jnp.concatenate([cosine, cosine], axis=1)
    sine = jnp.concatenate([-sine, sine], axis=1)
    return lambda t: t * cosine + pltpu.roll(t, half, 1) * sine


SMEM = pl.BlockSpec(memory_space=pltpu.SMEM)
VMEM = pl.BlockSpec(memory_space=pltpu.VMEM)
HBM = pl.BlockSpec(memory_space=pltpu.HBM)


def like(*dims, dtype=BF16):
    return jax.ShapeDtypeStruct(dims, dtype)


def call(body, name, out, ins, outs, scratch=(), limit=4, flops=0, moved=1, exps=0):
    return pl.pallas_call(
        body,
        out_shape=out,
        in_specs=ins,
        out_specs=outs,
        scratch_shapes=list(scratch),
        name=name,
        cost_estimate=pl.CostEstimate(
            flops=flops, bytes_accessed=moved * MIB, transcendentals=exps
        ),
        compiler_params=pltpu.CompilerParams(vmem_limit_bytes=limit * MIB),
    )


def core_index():
    return lax.rem(lax.axis_index("ctx"), 2)


def table_rows(table):
    return table.at[pl.ds(pl.multiple_of(lax.axis_index("ctx") * ROWS, ROWS), ROWS), :]


def started(copies):
    for copy in copies:
        copy.start()
    return copies


KV_PARTS = 4
CHIP = 2 * ROWS


def halves():
    core = core_index()
    own = pl.ds(pl.multiple_of(core * ROWS, ROWS), ROWS)
    other = pl.ds(pl.multiple_of((1 - core) * ROWS, ROWS), ROWS)
    return own, other


def own_body(tok, wk, wv, docs, table, half, tok_s, w_s, docs_s, table_s, acc, sems):
    part = tok.shape[1] // KV_PARTS
    cols = pl.ds(pl.multiple_of(core_index() * HD, HD), HD)
    copies = []
    for i in range(KV_PARTS):
        cut = pl.ds(i * part, part)
        copies.append(
            started([
                pltpu.make_async_copy(tok.at[:, cut], tok_s.at[:, cut], sems.at[3 * i]),
                pltpu.make_async_copy(
                    wk.at[cut, cols], w_s.at[cut, pl.ds(0, HD)], sems.at[3 * i + 1]
                ),
                pltpu.make_async_copy(
                    wv.at[cut, cols], w_s.at[cut, pl.ds(HD, HD)], sems.at[3 * i + 2]
                ),
            ])
        )
    first = pl.multiple_of(lax.div(lax.axis_index("ctx"), 2) * CHIP, CHIP)
    small = started([
        pltpu.make_async_copy(docs, docs_s, sems.at[3 * KV_PARTS]),
        pltpu.make_async_copy(table.at[pl.ds(first, CHIP), :], table_s, sems.at[3 * KV_PARTS + 1]),
    ])
    for i, group in enumerate(copies):
        for copy in group:
            copy.wait()
        cut = slice(i * part, (i + 1) * part)
        more = jnp.dot(tok_s[:, cut], w_s[cut, :], preferred_element_type=F32)
        if i == 0:
            acc[...] = more
        else:
            acc[...] += more
    for copy in small:
        copy.wait()
    rot = rotation(table_s[halves()[0], :])
    half[:, :HD] = rot(acc[:, :HD]).astype(BF16)
    half[:, HD:] = acc[:, HD:].astype(BF16)


def project_own(tokens, w_key, w_value, docs, table):
    depth = tokens.shape[1]
    return call(
        own_body, "project_own",
        (
            like(ROWS, 2 * HD),
            like(ROWS, depth),
            like(depth, 2 * HD),
            like(1, ROWS, dtype=jnp.int32),
            like(CHIP, HD, dtype=F32),
        ),
        [HBM] * 5, (VMEM,) * 5,
        [pltpu.VMEM((ROWS, 2 * HD), F32), pltpu.SemaphoreType.DMA((3 * KV_PARTS + 2,))],
        limit=6, flops=2 * ROWS * depth * 2 * HD, moved=3,
    )(tokens, w_key, w_value, docs, table)


def unit_body(half, came, w, docs, docs_came, table, unit):
    own, other = halves()
    got = jnp.dot(came[...], w[...], preferred_element_type=F32)
    unit[own, :] = half[...]
    unit[other, :HD] = rotation(table[other, :])(got[:, :HD]).astype(BF16)
    unit[other, HD:] = got[:, HD:].astype(BF16)
    first = core_index() == 0
    a, b = docs[...], docs_came[...]
    tags = jnp.concatenate([jnp.where(first, a, b), jnp.where(first, b, a)], axis=1)
    tags = (tags + 1).astype(F32)
    unit[CHIP:, :] = jnp.broadcast_to(tags, (8, CHIP)).astype(BF16)


def project_unit(half, came, w, docs, docs_came, table):
    return call(
        unit_body, "project_unit", like(UNIT, 2 * HD), [VMEM] * 6, VMEM, limit=2,
        flops=2 * ROWS * w.shape[0] * 2 * HD,
    )(half, came, w, docs, docs_came, table)


Q_PARTS = 4


def q_body(tok, came, wq, table, out, wq_s, sems):
    half = wq.shape[1] // 2
    part = wq.shape[0] // Q_PARTS
    cols = pl.ds(pl.multiple_of(core_index() * half, half), half)
    copies = []
    for i in range(Q_PARTS):
        rows = pl.ds(i * part, part)
        copies += started([
            pltpu.make_async_copy(wq.at[rows, cols], wq_s.at[rows, :], sems.at[i])
        ])
    got = [None, None]
    for i in range(Q_PARTS):
        copies[i].wait()
        rows = slice(i * part, (i + 1) * part)
        for side, src in enumerate((tok, came)):
            more = jnp.dot(src[:, rows], wq_s[rows, :], preferred_element_type=F32)
            got[side] = more if i == 0 else got[side] + more
    for side, span in enumerate(halves()):
        rot = rotation(table[span, :])
        for h in range(half // HD):
            out[h, span, :] = rot(got[side][:, h * HD : (h + 1) * HD]).astype(BF16)


def project_q(tokens, came, w_query, table):
    depth, width = w_query.shape
    return call(
        q_body, "project_q", like(width // 2 // HD, CHIP, HD), [VMEM, VMEM, HBM, VMEM], VMEM,
        [pltpu.VMEM((depth, width // 2), BF16), pltpu.SemaphoreType.DMA((Q_PARTS,))],
        limit=8, flops=2 * CHIP * depth * width // 2, moved=6,
    )(tokens, came, w_query, table)


NONE = 99
NEAR = ((1, 2, 3), (4, 8, NONE))
MIDDLE = ((8, 9, NONE, NONE), (2, 6, 3, 7))
LAST = ((4, 5, 6, 7), (1, 5, 9, NONE))


def fill(out, slots, late):
    place = lax.axis_index("ctx")
    column = lax.rem(lax.div(place, 2), 4)
    skip = jnp.where((lax.rem(place, 2) == 1) & (column >= late), 1, 0)
    for i in range(out.shape[0] // UNIT):
        out[i * UNIT : (i + 1) * UNIT, :] = slots[jnp.minimum(skip + i, 3)]


def pairs_body(unit, r1, r2, out_b, out_c, slots):
    for i, src in enumerate((unit, r1, r2)):
        slots[i] = src[...]
    fill(out_b, slots, 2)
    fill(out_c, slots, 1)


def bundle_pairs(unit, r1, r2):
    pair = like(2 * UNIT, 2 * HD)
    return call(
        pairs_body, "bundle_pairs", (pair, pair), [VMEM] * 3, (VMEM,) * 2,
        [pltpu.VMEM((3, UNIT, 2 * HD), BF16)], limit=2,
    )(unit, r1, r2)


def row_body(unit, r1, r2, r3, after, out_a, slots):
    for i, src in enumerate((unit, r1, r2, r3)):
        slots[i] = src[...]
    fill(out_a, slots, 3)


def bundle_row(unit, r1, r2, r3, after):
    return call(
        row_body, "bundle_row", like(4 * UNIT, 2 * HD), [VMEM] * 5, VMEM,
        [pltpu.VMEM((4, UNIT, 2 * HD), BF16)], limit=2,
    )(unit, r1, r2, r3, after)


CONTRACT = (((1,), (1,)), ((), ()))


def tags_of(unit):
    tags = unit[CHIP:UNIT, :].astype(F32)
    return tags, jnp.transpose(tags, (1, 0))[:, 0:1]


def with_ones(values):
    return jnp.concatenate([values, jnp.ones((CHIP, HD), BF16)], axis=1)


def add_units(queries, units, steps, q_tag, before, after):
    place = lax.axis_index("ctx")
    odd = lax.rem(place, 2) == 1
    chip = lax.div(place, 2)
    for i, (block, even_step, odd_step) in enumerate(zip(units, *steps)):
        valid = chip >= jnp.where(odd, odd_step, even_step)
        k_tag = block[CHIP:, :].astype(F32)[0:1, :]
        bias = jnp.where((k_tag == q_tag) & valid, 0.0, -1e30)
        keys = block[:CHIP, :HD]
        values = with_ones(block[:CHIP, HD:])
        for h in range(after[0].shape[0]):
            s = lax.dot_general(queries(h), keys, CONTRACT, preferred_element_type=F32)
            s = s * SCALE + bias
            if i == 0:
                old, old_sum, old_acc = before(h)
            else:
                old, old_sum, old_acc = (ref[h] for ref in after)
            top = jnp.maximum(old, jnp.max(s, axis=1, keepdims=True))
            fade = jnp.exp2(old - top)
            w = jnp.exp2(s - jnp.concatenate([top, top], axis=1)).astype(BF16)
            got = jnp.dot(w, values, preferred_element_type=F32)
            after[0][h] = top
            after[1][h] = fade * old_sum + got[:, HD:]
            after[2][h] = fade * old_acc + got[:, :HD]


def parts(src):
    return [src[i * UNIT : (i + 1) * UNIT, :] for i in range(src.shape[0] // UNIT)]


def near_body(qs, unit, r1, r2, r3, m_s, l_s, acc):
    tags, q_tag = tags_of(unit)
    rows = lax.broadcasted_iota(jnp.int32, (CHIP, CHIP), 0)
    cols = lax.broadcasted_iota(jnp.int32, (CHIP, CHIP), 1)
    bias = jnp.where((tags[0:1, :] == q_tag) & (cols <= rows), 0.0, -1e30)
    keys, values = unit[:CHIP, :HD], with_ones(unit[:CHIP, HD:])
    for h in range(qs.shape[0]):
        s = lax.dot_general(qs[h], keys, CONTRACT, preferred_element_type=F32)
        s = s * SCALE + bias
        top = jnp.max(s, axis=1, keepdims=True)
        got = jnp.dot(jnp.exp2(s - top).astype(BF16), values, preferred_element_type=F32)
        m_s[h] = jnp.broadcast_to(top, (CHIP, HD))
        l_s[h] = got[:, HD:]
        acc[h] = got[:, :HD]
    state = (m_s, l_s, acc)
    units = [src[...] for src in (r1, r2, r3)]
    add_units(lambda h: qs[h], units, NEAR, q_tag, lambda h: [ref[h] for ref in state], state)


def attend_near(qs, unit, r1, r2, r3):
    heads = qs.shape[0]
    state = like(heads, CHIP, HD, dtype=F32)
    return call(
        near_body, "attend_near", (state, state, state), [VMEM] * 5, (VMEM,) * 3, limit=8,
        flops=4 * heads * CHIP * 4 * CHIP * HD, exps=heads * CHIP * 4 * CHIP,
    )(qs, unit, r1, r2, r3)


def middle_body(qs, m_in, l_in, acc_in, unit, far_b, far_c, m_s, l_s, acc):
    before = (m_in, l_in, acc_in)
    add_units(
        lambda h: qs[h], parts(far_b) + parts(far_c), MIDDLE, tags_of(unit)[1],
        lambda h: [ref[h] for ref in before], (m_s, l_s, acc),
    )


def attend_middle(qs, m_in, l_in, acc_in, unit, far_b, far_c):
    heads = qs.shape[0]
    state = like(heads, CHIP, HD, dtype=F32)
    return call(
        middle_body, "attend_middle", (state,) * 3, [VMEM] * 7, (VMEM,) * 3, limit=8,
        flops=4 * heads * CHIP * 4 * CHIP * HD, exps=heads * CHIP * 4 * CHIP,
    )(qs, m_in, l_in, acc_in, unit, far_b, far_c)


def attend_last(side, qs, m_in, l_in, acc_in, unit, far_a):
    heads = qs.shape[0]

    def body(qs, m_in, l_in, acc_in, unit, far_a, out, tag_s, m_s, l_s, acc):
        rows = halves()[side]
        before = (m_in, l_in, acc_in)
        tag_s[...] = jnp.broadcast_to(tags_of(unit)[1], (CHIP, HD))
        add_units(
            lambda h: qs[h, rows, :], parts(far_a), LAST, tag_s[rows, :][:, 0:1],
            lambda h: [ref[h, rows, :] for ref in before], (m_s, l_s, acc),
        )
        for h in range(heads):
            out[:, h * HD : (h + 1) * HD] = (acc[h] / l_s[h]).astype(BF16)

    state = pltpu.VMEM((heads, ROWS, HD), F32)
    return call(
        body, "attend_last", like(ROWS, heads * HD), [VMEM] * 6, VMEM,
        [pltpu.VMEM((CHIP, HD), F32), state, state, state],
        limit=8, flops=4 * heads * ROWS * 4 * CHIP * HD, exps=heads * ROWS * 4 * CHIP,
    )(qs, m_in, l_in, acc_in, unit, far_a)


def project_out(xm, xr, w_out, groups, shifts, dtypes):
    depth = xm.shape[1]
    width = w_out.shape[1] // groups

    def body(xm, xr, w, *outs):
        core = core_index()
        own = pl.ds(pl.multiple_of(core * depth, depth), depth)
        other = pl.ds(pl.multiple_of((1 - core) * depth, depth), depth)
        for (even, odd), out in zip(shifts, outs):
            shift = jnp.where(core == 0, even, odd)
            group = lax.rem(lax.axis_index("head") + shift, groups)
            cols = pl.ds(pl.multiple_of(group * width, width), width)
            got = jnp.dot(xm[...], w[own, cols], preferred_element_type=F32)
            got += jnp.dot(xr[...], w[other, cols], preferred_element_type=F32)
            out[...] = got.astype(out.dtype)

    return call(
        body, "project_out", tuple(like(ROWS, width, dtype=d) for d in dtypes), [VMEM] * 3,
        (VMEM,) * len(shifts), limit=4,
        flops=2 * ROWS * 2 * depth * width * len(shifts), moved=2 * len(shifts),
    )(xm, xr, w_out)


def passing_body(own, came, out):
    out[...] = (own[...] + came[...].astype(F32)).astype(BF16)


def add_passing(own, came):
    return call(passing_body, "add_passing", like(*own.shape), [VMEM] * 2, VMEM, limit=2)(own, came)


def total_body(own, first, second, out):
    out[...] = (own[...] + first[...].astype(F32) + second[...].astype(F32)).astype(BF16)


def add_total(own, first, second):
    return call(total_body, "add_total", like(*own.shape), [VMEM] * 3, VMEM, limit=2)(
        own, first, second
    )


def shards(tokens, w_query, w_key, w_value, w_out, doc_ids):
    ranks = lax.axis_size("ctx")
    groups = lax.axis_size("head")
    table = jnp.asarray(rope_table(ranks * ROWS))

    def swap(value):
        return lax.ppermute(value, "ctx", [(r, r ^ 1) for r in range(ranks)])

    def along(value, even, odd):
        moves = [(r, 2 * (odd if r % 2 else even)(r // 2) + r % 2) for r in range(ranks)]
        return lax.ppermute(value, "ctx", moves)

    def ahead(step):
        return lambda chip: (chip + step) % (ranks // 2)

    def in_row(step):
        return lambda chip: chip // 4 * 4 + (chip + step) % 4

    docs = doc_ids.reshape(1, -1)
    came, docs_came = swap(tokens), swap(docs)
    tokens, w_key, w_value, w_query, table, docs = (
        pltpu.with_memory_space_constraint(a, pltpu.HBM)
        for a in (tokens, w_key, w_value, w_query, table, docs)
    )
    half, tokens, w_kv, docs, table = project_own(tokens, w_key, w_value, docs, table)
    unit = project_unit(half, came, w_kv, docs, docs_came, table)
    r1 = along(unit, ahead(1), ahead(4))
    r2 = along(unit, ahead(2), ahead(8))
    r3 = along(unit, ahead(3), ahead(12))
    r1, r2, r3, came = lax.optimization_barrier((r1, r2, r3, came))
    out_b, out_c = bundle_pairs(unit, r1, r2)
    far_b = along(out_b, ahead(8), in_row(2))
    far_c = along(out_c, ahead(12), in_row(3))
    far_a = along(bundle_row(unit, r1, r2, r3, out_c), ahead(4), in_row(1))
    qs = project_q(tokens, came, w_query, table)
    state = attend_near(qs, unit, r1, r2, r3)
    state = attend_middle(qs, *state, unit, far_b, far_c)
    xr = swap(attend_last(1, qs, *state, unit, far_a))
    xm = attend_last(0, qs, *state, unit, far_a)

    def across(value, even, odd):
        moves = []
        for r in range(ranks):
            for g in range(groups):
                to = (g + (odd if r % 2 else even)) % groups
                moves.append((r * groups + g, r * groups + to))
        return lax.ppermute(value, ("ctx", "head"), moves)

    (opposite,) = project_out(xm, xr, w_out, groups, ((2, 2),), (BF16,))
    passing = across(opposite, 1, 3)
    direct, onward, total = project_out(
        xm, xr, w_out, groups, ((3, 1), (1, 3), (0, 0)), (BF16, F32, F32)
    )
    direct = across(direct, 3, 1)
    onward = across(add_passing(onward, passing), 1, 3)
    return add_total(total, direct, onward)


def solution(mesh):
    return jax.shard_map(
        shards,
        mesh=mesh,
        in_specs=(
            P("ctx", None),
            P(None, "head"),
            P(None, "head"),
            P(None, "head"),
            P("head", None),
            P("ctx"),
        ),
        out_specs=P("ctx", "head"),
        check_vma=False,
    )
```

```python
import math

import jax
import jax.numpy as jnp
import numpy as np
from jax import lax
from jax.experimental import pallas as pl
from jax.experimental.pallas import tpu as pltpu
from jax.sharding import PartitionSpec as P

HD = 128
ROWS = 128
UNIT = 264
F32 = jnp.float32
BF16 = jnp.bfloat16
MIB = 1 << 20
SCALE = math.log2(math.e) / math.sqrt(HD)


def rope_table(count):
    half = HD // 2
    freqs = 500000.0 ** (-2.0 * np.arange(half, dtype=np.float64) / HD)
    angles = np.arange(count, dtype=np.float64)[:, None] * freqs[None, :]
    return np.concatenate([np.cos(angles), np.sin(angles)], axis=1).astype(np.float32)


def rotation(table):
    half = HD // 2
    cosine, sine = table[:, :half], table[:, half:]
    cosine = jnp.concatenate([cosine, cosine], axis=1)
    sine = jnp.concatenate([-sine, sine], axis=1)
    return lambda t: t * cosine + pltpu.roll(t, half, 1) * sine


SMEM = pl.BlockSpec(memory_space=pltpu.SMEM)
VMEM = pl.BlockSpec(memory_space=pltpu.VMEM)
HBM = pl.BlockSpec(memory_space=pltpu.HBM)


def like(*dims, dtype=BF16):
    return jax.ShapeDtypeStruct(dims, dtype)


def call(body, name, out, ins, outs, scratch=(), limit=4, flops=0, moved=1, exps=0):
    return pl.pallas_call(
        body,
        out_shape=out,
        in_specs=ins,
        out_specs=outs,
        scratch_shapes=list(scratch),
        name=name,
        cost_estimate=pl.CostEstimate(
            flops=flops, bytes_accessed=moved * MIB, transcendentals=exps
        ),
        compiler_params=pltpu.CompilerParams(vmem_limit_bytes=limit * MIB),
    )


def core_index():
    return lax.rem(lax.axis_index("ctx"), 2)


def table_rows(table):
    return table.at[pl.ds(pl.multiple_of(lax.axis_index("ctx") * ROWS, ROWS), ROWS), :]


def started(copies):
    for copy in copies:
        copy.start()
    return copies


KV_PARTS = 4
CHIP = 2 * ROWS


def halves():
    core = core_index()
    own = pl.ds(pl.multiple_of(core * ROWS, ROWS), ROWS)
    other = pl.ds(pl.multiple_of((1 - core) * ROWS, ROWS), ROWS)
    return own, other


def own_body(tok, wk, wv, docs, table, half, tok_s, w_s, docs_s, table_s, acc, sems):
    part = tok.shape[1] // KV_PARTS
    cols = pl.ds(pl.multiple_of(core_index() * HD, HD), HD)
    copies = []
    for i in range(KV_PARTS):
        cut = pl.ds(i * part, part)
        copies.append(
            started([
                pltpu.make_async_copy(tok.at[:, cut], tok_s.at[:, cut], sems.at[3 * i]),
                pltpu.make_async_copy(
                    wk.at[cut, cols], w_s.at[cut, pl.ds(0, HD)], sems.at[3 * i + 1]
                ),
                pltpu.make_async_copy(
                    wv.at[cut, cols], w_s.at[cut, pl.ds(HD, HD)], sems.at[3 * i + 2]
                ),
            ])
        )
    first = pl.multiple_of(lax.div(lax.axis_index("ctx"), 2) * CHIP, CHIP)
    small = started([
        pltpu.make_async_copy(docs, docs_s, sems.at[3 * KV_PARTS]),
        pltpu.make_async_copy(table.at[pl.ds(first, CHIP), :], table_s, sems.at[3 * KV_PARTS + 1]),
    ])
    for i, group in enumerate(copies):
        for copy in group:
            copy.wait()
        cut = slice(i * part, (i + 1) * part)
        more = jnp.dot(tok_s[:, cut], w_s[cut, :], preferred_element_type=F32)
        if i == 0:
            acc[...] = more
        else:
            acc[...] += more
    for copy in small:
        copy.wait()
    rot = rotation(table_s[halves()[0], :])
    half[:, :HD] = rot(acc[:, :HD]).astype(BF16)
    half[:, HD:] = acc[:, HD:].astype(BF16)


def project_own(tokens, w_key, w_value, docs, table):
    depth = tokens.shape[1]
    return call(
        own_body, "project_own",
        (
            like(ROWS, 2 * HD),
            like(ROWS, depth),
            like(depth, 2 * HD),
            like(1, ROWS, dtype=jnp.int32),
            like(CHIP, HD, dtype=F32),
        ),
        [HBM] * 5, (VMEM,) * 5,
        [pltpu.VMEM((ROWS, 2 * HD), F32), pltpu.SemaphoreType.DMA((3 * KV_PARTS + 2,))],
        limit=6, flops=2 * ROWS * depth * 2 * HD, moved=3,
    )(tokens, w_key, w_value, docs, table)


def unit_body(half, came, w, docs, docs_came, table, unit):
    own, other = halves()
    got = jnp.dot(came[...], w[...], preferred_element_type=F32)
    unit[own, :] = half[...]
    unit[other, :HD] = rotation(table[other, :])(got[:, :HD]).astype(BF16)
    unit[other, HD:] = got[:, HD:].astype(BF16)
    first = core_index() == 0
    a, b = docs[...], docs_came[...]
    tags = jnp.concatenate([jnp.where(first, a, b), jnp.where(first, b, a)], axis=1)
    tags = (tags + 1).astype(F32)
    unit[CHIP:, :] = jnp.broadcast_to(tags, (8, CHIP)).astype(BF16)


def project_unit(half, came, w, docs, docs_came, table):
    return call(
        unit_body, "project_unit", like(UNIT, 2 * HD), [VMEM] * 6, VMEM, limit=2,
        flops=2 * ROWS * w.shape[0] * 2 * HD,
    )(half, came, w, docs, docs_came, table)


Q_PARTS = 4


def q_body(tok, came, wq, table, out, wq_s, sems):
    half = wq.shape[1] // 2
    part = wq.shape[0] // Q_PARTS
    cols = pl.ds(pl.multiple_of(core_index() * half, half), half)
    copies = []
    for i in range(Q_PARTS):
        rows = pl.ds(i * part, part)
        copies += started([
            pltpu.make_async_copy(wq.at[rows, cols], wq_s.at[rows, :], sems.at[i])
        ])
    got = [None, None]
    for i in range(Q_PARTS):
        copies[i].wait()
        rows = slice(i * part, (i + 1) * part)
        for side, src in enumerate((tok, came)):
            more = jnp.dot(src[:, rows], wq_s[rows, :], preferred_element_type=F32)
            got[side] = more if i == 0 else got[side] + more
    for side, span in enumerate(halves()):
        rot = rotation(table[span, :])
        for h in range(half // HD):
            out[h, span, :] = rot(got[side][:, h * HD : (h + 1) * HD]).astype(BF16)


def project_q(tokens, came, w_query, table):
    depth, width = w_query.shape
    return call(
        q_body, "project_q", like(width // 2 // HD, CHIP, HD), [VMEM, VMEM, HBM, VMEM], VMEM,
        [pltpu.VMEM((depth, width // 2), BF16), pltpu.SemaphoreType.DMA((Q_PARTS,))],
        limit=8, flops=2 * CHIP * depth * width // 2, moved=6,
    )(tokens, came, w_query, table)


NONE = 99
NEAR = ((1, 2, 3), (4, 8, NONE))
MIDDLE = ((8, 9, NONE, NONE), (2, 6, 3, 7))
LAST = ((4, 5, 6, 7), (1, 5, 9, NONE))


def fill(out, slots, late):
    place = lax.axis_index("ctx")
    column = lax.rem(lax.div(place, 2), 4)
    skip = jnp.where((lax.rem(place, 2) == 1) & (column >= late), 1, 0)
    for i in range(out.shape[0] // UNIT):
        out[i * UNIT : (i + 1) * UNIT, :] = slots[jnp.minimum(skip + i, 3)]


def pairs_body(unit, r1, r2, out_b, out_c, slots):
    for i, src in enumerate((unit, r1, r2)):
        slots[i] = src[...]
    fill(out_b, slots, 2)
    fill(out_c, slots, 1)


def bundle_pairs(unit, r1, r2):
    pair = like(2 * UNIT, 2 * HD)
    return call(
        pairs_body, "bundle_pairs", (pair, pair), [VMEM] * 3, (VMEM,) * 2,
        [pltpu.VMEM((3, UNIT, 2 * HD), BF16)], limit=2,
    )(unit, r1, r2)


def row_body(unit, r1, r2, r3, after, out_a, slots):
    for i, src in enumerate((unit, r1, r2, r3)):
        slots[i] = src[...]
    fill(out_a, slots, 3)


def bundle_row(unit, r1, r2, r3, after):
    return call(
        row_body, "bundle_row", like(4 * UNIT, 2 * HD), [VMEM] * 5, VMEM,
        [pltpu.VMEM((4, UNIT, 2 * HD), BF16)], limit=2,
    )(unit, r1, r2, r3, after)


CONTRACT = (((1,), (1,)), ((), ()))


def tags_of(unit):
    tags = unit[CHIP:UNIT, :].astype(F32)
    return tags, jnp.transpose(tags, (1, 0))[:, 0:1]


def with_ones(values):
    return jnp.concatenate([values, jnp.ones((CHIP, HD), BF16)], axis=1)


def add_units(queries, units, steps, q_tag, before, after):
    place = lax.axis_index("ctx")
    odd = lax.rem(place, 2) == 1
    chip = lax.div(place, 2)
    for i, (block, even_step, odd_step) in enumerate(zip(units, *steps)):
        valid = chip >= jnp.where(odd, odd_step, even_step)
        k_tag = block[CHIP:, :].astype(F32)[0:1, :]
        bias = jnp.where((k_tag == q_tag) & valid, 0.0, -1e30)
        keys = block[:CHIP, :HD]
        values = with_ones(block[:CHIP, HD:])
        for h in range(after[0].shape[0]):
            s = lax.dot_general(queries(h), keys, CONTRACT, preferred_element_type=F32)
            s = s * SCALE + bias
            if i == 0:
                old, old_sum, old_acc = before(h)
            else:
                old, old_sum, old_acc = (ref[h] for ref in after)
            top = jnp.maximum(old, jnp.max(s, axis=1, keepdims=True))
            fade = jnp.exp2(old - top)
            w = jnp.exp2(s - jnp.concatenate([top, top], axis=1)).astype(BF16)
            got = jnp.dot(w, values, preferred_element_type=F32)
            after[0][h] = top
            after[1][h] = fade * old_sum + got[:, HD:]
            after[2][h] = fade * old_acc + got[:, :HD]


def parts(src):
    return [src[i * UNIT : (i + 1) * UNIT, :] for i in range(src.shape[0] // UNIT)]


def near_body(qs, unit, r1, r2, r3, m_s, l_s, acc):
    tags, q_tag = tags_of(unit)
    rows = lax.broadcasted_iota(jnp.int32, (CHIP, CHIP), 0)
    cols = lax.broadcasted_iota(jnp.int32, (CHIP, CHIP), 1)
    bias = jnp.where((tags[0:1, :] == q_tag) & (cols <= rows), 0.0, -1e30)
    keys, values = unit[:CHIP, :HD], with_ones(unit[:CHIP, HD:])
    for h in range(qs.shape[0]):
        s = lax.dot_general(qs[h], keys, CONTRACT, preferred_element_type=F32)
        s = s * SCALE + bias
        top = jnp.max(s, axis=1, keepdims=True)
        got = jnp.dot(jnp.exp2(s - top).astype(BF16), values, preferred_element_type=F32)
        m_s[h] = jnp.broadcast_to(top, (CHIP, HD))
        l_s[h] = got[:, HD:]
        acc[h] = got[:, :HD]
    state = (m_s, l_s, acc)
    units = [src[...] for src in (r1, r2, r3)]
    add_units(lambda h: qs[h], units, NEAR, q_tag, lambda h: [ref[h] for ref in state], state)


def attend_near(qs, unit, r1, r2, r3):
    heads = qs.shape[0]
    state = like(heads, CHIP, HD, dtype=F32)
    return call(
        near_body, "attend_near", (state, state, state), [VMEM] * 5, (VMEM,) * 3, limit=8,
        flops=4 * heads * CHIP * 4 * CHIP * HD, exps=heads * CHIP * 4 * CHIP,
    )(qs, unit, r1, r2, r3)


def middle_body(qs, m_in, l_in, acc_in, unit, far_b, far_c, m_s, l_s, acc):
    before = (m_in, l_in, acc_in)
    add_units(
        lambda h: qs[h], parts(far_b) + parts(far_c), MIDDLE, tags_of(unit)[1],
        lambda h: [ref[h] for ref in before], (m_s, l_s, acc),
    )


def attend_middle(qs, m_in, l_in, acc_in, unit, far_b, far_c):
    heads = qs.shape[0]
    state = like(heads, CHIP, HD, dtype=F32)
    return call(
        middle_body, "attend_middle", (state,) * 3, [VMEM] * 7, (VMEM,) * 3, limit=8,
        flops=32 * heads * CHIP * 4 * CHIP * HD, exps=heads * CHIP * 4 * CHIP,
    )(qs, m_in, l_in, acc_in, unit, far_b, far_c)


def attend_last(side, qs, m_in, l_in, acc_in, unit, far_a):
    heads = qs.shape[0]

    def body(qs, m_in, l_in, acc_in, unit, far_a, out, tag_s, m_s, l_s, acc):
        rows = halves()[side]
        before = (m_in, l_in, acc_in)
        tag_s[...] = jnp.broadcast_to(tags_of(unit)[1], (CHIP, HD))
        add_units(
            lambda h: qs[h, rows, :], parts(far_a), LAST, tag_s[rows, :][:, 0:1],
            lambda h: [ref[h, rows, :] for ref in before], (m_s, l_s, acc),
        )
        for h in range(heads):
            out[:, h * HD : (h + 1) * HD] = (acc[h] / l_s[h]).astype(BF16)

    state = pltpu.VMEM((heads, ROWS, HD), F32)
    return call(
        body, "attend_last", like(ROWS, heads * HD), [VMEM] * 6, VMEM,
        [pltpu.VMEM((CHIP, HD), F32), state, state, state],
        limit=8, flops=4 * heads * ROWS * 4 * CHIP * HD, exps=heads * ROWS * 4 * CHIP,
    )(qs, m_in, l_in, acc_in, unit, far_a)


def project_out(xm, xr, w_out, groups, parts, dtype):
    depth = xm.shape[1]
    width = w_out.shape[1] // groups
    half = width // 2

    def body(xm, xr, w, *outs):
        core = core_index()
        own = pl.ds(pl.multiple_of(core * depth, depth), depth)
        other = pl.ds(pl.multiple_of((1 - core) * depth, depth), depth)
        for (shift, side), out in zip(parts, outs):
            group = lax.rem(lax.axis_index("head") + shift, groups)
            cols = pl.ds(pl.multiple_of(group * width + side * half, half), half)
            got = jnp.dot(xm[...], w[own, cols], preferred_element_type=F32)
            got += jnp.dot(xr[...], w[other, cols], preferred_element_type=F32)
            out[...] = got.astype(dtype)

    return call(
        body, "project_out", (like(ROWS, half, dtype=dtype),) * len(parts), [VMEM] * 3,
        (VMEM,) * len(parts), limit=4,
        flops=2 * ROWS * 2 * depth * half * len(parts), moved=len(parts),
    )(xm, xr, w_out)


def add_body(a, b, p, q, out_a, out_b):
    out_a[...] = (a[...] + p[...].astype(F32)).astype(BF16)
    out_b[...] = (b[...] + q[...].astype(F32)).astype(BF16)


def add_passing(a, b, p, q):
    out = like(*p.shape)
    return call(add_body, "add_passing", (out, out), [VMEM] * 4, (VMEM,) * 2, limit=2)(a, b, p, q)


def total_body(own_a, own_b, left_a, left_b, right_a, right_b, out):
    half = own_a.shape[1]
    for at, pieces in ((0, (own_a, left_a, right_a)), (half, (own_b, left_b, right_b))):
        total = pieces[0][...] + pieces[1][...].astype(F32) + pieces[2][...].astype(F32)
        out[:, at : at + half] = total.astype(BF16)


def add_total(*pieces):
    rows, half = pieces[0].shape
    return call(total_body, "add_total", like(rows, 2 * half), [VMEM] * 6, VMEM, limit=2)(*pieces)


def shards(tokens, w_query, w_key, w_value, w_out, doc_ids):
    ranks = lax.axis_size("ctx")
    groups = lax.axis_size("head")
    table = jnp.asarray(rope_table(ranks * ROWS))

    def swap(value):
        return lax.ppermute(value, "ctx", [(r, r ^ 1) for r in range(ranks)])

    def along(value, even, odd):
        moves = [(r, 2 * (odd if r % 2 else even)(r // 2) + r % 2) for r in range(ranks)]
        return lax.ppermute(value, "ctx", moves)

    def ahead(step):
        return lambda chip: (chip + step) % (ranks // 2)

    def in_row(step):
        return lambda chip: chip // 4 * 4 + (chip + step) % 4

    docs = doc_ids.reshape(1, -1)
    came, docs_came = swap(tokens), swap(docs)
    tokens, w_key, w_value, w_query, table, docs = (
        pltpu.with_memory_space_constraint(a, pltpu.HBM)
        for a in (tokens, w_key, w_value, w_query, table, docs)
    )
    half, tokens, w_kv, docs, table = project_own(tokens, w_key, w_value, docs, table)
    unit = project_unit(half, came, w_kv, docs, docs_came, table)
    r1 = along(unit, ahead(1), ahead(4))
    r2 = along(unit, ahead(2), ahead(8))
    r3 = along(unit, ahead(3), ahead(12))
    r1, r2, came = lax.optimization_barrier((r1, r2, came))
    out_b, out_c = bundle_pairs(unit, r1, r2)
    far_b = along(out_b, ahead(8), in_row(2))
    far_c = along(out_c, ahead(12), in_row(3))
    far_a = along(bundle_row(unit, r1, r2, r3, out_c), ahead(4), in_row(1))
    qs = project_q(tokens, came, w_query, table)
    state = attend_near(qs, unit, r1, r2, r3)
    state = attend_middle(qs, *state, unit, far_b, far_c)
    xr = swap(attend_last(1, qs, *state, unit, far_a))
    xm = attend_last(0, qs, *state, unit, far_a)

    def shift(value, step):
        return lax.ppermute(value, "head", [(g, (g + step) % groups) for g in range(groups)])

    a2, b2 = project_out(xm, xr, w_out, groups, ((2, 0), (2, 1)), BF16)
    pass_a, pass_b = shift(a2, 1), shift(b2, -1)
    b1, a3 = project_out(xm, xr, w_out, groups, ((1, 1), (3, 0)), BF16)
    left_b, right_a = shift(b1, 1), shift(a3, -1)
    a1, b3, a0, b0 = project_out(xm, xr, w_out, groups, ((1, 0), (3, 1), (0, 0), (0, 1)), F32)
    a1, b3 = add_passing(a1, b3, pass_a, pass_b)
    left_a, right_b = shift(a1, 1), shift(b3, -1)
    return add_total(a0, b0, left_a, left_b, right_a, right_b)


def solution(mesh):
    return jax.shard_map(
        shards,
        mesh=mesh,
        in_specs=(
            P("ctx", None),
            P(None, "head"),
            P(None, "head"),
            P(None, "head"),
            P("head", None),
            P("ctx"),
        ),
        out_specs=P("ctx", "head"),
        check_vma=False,
    )
```

```python
import math

import jax
import jax.numpy as jnp
import numpy as np
from jax import lax
from jax.experimental import pallas as pl
from jax.experimental.pallas import tpu as pltpu
from jax.sharding import PartitionSpec as P

HD = 128
ROWS = 128
UNIT = 264
F32 = jnp.float32
BF16 = jnp.bfloat16
MIB = 1 << 20
SCALE = math.log2(math.e) / math.sqrt(HD)


def rope_table(count):
    half = HD // 2
    freqs = 500000.0 ** (-2.0 * np.arange(half, dtype=np.float64) / HD)
    angles = np.arange(count, dtype=np.float64)[:, None] * freqs[None, :]
    return np.concatenate([np.cos(angles), np.sin(angles)], axis=1).astype(np.float32)


def rotation(table):
    half = HD // 2
    cosine, sine = table[:, :half], table[:, half:]
    cosine = jnp.concatenate([cosine, cosine], axis=1)
    sine = jnp.concatenate([-sine, sine], axis=1)
    return lambda t: t * cosine + pltpu.roll(t, half, 1) * sine


SMEM = pl.BlockSpec(memory_space=pltpu.SMEM)
VMEM = pl.BlockSpec(memory_space=pltpu.VMEM)
HBM = pl.BlockSpec(memory_space=pltpu.HBM)


def like(*dims, dtype=BF16):
    return jax.ShapeDtypeStruct(dims, dtype)


def call(body, name, out, ins, outs, scratch=(), limit=4, flops=0, moved=1, exps=0):
    return pl.pallas_call(
        body,
        out_shape=out,
        in_specs=ins,
        out_specs=outs,
        scratch_shapes=list(scratch),
        name=name,
        cost_estimate=pl.CostEstimate(
            flops=flops, bytes_accessed=moved * MIB, transcendentals=exps
        ),
        compiler_params=pltpu.CompilerParams(vmem_limit_bytes=limit * MIB),
    )


def core_index():
    return lax.rem(lax.axis_index("ctx"), 2)


def table_rows(table):
    return table.at[pl.ds(pl.multiple_of(lax.axis_index("ctx") * ROWS, ROWS), ROWS), :]


def started(copies):
    for copy in copies:
        copy.start()
    return copies


KV_PARTS = 4
CHIP = 2 * ROWS


def halves():
    core = core_index()
    own = pl.ds(pl.multiple_of(core * ROWS, ROWS), ROWS)
    other = pl.ds(pl.multiple_of((1 - core) * ROWS, ROWS), ROWS)
    return own, other


def own_body(tok, wk, wv, docs, table, half, tok_s, w_s, docs_s, table_s, acc, sems):
    part = tok.shape[1] // KV_PARTS
    cols = pl.ds(pl.multiple_of(core_index() * HD, HD), HD)
    copies = []
    for i in range(KV_PARTS):
        cut = pl.ds(i * part, part)
        copies.append(
            started([
                pltpu.make_async_copy(tok.at[:, cut], tok_s.at[:, cut], sems.at[3 * i]),
                pltpu.make_async_copy(
                    wk.at[cut, cols], w_s.at[cut, pl.ds(0, HD)], sems.at[3 * i + 1]
                ),
                pltpu.make_async_copy(
                    wv.at[cut, cols], w_s.at[cut, pl.ds(HD, HD)], sems.at[3 * i + 2]
                ),
            ])
        )
    first = pl.multiple_of(lax.div(lax.axis_index("ctx"), 2) * CHIP, CHIP)
    small = started([
        pltpu.make_async_copy(docs, docs_s, sems.at[3 * KV_PARTS]),
        pltpu.make_async_copy(table.at[pl.ds(first, CHIP), :], table_s, sems.at[3 * KV_PARTS + 1]),
    ])
    for i, group in enumerate(copies):
        for copy in group:
            copy.wait()
        cut = slice(i * part, (i + 1) * part)
        more = jnp.dot(tok_s[:, cut], w_s[cut, :], preferred_element_type=F32)
        if i == 0:
            acc[...] = more
        else:
            acc[...] += more
    for copy in small:
        copy.wait()
    rot = rotation(table_s[halves()[0], :])
    half[:, :HD] = rot(acc[:, :HD]).astype(BF16)
    half[:, HD:] = acc[:, HD:].astype(BF16)


def project_own(tokens, w_key, w_value, docs, table):
    depth = tokens.shape[1]
    return call(
        own_body, "project_own",
        (
            like(ROWS, 2 * HD),
            like(ROWS, depth),
            like(depth, 2 * HD),
            like(1, ROWS, dtype=jnp.int32),
            like(CHIP, HD, dtype=F32),
        ),
        [HBM] * 5, (VMEM,) * 5,
        [pltpu.VMEM((ROWS, 2 * HD), F32), pltpu.SemaphoreType.DMA((3 * KV_PARTS + 2,))],
        limit=6, flops=2 * ROWS * depth * 2 * HD, moved=3,
    )(tokens, w_key, w_value, docs, table)


def unit_body(half, came, w, docs, docs_came, table, unit):
    own, other = halves()
    got = jnp.dot(came[...], w[...], preferred_element_type=F32)
    unit[own, :] = half[...]
    unit[other, :HD] = rotation(table[other, :])(got[:, :HD]).astype(BF16)
    unit[other, HD:] = got[:, HD:].astype(BF16)
    first = core_index() == 0
    a, b = docs[...], docs_came[...]
    tags = jnp.concatenate([jnp.where(first, a, b), jnp.where(first, b, a)], axis=1)
    tags = (tags + 1).astype(F32)
    unit[CHIP:, :] = jnp.broadcast_to(tags, (8, CHIP)).astype(BF16)


def project_unit(half, came, w, docs, docs_came, table):
    return call(
        unit_body, "project_unit", like(UNIT, 2 * HD), [VMEM] * 6, VMEM, limit=2,
        flops=2 * ROWS * w.shape[0] * 2 * HD,
    )(half, came, w, docs, docs_came, table)


Q_PARTS = 4


def q_body(tok, came, wq, table, out, wq_s, sems):
    half = wq.shape[1] // 2
    part = wq.shape[0] // Q_PARTS
    cols = pl.ds(pl.multiple_of(core_index() * half, half), half)
    copies = []
    for i in range(Q_PARTS):
        rows = pl.ds(i * part, part)
        copies += started([
            pltpu.make_async_copy(wq.at[rows, cols], wq_s.at[rows, :], sems.at[i])
        ])
    got = [None, None]
    for i in range(Q_PARTS):
        copies[i].wait()
        rows = slice(i * part, (i + 1) * part)
        for side, src in enumerate((tok, came)):
            more = jnp.dot(src[:, rows], wq_s[rows, :], preferred_element_type=F32)
            got[side] = more if i == 0 else got[side] + more
    for side, span in enumerate(halves()):
        rot = rotation(table[span, :])
        for h in range(half // HD):
            out[h, span, :] = rot(got[side][:, h * HD : (h + 1) * HD]).astype(BF16)


def project_q(tokens, came, w_query, table):
    depth, width = w_query.shape
    return call(
        q_body, "project_q", like(width // 2 // HD, CHIP, HD), [VMEM, VMEM, HBM, VMEM], VMEM,
        [pltpu.VMEM((depth, width // 2), BF16), pltpu.SemaphoreType.DMA((Q_PARTS,))],
        limit=8, flops=2 * CHIP * depth * width // 2, moved=6,
    )(tokens, came, w_query, table)


NONE = 99
NEAR = ((1, 2, 3), (4, 8, NONE))
MIDDLE = ((8, 9, 4, NONE), (2, 6, 3, 7))
LAST = ((5, 6, 7), (1, 5, 9))


def fill(out, slots, late, even):
    place = lax.axis_index("ctx")
    column = lax.rem(lax.div(place, 2), 4)
    skip = jnp.where(lax.rem(place, 2) == 0, even, jnp.where(column >= late, 1, 0))
    for i in range(out.shape[0] // UNIT):
        out[i * UNIT : (i + 1) * UNIT, :] = slots[skip + i]


def pairs_body(unit, r1, r2, out_b, out_c, slots):
    for i, src in enumerate((unit, r1, r2)):
        slots[i] = src[...]
    fill(out_b, slots, 2, 0)
    fill(out_c, slots, 1, 0)


def bundle_pairs(unit, r1, r2):
    pair = like(2 * UNIT, 2 * HD)
    return call(
        pairs_body, "bundle_pairs", (pair, pair), [VMEM] * 3, (VMEM,) * 2,
        [pltpu.VMEM((3, UNIT, 2 * HD), BF16)], limit=2,
    )(unit, r1, r2)


def row_body(unit, r1, r2, r3, after, out_a, slots):
    for i, src in enumerate((unit, r1, r2, r3)):
        slots[i] = src[...]
    fill(out_a, slots, 3, 1)


def bundle_row(unit, r1, r2, r3, after):
    return call(
        row_body, "bundle_row", like(3 * UNIT, 2 * HD), [VMEM] * 5, VMEM,
        [pltpu.VMEM((4, UNIT, 2 * HD), BF16)], limit=2,
    )(unit, r1, r2, r3, after)


CONTRACT = (((1,), (1,)), ((), ()))


def tags_of(unit):
    tags = unit[CHIP:UNIT, :].astype(F32)
    return tags, jnp.transpose(tags, (1, 0))[:, 0:1]


def with_ones(values):
    return jnp.concatenate([values, jnp.ones((CHIP, HD), BF16)], axis=1)


def add_units(queries, units, steps, q_tag, before, after):
    place = lax.axis_index("ctx")
    odd = lax.rem(place, 2) == 1
    chip = lax.div(place, 2)
    for i, (block, even_step, odd_step) in enumerate(zip(units, *steps)):
        valid = chip >= jnp.where(odd, odd_step, even_step)
        k_tag = block[CHIP:, :].astype(F32)[0:1, :]
        bias = jnp.where((k_tag == q_tag) & valid, 0.0, -1e30)
        keys = block[:CHIP, :HD]
        values = with_ones(block[:CHIP, HD:])
        for h in range(after[0].shape[0]):
            s = lax.dot_general(queries(h), keys, CONTRACT, preferred_element_type=F32)
            s = s * SCALE + bias
            if i == 0:
                old, old_sum, old_acc = before(h)
            else:
                old, old_sum, old_acc = (ref[h] for ref in after)
            top = jnp.maximum(old, jnp.max(s, axis=1, keepdims=True))
            fade = jnp.exp2(old - top)
            w = jnp.exp2(s - jnp.concatenate([top, top], axis=1)).astype(BF16)
            got = jnp.dot(w, values, preferred_element_type=F32)
            after[0][h] = top
            after[1][h] = fade * old_sum + got[:, HD:]
            after[2][h] = fade * old_acc + got[:, :HD]


def parts(src):
    return [src[i * UNIT : (i + 1) * UNIT, :] for i in range(src.shape[0] // UNIT)]


def near_body(qs, unit, r1, r2, r3, m_s, l_s, acc):
    tags, q_tag = tags_of(unit)
    rows = lax.broadcasted_iota(jnp.int32, (CHIP, CHIP), 0)
    cols = lax.broadcasted_iota(jnp.int32, (CHIP, CHIP), 1)
    bias = jnp.where((tags[0:1, :] == q_tag) & (cols <= rows), 0.0, -1e30)
    keys, values = unit[:CHIP, :HD], with_ones(unit[:CHIP, HD:])
    for h in range(qs.shape[0]):
        s = lax.dot_general(qs[h], keys, CONTRACT, preferred_element_type=F32)
        s = s * SCALE + bias
        top = jnp.max(s, axis=1, keepdims=True)
        got = jnp.dot(jnp.exp2(s - top).astype(BF16), values, preferred_element_type=F32)
        m_s[h] = jnp.broadcast_to(top, (CHIP, HD))
        l_s[h] = got[:, HD:]
        acc[h] = got[:, :HD]
    state = (m_s, l_s, acc)
    units = [src[...] for src in (r1, r2, r3)]
    add_units(lambda h: qs[h], units, NEAR, q_tag, lambda h: [ref[h] for ref in state], state)


def attend_near(qs, unit, r1, r2, r3):
    heads = qs.shape[0]
    state = like(heads, CHIP, HD, dtype=F32)
    return call(
        near_body, "attend_near", (state, state, state), [VMEM] * 5, (VMEM,) * 3, limit=8,
        flops=4 * heads * CHIP * 4 * CHIP * HD, exps=heads * CHIP * 4 * CHIP,
    )(qs, unit, r1, r2, r3)


def middle_body(qs, m_in, l_in, acc_in, unit, r4, far_b, far_c, m_s, l_s, acc):
    before = (m_in, l_in, acc_in)
    third, fourth = parts(far_c)
    third = jnp.where(core_index() == 0, r4[...], third)
    add_units(
        lambda h: qs[h], parts(far_b) + [third, fourth], MIDDLE, tags_of(unit)[1],
        lambda h: [ref[h] for ref in before], (m_s, l_s, acc),
    )


def attend_middle(qs, m_in, l_in, acc_in, unit, r4, far_b, far_c):
    heads = qs.shape[0]
    state = like(heads, CHIP, HD, dtype=F32)
    return call(
        middle_body, "attend_middle", (state,) * 3, [VMEM] * 8, (VMEM,) * 3, limit=8,
        flops=32 * heads * CHIP * 4 * CHIP * HD, exps=heads * CHIP * 4 * CHIP,
    )(qs, m_in, l_in, acc_in, unit, r4, far_b, far_c)


def attend_last(side, qs, m_in, l_in, acc_in, unit, far_a):
    heads = qs.shape[0]

    def body(qs, m_in, l_in, acc_in, unit, far_a, out, tag_s, m_s, l_s, acc):
        rows = halves()[side]
        before = (m_in, l_in, acc_in)
        tag_s[...] = jnp.broadcast_to(tags_of(unit)[1], (CHIP, HD))
        add_units(
            lambda h: qs[h, rows, :], parts(far_a), LAST, tag_s[rows, :][:, 0:1],
            lambda h: [ref[h, rows, :] for ref in before], (m_s, l_s, acc),
        )
        for h in range(heads):
            out[:, h * HD : (h + 1) * HD] = (acc[h] / l_s[h]).astype(BF16)

    state = pltpu.VMEM((heads, ROWS, HD), F32)
    return call(
        body, "attend_last", like(ROWS, heads * HD), [VMEM] * 6, VMEM,
        [pltpu.VMEM((CHIP, HD), F32), state, state, state],
        limit=8, flops=4 * heads * ROWS * 3 * CHIP * HD, exps=heads * ROWS * 3 * CHIP,
    )(qs, m_in, l_in, acc_in, unit, far_a)


def project_out(xm, xr, w_out, groups, parts, dtype):
    depth = xm.shape[1]
    width = w_out.shape[1] // groups
    half = width // 2

    def body(xm, xr, w, *outs):
        core = core_index()
        own = pl.ds(pl.multiple_of(core * depth, depth), depth)
        other = pl.ds(pl.multiple_of((1 - core) * depth, depth), depth)
        for (shift, side), out in zip(parts, outs):
            group = lax.rem(lax.axis_index("head") + shift, groups)
            cols = pl.ds(pl.multiple_of(group * width + side * half, half), half)
            got = jnp.dot(xm[...], w[own, cols], preferred_element_type=F32)
            got += jnp.dot(xr[...], w[other, cols], preferred_element_type=F32)
            out[...] = got.astype(dtype)

    return call(
        body, "project_out", (like(ROWS, half, dtype=dtype),) * len(parts), [VMEM] * 3,
        (VMEM,) * len(parts), limit=4,
        flops=2 * ROWS * 2 * depth * half * len(parts), moved=len(parts),
    )(xm, xr, w_out)


def add_body(a, b, p, q, out_a, out_b):
    out_a[...] = (a[...] + p[...].astype(F32)).astype(BF16)
    out_b[...] = (b[...] + q[...].astype(F32)).astype(BF16)


def add_passing(a, b, p, q):
    out = like(*p.shape)
    return call(add_body, "add_passing", (out, out), [VMEM] * 4, (VMEM,) * 2, limit=2)(a, b, p, q)


def total_body(own_a, own_b, left_a, left_b, right_a, right_b, out):
    half = own_a.shape[1]
    for at, pieces in ((0, (own_a, left_a, right_a)), (half, (own_b, left_b, right_b))):
        total = pieces[0][...] + pieces[1][...].astype(F32) + pieces[2][...].astype(F32)
        out[:, at : at + half] = total.astype(BF16)


def add_total(*pieces):
    rows, half = pieces[0].shape
    return call(total_body, "add_total", like(rows, 2 * half), [VMEM] * 6, VMEM, limit=2)(*pieces)


def shards(tokens, w_query, w_key, w_value, w_out, doc_ids):
    ranks = lax.axis_size("ctx")
    groups = lax.axis_size("head")
    table = jnp.asarray(rope_table(ranks * ROWS))

    def swap(value):
        return lax.ppermute(value, "ctx", [(r, r ^ 1) for r in range(ranks)])

    def along(value, even, odd):
        moves = [(r, 2 * (odd if r % 2 else even)(r // 2) + r % 2) for r in range(ranks)]
        return lax.ppermute(value, "ctx", moves)

    def ahead(step):
        return lambda chip: (chip + step) % (ranks // 2)

    def in_row(step):
        return lambda chip: chip // 4 * 4 + (chip + step) % 4

    docs = doc_ids.reshape(1, -1)
    came, docs_came = swap(tokens), swap(docs)
    tokens, w_key, w_value, w_query, table, docs = (
        pltpu.with_memory_space_constraint(a, pltpu.HBM)
        for a in (tokens, w_key, w_value, w_query, table, docs)
    )
    half, tokens, w_kv, docs, table = project_own(tokens, w_key, w_value, docs, table)
    unit = project_unit(half, came, w_kv, docs, docs_came, table)
    r1 = along(unit, ahead(1), ahead(4))
    r2 = along(unit, ahead(2), ahead(8))
    r3 = along(unit, ahead(3), ahead(12))
    r4 = along(unit, ahead(4), in_row(3))
    r1, r2, came = lax.optimization_barrier((r1, r2, came))
    out_b, out_c = bundle_pairs(unit, r1, r2)
    far_b = along(out_b, ahead(8), in_row(2))
    far_c = along(out_c, ahead(12), in_row(3))
    far_a = along(bundle_row(unit, r1, r2, r3, r4), ahead(4), in_row(1))
    qs = project_q(tokens, came, w_query, table)
    state = attend_near(qs, unit, r1, r2, r3)
    state = attend_middle(qs, *state, unit, r4, far_b, far_c)
    xr = swap(attend_last(1, qs, *state, unit, far_a))
    xm = attend_last(0, qs, *state, unit, far_a)

    def shift(value, step):
        return lax.ppermute(value, "head", [(g, (g + step) % groups) for g in range(groups)])

    a2, b2 = project_out(xm, xr, w_out, groups, ((2, 0), (2, 1)), BF16)
    pass_a, pass_b = shift(a2, 1), shift(b2, -1)
    b1, a3 = project_out(xm, xr, w_out, groups, ((1, 1), (3, 0)), BF16)
    left_b, right_a = shift(b1, 1), shift(a3, -1)
    a1, b3, a0, b0 = project_out(xm, xr, w_out, groups, ((1, 0), (3, 1), (0, 0), (0, 1)), F32)
    a1, b3 = add_passing(a1, b3, pass_a, pass_b)
    left_a, right_b = shift(a1, 1), shift(b3, -1)
    return add_total(a0, b0, left_a, left_b, right_a, right_b)


def solution(mesh):
    return jax.shard_map(
        shards,
        mesh=mesh,
        in_specs=(
            P("ctx", None),
            P(None, "head"),
            P(None, "head"),
            P(None, "head"),
            P("head", None),
            P("ctx"),
        ),
        out_specs=P("ctx", "head"),
        check_vma=False,
    )
```

```python
import math

import jax
import jax.numpy as jnp
import numpy as np
from jax import lax
from jax.experimental import pallas as pl
from jax.experimental.pallas import tpu as pltpu
from jax.sharding import PartitionSpec as P

HD = 128
ROWS = 128
UNIT = 264
F32 = jnp.float32
BF16 = jnp.bfloat16
MIB = 1 << 20
SCALE = math.log2(math.e) / math.sqrt(HD)


def rope_table(count):
    half = HD // 2
    freqs = 500000.0 ** (-2.0 * np.arange(half, dtype=np.float64) / HD)
    angles = np.arange(count, dtype=np.float64)[:, None] * freqs[None, :]
    return np.concatenate([np.cos(angles), np.sin(angles)], axis=1).astype(np.float32)


def rotation(table):
    half = HD // 2
    cosine, sine = table[:, :half], table[:, half:]
    cosine = jnp.concatenate([cosine, cosine], axis=1)
    sine = jnp.concatenate([-sine, sine], axis=1)
    return lambda t: t * cosine + pltpu.roll(t, half, 1) * sine


SMEM = pl.BlockSpec(memory_space=pltpu.SMEM)
VMEM = pl.BlockSpec(memory_space=pltpu.VMEM)
HBM = pl.BlockSpec(memory_space=pltpu.HBM)


def like(*dims, dtype=BF16):
    return jax.ShapeDtypeStruct(dims, dtype)


def call(body, name, out, ins, outs, scratch=(), limit=4, flops=0, moved=1, exps=0):
    return pl.pallas_call(
        body,
        out_shape=out,
        in_specs=ins,
        out_specs=outs,
        scratch_shapes=list(scratch),
        name=name,
        cost_estimate=pl.CostEstimate(
            flops=flops, bytes_accessed=moved * MIB, transcendentals=exps
        ),
        compiler_params=pltpu.CompilerParams(vmem_limit_bytes=limit * MIB),
    )


def core_index():
    return lax.rem(lax.axis_index("ctx"), 2)


def table_rows(table):
    return table.at[pl.ds(pl.multiple_of(lax.axis_index("ctx") * ROWS, ROWS), ROWS), :]


def started(copies):
    for copy in copies:
        copy.start()
    return copies


KV_PARTS = 4
CHIP = 2 * ROWS


def halves():
    core = core_index()
    own = pl.ds(pl.multiple_of(core * ROWS, ROWS), ROWS)
    other = pl.ds(pl.multiple_of((1 - core) * ROWS, ROWS), ROWS)
    return own, other


def own_body(tok, wk, wv, docs, table, half, tok_s, w_s, docs_s, table_s, acc, sems):
    part = tok.shape[1] // KV_PARTS
    cols = pl.ds(pl.multiple_of(core_index() * HD, HD), HD)
    copies = []
    for i in range(KV_PARTS):
        cut = pl.ds(i * part, part)
        copies.append(
            started([
                pltpu.make_async_copy(tok.at[:, cut], tok_s.at[:, cut], sems.at[3 * i]),
                pltpu.make_async_copy(
                    wk.at[cut, cols], w_s.at[cut, pl.ds(0, HD)], sems.at[3 * i + 1]
                ),
                pltpu.make_async_copy(
                    wv.at[cut, cols], w_s.at[cut, pl.ds(HD, HD)], sems.at[3 * i + 2]
                ),
            ])
        )
    first = pl.multiple_of(lax.div(lax.axis_index("ctx"), 2) * CHIP, CHIP)
    small = started([
        pltpu.make_async_copy(docs, docs_s, sems.at[3 * KV_PARTS]),
        pltpu.make_async_copy(table.at[pl.ds(first, CHIP), :], table_s, sems.at[3 * KV_PARTS + 1]),
    ])
    for i, group in enumerate(copies):
        for copy in group:
            copy.wait()
        cut = slice(i * part, (i + 1) * part)
        more = jnp.dot(tok_s[:, cut], w_s[cut, :], preferred_element_type=F32)
        if i == 0:
            acc[...] = more
        else:
            acc[...] += more
    for copy in small:
        copy.wait()
    rot = rotation(table_s[halves()[0], :])
    half[:, :HD] = rot(acc[:, :HD]).astype(BF16)
    half[:, HD:] = acc[:, HD:].astype(BF16)


def project_own(tokens, w_key, w_value, docs, table):
    depth = tokens.shape[1]
    return call(
        own_body, "project_own",
        (
            like(ROWS, 2 * HD),
            like(ROWS, depth),
            like(depth, 2 * HD),
            like(1, ROWS, dtype=jnp.int32),
            like(CHIP, HD, dtype=F32),
        ),
        [HBM] * 5, (VMEM,) * 5,
        [pltpu.VMEM((ROWS, 2 * HD), F32), pltpu.SemaphoreType.DMA((3 * KV_PARTS + 2,))],
        limit=6, flops=2 * ROWS * depth * 2 * HD, moved=3,
    )(tokens, w_key, w_value, docs, table)


def unit_body(half, came, w, docs, docs_came, table, unit):
    own, other = halves()
    got = jnp.dot(came[...], w[...], preferred_element_type=F32)
    unit[own, :] = half[...]
    unit[other, :HD] = rotation(table[other, :])(got[:, :HD]).astype(BF16)
    unit[other, HD:] = got[:, HD:].astype(BF16)
    first = core_index() == 0
    a, b = docs[...], docs_came[...]
    tags = jnp.concatenate([jnp.where(first, a, b), jnp.where(first, b, a)], axis=1)
    tags = (tags + 1).astype(F32)
    unit[CHIP:, :] = jnp.broadcast_to(tags, (8, CHIP)).astype(BF16)


def project_unit(half, came, w, docs, docs_came, table):
    return call(
        unit_body, "project_unit", like(UNIT, 2 * HD), [VMEM] * 6, VMEM, limit=2,
        flops=2 * ROWS * w.shape[0] * 2 * HD,
    )(half, came, w, docs, docs_came, table)


Q_PARTS = 4


def q_body(tok, came, wq, table, out, wq_s, sems):
    half = wq.shape[1] // 2
    part = wq.shape[0] // Q_PARTS
    cols = pl.ds(pl.multiple_of(core_index() * half, half), half)
    copies = []
    for i in range(Q_PARTS):
        rows = pl.ds(i * part, part)
        copies += started([
            pltpu.make_async_copy(wq.at[rows, cols], wq_s.at[rows, :], sems.at[i])
        ])
    got = [None, None]
    for i in range(Q_PARTS):
        copies[i].wait()
        rows = slice(i * part, (i + 1) * part)
        for side, src in enumerate((tok, came)):
            more = jnp.dot(src[:, rows], wq_s[rows, :], preferred_element_type=F32)
            got[side] = more if i == 0 else got[side] + more
    for side, span in enumerate(halves()):
        rot = rotation(table[span, :])
        for h in range(half // HD):
            out[h, span, :] = rot(got[side][:, h * HD : (h + 1) * HD]).astype(BF16)


def project_q(tokens, came, w_query, table):
    depth, width = w_query.shape
    return call(
        q_body, "project_q", like(width // 2 // HD, CHIP, HD), [VMEM, VMEM, HBM, VMEM], VMEM,
        [pltpu.VMEM((depth, width // 2), BF16), pltpu.SemaphoreType.DMA((Q_PARTS,))],
        limit=8, flops=2 * CHIP * depth * width // 2, moved=6,
    )(tokens, came, w_query, table)


NONE = 99
NEAR = ((1, 2, 3), (4, 8, NONE))
MIDDLE = ((8, 9, 4, NONE), (2, 6, 3, 7))
LAST = ((5, 6, 7), (1, 5, 9))


def fill(out, slots, late, even):
    place = lax.axis_index("ctx")
    column = lax.rem(lax.div(place, 2), 4)
    skip = jnp.where(lax.rem(place, 2) == 0, even, jnp.where(column >= late, 1, 0))
    for i in range(out.shape[0] // UNIT):
        out[i * UNIT : (i + 1) * UNIT, :] = slots[skip + i]


def pairs_body(unit, r1, r2, out_b, out_c, slots):
    for i, src in enumerate((unit, r1, r2)):
        slots[i] = src[...]
    fill(out_b, slots, 2, 0)
    fill(out_c, slots, 1, 0)


def bundle_pairs(unit, r1, r2):
    pair = like(2 * UNIT, 2 * HD)
    return call(
        pairs_body, "bundle_pairs", (pair, pair), [VMEM] * 3, (VMEM,) * 2,
        [pltpu.VMEM((3, UNIT, 2 * HD), BF16)], limit=2,
    )(unit, r1, r2)


def row_body(unit, r1, r2, r3, after, out_a, slots):
    for i, src in enumerate((unit, r1, r2, r3)):
        slots[i] = src[...]
    fill(out_a, slots, 3, 1)


def bundle_row(unit, r1, r2, r3, after):
    return call(
        row_body, "bundle_row", like(3 * UNIT, 2 * HD), [VMEM] * 5, VMEM,
        [pltpu.VMEM((4, UNIT, 2 * HD), BF16)], limit=2,
    )(unit, r1, r2, r3, after)


CONTRACT = (((1,), (1,)), ((), ()))


def tags_of(unit):
    tags = unit[CHIP:UNIT, :].astype(F32)
    return tags, jnp.transpose(tags, (1, 0))[:, 0:1]


def with_ones(values):
    return jnp.concatenate([values, jnp.ones((CHIP, HD), BF16)], axis=1)


def add_units(queries, units, steps, q_tag, before, after):
    place = lax.axis_index("ctx")
    odd = lax.rem(place, 2) == 1
    chip = lax.div(place, 2)
    for i, (block, even_step, odd_step) in enumerate(zip(units, *steps)):
        valid = chip >= jnp.where(odd, odd_step, even_step)
        k_tag = block[CHIP:, :].astype(F32)[0:1, :]
        bias = jnp.where((k_tag == q_tag) & valid, 0.0, -1e30)
        keys = block[:CHIP, :HD]
        values = with_ones(block[:CHIP, HD:])
        for h in range(after[0].shape[0]):
            s = lax.dot_general(queries(h), keys, CONTRACT, preferred_element_type=F32)
            s = s * SCALE + bias
            if i == 0:
                old, old_sum, old_acc = before(h)
            else:
                old, old_sum, old_acc = (ref[h] for ref in after)
            top = jnp.maximum(old, jnp.max(s, axis=1, keepdims=True))
            fade = jnp.exp2(old - top)
            w = jnp.exp2(s - jnp.concatenate([top, top], axis=1)).astype(BF16)
            got = jnp.dot(w, values, preferred_element_type=F32)
            after[0][h] = top
            after[1][h] = fade * old_sum + got[:, HD:]
            after[2][h] = fade * old_acc + got[:, :HD]


def parts(src):
    return [src[i * UNIT : (i + 1) * UNIT, :] for i in range(src.shape[0] // UNIT)]


def near_body(qs, unit, r1, r2, r3, m_s, l_s, acc):
    tags, q_tag = tags_of(unit)
    rows = lax.broadcasted_iota(jnp.int32, (CHIP, CHIP), 0)
    cols = lax.broadcasted_iota(jnp.int32, (CHIP, CHIP), 1)
    bias = jnp.where((tags[0:1, :] == q_tag) & (cols <= rows), 0.0, -1e30)
    keys, values = unit[:CHIP, :HD], with_ones(unit[:CHIP, HD:])
    for h in range(qs.shape[0]):
        s = lax.dot_general(qs[h], keys, CONTRACT, preferred_element_type=F32)
        s = s * SCALE + bias
        top = jnp.max(s, axis=1, keepdims=True)
        got = jnp.dot(jnp.exp2(s - top).astype(BF16), values, preferred_element_type=F32)
        m_s[h] = jnp.broadcast_to(top, (CHIP, HD))
        l_s[h] = got[:, HD:]
        acc[h] = got[:, :HD]
    state = (m_s, l_s, acc)
    units = [src[...] for src in (r1, r2, r3)]
    add_units(lambda h: qs[h], units, NEAR, q_tag, lambda h: [ref[h] for ref in state], state)


def attend_near(qs, unit, r1, r2, r3):
    heads = qs.shape[0]
    state = like(heads, CHIP, HD, dtype=F32)
    return call(
        near_body, "attend_near", (state, state, state), [VMEM] * 5, (VMEM,) * 3, limit=8,
        flops=16 * heads * CHIP * 4 * CHIP * HD, exps=heads * CHIP * 4 * CHIP,
    )(qs, unit, r1, r2, r3)


def middle_body(qs, m_in, l_in, acc_in, unit, r4, far_b, far_c, m_s, l_s, acc):
    before = (m_in, l_in, acc_in)
    third, fourth = parts(far_c)
    third = jnp.where(core_index() == 0, r4[...], third)
    add_units(
        lambda h: qs[h], parts(far_b) + [third, fourth], MIDDLE, tags_of(unit)[1],
        lambda h: [ref[h] for ref in before], (m_s, l_s, acc),
    )


def attend_middle(qs, m_in, l_in, acc_in, unit, r4, far_b, far_c):
    heads = qs.shape[0]
    state = like(heads, CHIP, HD, dtype=F32)
    return call(
        middle_body, "attend_middle", (state,) * 3, [VMEM] * 8, (VMEM,) * 3, limit=8,
        flops=32 * heads * CHIP * 4 * CHIP * HD, exps=heads * CHIP * 4 * CHIP,
    )(qs, m_in, l_in, acc_in, unit, r4, far_b, far_c)


def attend_last(side, qs, m_in, l_in, acc_in, unit, far_a):
    heads = qs.shape[0]

    def body(qs, m_in, l_in, acc_in, unit, far_a, out, tag_s, m_s, l_s, acc):
        rows = halves()[side]
        before = (m_in, l_in, acc_in)
        tag_s[...] = jnp.broadcast_to(tags_of(unit)[1], (CHIP, HD))
        add_units(
            lambda h: qs[h, rows, :], parts(far_a), LAST, tag_s[rows, :][:, 0:1],
            lambda h: [ref[h, rows, :] for ref in before], (m_s, l_s, acc),
        )
        for h in range(heads):
            out[:, h * HD : (h + 1) * HD] = (acc[h] / l_s[h]).astype(BF16)

    state = pltpu.VMEM((heads, ROWS, HD), F32)
    return call(
        body, "attend_last", like(ROWS, heads * HD), [VMEM] * 6, VMEM,
        [pltpu.VMEM((CHIP, HD), F32), state, state, state],
        limit=8, flops=4 * heads * ROWS * 3 * CHIP * HD, exps=heads * ROWS * 3 * CHIP,
    )(qs, m_in, l_in, acc_in, unit, far_a)


def project_out(xm, xr, w_out, groups, parts, dtype):
    depth = xm.shape[1]
    width = w_out.shape[1] // groups
    half = width // 2

    def body(xm, xr, w, *outs):
        core = core_index()
        own = pl.ds(pl.multiple_of(core * depth, depth), depth)
        other = pl.ds(pl.multiple_of((1 - core) * depth, depth), depth)
        for (shift, side), out in zip(parts, outs):
            group = lax.rem(lax.axis_index("head") + shift, groups)
            cols = pl.ds(pl.multiple_of(group * width + side * half, half), half)
            got = jnp.dot(xm[...], w[own, cols], preferred_element_type=F32)
            got += jnp.dot(xr[...], w[other, cols], preferred_element_type=F32)
            out[...] = got.astype(dtype)

    return call(
        body, "project_out", (like(ROWS, half, dtype=dtype),) * len(parts), [VMEM] * 3,
        (VMEM,) * len(parts), limit=4,
        flops=2 * ROWS * 2 * depth * half * len(parts), moved=len(parts),
    )(xm, xr, w_out)


def add_body(a, b, p, q, out_a, out_b):
    out_a[...] = (a[...] + p[...].astype(F32)).astype(BF16)
    out_b[...] = (b[...] + q[...].astype(F32)).astype(BF16)


def add_passing(a, b, p, q):
    out = like(*p.shape)
    return call(add_body, "add_passing", (out, out), [VMEM] * 4, (VMEM,) * 2, limit=2)(a, b, p, q)


def total_body(own_a, own_b, left_a, left_b, right_a, right_b, out):
    half = own_a.shape[1]
    for at, pieces in ((0, (own_a, left_a, right_a)), (half, (own_b, left_b, right_b))):
        total = pieces[0][...] + pieces[1][...].astype(F32) + pieces[2][...].astype(F32)
        out[:, at : at + half] = total.astype(BF16)


def add_total(*pieces):
    rows, half = pieces[0].shape
    return call(total_body, "add_total", like(rows, 2 * half), [VMEM] * 6, VMEM, limit=2)(*pieces)


def shards(tokens, w_query, w_key, w_value, w_out, doc_ids):
    ranks = lax.axis_size("ctx")
    groups = lax.axis_size("head")
    table = jnp.asarray(rope_table(ranks * ROWS))

    def swap(value):
        return lax.ppermute(value, "ctx", [(r, r ^ 1) for r in range(ranks)])

    def along(value, even, odd):
        moves = [(r, 2 * (odd if r % 2 else even)(r // 2) + r % 2) for r in range(ranks)]
        return lax.ppermute(value, "ctx", moves)

    def ahead(step):
        return lambda chip: (chip + step) % (ranks // 2)

    def in_row(step):
        return lambda chip: chip // 4 * 4 + (chip + step) % 4

    docs = doc_ids.reshape(1, -1)
    came, docs_came = swap(tokens), swap(docs)
    tokens, w_key, w_value, w_query, table, docs = (
        pltpu.with_memory_space_constraint(a, pltpu.HBM)
        for a in (tokens, w_key, w_value, w_query, table, docs)
    )
    half, tokens, w_kv, docs, table = project_own(tokens, w_key, w_value, docs, table)
    unit = project_unit(half, came, w_kv, docs, docs_came, table)
    r1 = along(unit, ahead(1), ahead(4))
    r2 = along(unit, ahead(2), ahead(8))
    r3 = along(unit, ahead(3), ahead(12))
    r4 = along(unit, ahead(4), in_row(3))
    qs = project_q(tokens, came, w_query, table)
    r1, r2, qs = lax.optimization_barrier((r1, r2, qs))
    out_b, out_c = bundle_pairs(unit, r1, r2)
    far_b = along(out_b, ahead(8), in_row(2))
    far_c = along(out_c, ahead(12), in_row(3))
    far_a = along(bundle_row(unit, r1, r2, r3, r4), ahead(4), in_row(1))
    state = attend_near(qs, unit, r1, r2, r3)
    state = attend_middle(qs, *state, unit, r4, far_b, far_c)
    xr = swap(attend_last(1, qs, *state, unit, far_a))
    xm = attend_last(0, qs, *state, unit, far_a)

    def shift(value, step):
        return lax.ppermute(value, "head", [(g, (g + step) % groups) for g in range(groups)])

    a2, b2 = project_out(xm, xr, w_out, groups, ((2, 0), (2, 1)), BF16)
    pass_a, pass_b = shift(a2, 1), shift(b2, -1)
    b1, a3 = project_out(xm, xr, w_out, groups, ((1, 1), (3, 0)), BF16)
    left_b, right_a = shift(b1, 1), shift(a3, -1)
    a1, b3, a0, b0 = project_out(xm, xr, w_out, groups, ((1, 0), (3, 1), (0, 0), (0, 1)), F32)
    a1, b3 = add_passing(a1, b3, pass_a, pass_b)
    left_a, right_b = shift(a1, 1), shift(b3, -1)
    return add_total(a0, b0, left_a, left_b, right_a, right_b)


def solution(mesh):
    return jax.shard_map(
        shards,
        mesh=mesh,
        in_specs=(
            P("ctx", None),
            P(None, "head"),
            P(None, "head"),
            P(None, "head"),
            P("head", None),
            P("ctx"),
        ),
        out_specs=P("ctx", "head"),
        check_vma=False,
    )
```

```python
import math

import jax
import jax.numpy as jnp
import numpy as np
from jax import lax
from jax.experimental import pallas as pl
from jax.experimental.pallas import tpu as pltpu
from jax.sharding import PartitionSpec as P

HD = 128
ROWS = 128
UNIT = 264
F32 = jnp.float32
BF16 = jnp.bfloat16
MIB = 1 << 20
SCALE = math.log2(math.e) / math.sqrt(HD)


def rope_table(count):
    half = HD // 2
    freqs = 500000.0 ** (-2.0 * np.arange(half, dtype=np.float64) / HD)
    angles = np.arange(count, dtype=np.float64)[:, None] * freqs[None, :]
    return np.concatenate([np.cos(angles), np.sin(angles)], axis=1).astype(np.float32)


def rotation(table):
    half = HD // 2
    cosine, sine = table[:, :half], table[:, half:]
    cosine = jnp.concatenate([cosine, cosine], axis=1)
    sine = jnp.concatenate([-sine, sine], axis=1)
    return lambda t: t * cosine + pltpu.roll(t, half, 1) * sine


SMEM = pl.BlockSpec(memory_space=pltpu.SMEM)
VMEM = pl.BlockSpec(memory_space=pltpu.VMEM)
HBM = pl.BlockSpec(memory_space=pltpu.HBM)


def like(*dims, dtype=BF16):
    return jax.ShapeDtypeStruct(dims, dtype)


def call(body, name, out, ins, outs, scratch=(), limit=4, flops=0, moved=1, exps=0):
    return pl.pallas_call(
        body,
        out_shape=out,
        in_specs=ins,
        out_specs=outs,
        scratch_shapes=list(scratch),
        name=name,
        cost_estimate=pl.CostEstimate(
            flops=flops, bytes_accessed=moved * MIB, transcendentals=exps
        ),
        compiler_params=pltpu.CompilerParams(vmem_limit_bytes=limit * MIB),
    )


def core_index():
    return lax.rem(lax.axis_index("ctx"), 2)


def table_rows(table):
    return table.at[pl.ds(pl.multiple_of(lax.axis_index("ctx") * ROWS, ROWS), ROWS), :]


def started(copies):
    for copy in copies:
        copy.start()
    return copies


KV_PARTS = 4
CHIP = 2 * ROWS


def halves():
    core = core_index()
    own = pl.ds(pl.multiple_of(core * ROWS, ROWS), ROWS)
    other = pl.ds(pl.multiple_of((1 - core) * ROWS, ROWS), ROWS)
    return own, other


def own_body(tok, wk, wv, docs, table, half, tok_s, w_s, docs_s, table_s, acc, sems):
    part = tok.shape[1] // KV_PARTS
    cols = pl.ds(pl.multiple_of(core_index() * HD, HD), HD)
    copies = []
    for i in range(KV_PARTS):
        cut = pl.ds(i * part, part)
        copies.append(
            started([
                pltpu.make_async_copy(tok.at[:, cut], tok_s.at[:, cut], sems.at[3 * i]),
                pltpu.make_async_copy(
                    wk.at[cut, cols], w_s.at[cut, pl.ds(0, HD)], sems.at[3 * i + 1]
                ),
                pltpu.make_async_copy(
                    wv.at[cut, cols], w_s.at[cut, pl.ds(HD, HD)], sems.at[3 * i + 2]
                ),
            ])
        )
    first = pl.multiple_of(lax.div(lax.axis_index("ctx"), 2) * CHIP, CHIP)
    small = started([
        pltpu.make_async_copy(docs, docs_s, sems.at[3 * KV_PARTS]),
        pltpu.make_async_copy(table.at[pl.ds(first, CHIP), :], table_s, sems.at[3 * KV_PARTS + 1]),
    ])
    for i, group in enumerate(copies):
        for copy in group:
            copy.wait()
        cut = slice(i * part, (i + 1) * part)
        more = jnp.dot(tok_s[:, cut], w_s[cut, :], preferred_element_type=F32)
        if i == 0:
            acc[...] = more
        else:
            acc[...] += more
    for copy in small:
        copy.wait()
    rot = rotation(table_s[halves()[0], :])
    half[:, :HD] = rot(acc[:, :HD]).astype(BF16)
    half[:, HD:] = acc[:, HD:].astype(BF16)


def project_own(tokens, w_key, w_value, docs, table):
    depth = tokens.shape[1]
    return call(
        own_body, "project_own",
        (
            like(ROWS, 2 * HD),
            like(ROWS, depth),
            like(depth, 2 * HD),
            like(1, ROWS, dtype=jnp.int32),
            like(CHIP, HD, dtype=F32),
        ),
        [HBM] * 5, (VMEM,) * 5,
        [pltpu.VMEM((ROWS, 2 * HD), F32), pltpu.SemaphoreType.DMA((3 * KV_PARTS + 2,))],
        limit=6, flops=2 * ROWS * depth * 2 * HD, moved=3,
    )(tokens, w_key, w_value, docs, table)


def unit_body(half, came, w, docs, docs_came, table, unit):
    own, other = halves()
    got = jnp.dot(came[...], w[...], preferred_element_type=F32)
    unit[own, :] = half[...]
    unit[other, :HD] = rotation(table[other, :])(got[:, :HD]).astype(BF16)
    unit[other, HD:] = got[:, HD:].astype(BF16)
    first = core_index() == 0
    a, b = docs[...], docs_came[...]
    tags = jnp.concatenate([jnp.where(first, a, b), jnp.where(first, b, a)], axis=1)
    tags = (tags + 1).astype(F32)
    unit[CHIP:, :] = jnp.broadcast_to(tags, (8, CHIP)).astype(BF16)


def project_unit(half, came, w, docs, docs_came, table):
    return call(
        unit_body, "project_unit", like(UNIT, 2 * HD), [VMEM] * 6, VMEM, limit=2,
        flops=2 * ROWS * w.shape[0] * 2 * HD,
    )(half, came, w, docs, docs_came, table)


Q_PARTS = 4


def q_body(tok, came, wq, table, out, wq_s, sems):
    half = wq.shape[1] // 2
    part = wq.shape[0] // Q_PARTS
    cols = pl.ds(pl.multiple_of(core_index() * half, half), half)
    copies = []
    for i in range(Q_PARTS):
        rows = pl.ds(i * part, part)
        copies += started([
            pltpu.make_async_copy(wq.at[rows, cols], wq_s.at[rows, :], sems.at[i])
        ])
    got = [None, None]
    for i in range(Q_PARTS):
        copies[i].wait()
        rows = slice(i * part, (i + 1) * part)
        for side, src in enumerate((tok, came)):
            more = jnp.dot(src[:, rows], wq_s[rows, :], preferred_element_type=F32)
            got[side] = more if i == 0 else got[side] + more
    for side, span in enumerate(halves()):
        rot = rotation(table[span, :])
        for h in range(half // HD):
            out[h, span, :] = rot(got[side][:, h * HD : (h + 1) * HD]).astype(BF16)


def project_q(tokens, came, w_query, table):
    depth, width = w_query.shape
    return call(
        q_body, "project_q", like(width // 2 // HD, CHIP, HD), [VMEM, VMEM, HBM, VMEM], VMEM,
        [pltpu.VMEM((depth, width // 2), BF16), pltpu.SemaphoreType.DMA((Q_PARTS,))],
        limit=8, flops=2 * CHIP * depth * width // 2, moved=6,
    )(tokens, came, w_query, table)


NONE = 99
NEAR = ((1, 2), (4, 8))
EARLY = ((8, 9), (2, 6))
MIDDLE = ((3, 4), (3, 7))
LAST = ((5, 6, 7), (1, 5, 9))


def fill(out, slots, late, even):
    place = lax.axis_index("ctx")
    column = lax.rem(lax.div(place, 2), 4)
    skip = jnp.where(lax.rem(place, 2) == 0, even, jnp.where(column >= late, 1, 0))
    for i in range(out.shape[0] // UNIT):
        out[i * UNIT : (i + 1) * UNIT, :] = slots[skip + i]


def pairs_body(unit, r1, r2, out_b, out_c, slots):
    for i, src in enumerate((unit, r1, r2)):
        slots[i] = src[...]
    fill(out_b, slots, 2, 0)
    fill(out_c, slots, 1, 0)


def bundle_pairs(unit, r1, r2):
    pair = like(2 * UNIT, 2 * HD)
    return call(
        pairs_body, "bundle_pairs", (pair, pair), [VMEM] * 3, (VMEM,) * 2,
        [pltpu.VMEM((3, UNIT, 2 * HD), BF16)], limit=2,
    )(unit, r1, r2)


def row_body(unit, r1, r2, r3, after, out_a, slots):
    for i, src in enumerate((unit, r1, r2, r3)):
        slots[i] = src[...]
    fill(out_a, slots, 3, 1)


def bundle_row(unit, r1, r2, r3, after):
    return call(
        row_body, "bundle_row", like(3 * UNIT, 2 * HD), [VMEM] * 5, VMEM,
        [pltpu.VMEM((4, UNIT, 2 * HD), BF16)], limit=2,
    )(unit, r1, r2, r3, after)


CONTRACT = (((1,), (1,)), ((), ()))


def tags_of(unit):
    tags = unit[CHIP:UNIT, :].astype(F32)
    return tags, jnp.transpose(tags, (1, 0))[:, 0:1]


def with_ones(values):
    return jnp.concatenate([values, jnp.ones((CHIP, HD), BF16)], axis=1)


def add_units(queries, units, steps, q_tag, before, after):
    place = lax.axis_index("ctx")
    odd = lax.rem(place, 2) == 1
    chip = lax.div(place, 2)
    for i, (block, even_step, odd_step) in enumerate(zip(units, *steps)):
        valid = chip >= jnp.where(odd, odd_step, even_step)
        k_tag = block[CHIP:, :].astype(F32)[0:1, :]
        bias = jnp.where((k_tag == q_tag) & valid, 0.0, -1e30)
        keys = block[:CHIP, :HD]
        values = with_ones(block[:CHIP, HD:])
        for h in range(after[0].shape[0]):
            s = lax.dot_general(queries(h), keys, CONTRACT, preferred_element_type=F32)
            s = s * SCALE + bias
            if i == 0:
                old, old_sum, old_acc = before(h)
            else:
                old, old_sum, old_acc = (ref[h] for ref in after)
            top = jnp.maximum(old, jnp.max(s, axis=1, keepdims=True))
            fade = jnp.exp2(old - top)
            w = jnp.exp2(s - jnp.concatenate([top, top], axis=1)).astype(BF16)
            got = jnp.dot(w, values, preferred_element_type=F32)
            after[0][h] = top
            after[1][h] = fade * old_sum + got[:, HD:]
            after[2][h] = fade * old_acc + got[:, :HD]


def parts(src):
    return [src[i * UNIT : (i + 1) * UNIT, :] for i in range(src.shape[0] // UNIT)]


def near_body(qs, unit, r1, r2, m_s, l_s, acc):
    tags, q_tag = tags_of(unit)
    rows = lax.broadcasted_iota(jnp.int32, (CHIP, CHIP), 0)
    cols = lax.broadcasted_iota(jnp.int32, (CHIP, CHIP), 1)
    bias = jnp.where((tags[0:1, :] == q_tag) & (cols <= rows), 0.0, -1e30)
    keys, values = unit[:CHIP, :HD], with_ones(unit[:CHIP, HD:])
    for h in range(qs.shape[0]):
        s = lax.dot_general(qs[h], keys, CONTRACT, preferred_element_type=F32)
        s = s * SCALE + bias
        top = jnp.max(s, axis=1, keepdims=True)
        got = jnp.dot(jnp.exp2(s - top).astype(BF16), values, preferred_element_type=F32)
        m_s[h] = jnp.broadcast_to(top, (CHIP, HD))
        l_s[h] = got[:, HD:]
        acc[h] = got[:, :HD]
    state = (m_s, l_s, acc)
    units = [src[...] for src in (r1, r2)]
    add_units(lambda h: qs[h], units, NEAR, q_tag, lambda h: [ref[h] for ref in state], state)


def attend_near(qs, unit, r1, r2):
    heads = qs.shape[0]
    state = like(heads, CHIP, HD, dtype=F32)
    return call(
        near_body, "attend_near", (state, state, state), [VMEM] * 4, (VMEM,) * 3, limit=8,
        flops=12 * heads * CHIP * CHIP * HD, exps=3 * heads * CHIP * CHIP,
    )(qs, unit, r1, r2)


def early_body(qs, m_in, l_in, acc_in, unit, far_b, m_s, l_s, acc):
    before = (m_in, l_in, acc_in)
    add_units(
        lambda h: qs[h], parts(far_b), EARLY, tags_of(unit)[1],
        lambda h: [ref[h] for ref in before], (m_s, l_s, acc),
    )


def attend_early(qs, m_in, l_in, acc_in, unit, far_b):
    heads = qs.shape[0]
    state = like(heads, CHIP, HD, dtype=F32)
    return call(
        early_body, "attend_early", (state,) * 3, [VMEM] * 6, (VMEM,) * 3, limit=8,
        flops=64 * heads * CHIP * CHIP * HD, exps=2 * heads * CHIP * CHIP,
    )(qs, m_in, l_in, acc_in, unit, far_b)


def middle_body(qs, m_in, l_in, acc_in, unit, r3, r4, far_c, m_s, l_s, acc):
    before = (m_in, l_in, acc_in)
    even = core_index() == 0
    third, fourth = parts(far_c)
    units = [jnp.where(even, r3[...], third), jnp.where(even, r4[...], fourth)]
    add_units(
        lambda h: qs[h], units, MIDDLE, tags_of(unit)[1],
        lambda h: [ref[h] for ref in before], (m_s, l_s, acc),
    )


def attend_middle(qs, m_in, l_in, acc_in, unit, r3, r4, far_c):
    heads = qs.shape[0]
    state = like(heads, CHIP, HD, dtype=F32)
    return call(
        middle_body, "attend_middle", (state,) * 3, [VMEM] * 8, (VMEM,) * 3, limit=8,
        flops=64 * heads * CHIP * CHIP * HD, exps=2 * heads * CHIP * CHIP,
    )(qs, m_in, l_in, acc_in, unit, r3, r4, far_c)


def attend_last(side, qs, m_in, l_in, acc_in, unit, far_a):
    heads = qs.shape[0]

    def body(qs, m_in, l_in, acc_in, unit, far_a, out, tag_s, m_s, l_s, acc):
        rows = halves()[side]
        before = (m_in, l_in, acc_in)
        tag_s[...] = jnp.broadcast_to(tags_of(unit)[1], (CHIP, HD))
        add_units(
            lambda h: qs[h, rows, :], parts(far_a), LAST, tag_s[rows, :][:, 0:1],
            lambda h: [ref[h, rows, :] for ref in before], (m_s, l_s, acc),
        )
        for h in range(heads):
            out[:, h * HD : (h + 1) * HD] = (acc[h] / l_s[h]).astype(BF16)

    state = pltpu.VMEM((heads, ROWS, HD), F32)
    return call(
        body, "attend_last", like(ROWS, heads * HD), [VMEM] * 6, VMEM,
        [pltpu.VMEM((CHIP, HD), F32), state, state, state],
        limit=8, flops=4 * heads * ROWS * 3 * CHIP * HD, exps=heads * ROWS * 3 * CHIP,
    )(qs, m_in, l_in, acc_in, unit, far_a)


def project_out(xm, xr, w_out, groups, parts, dtype):
    depth = xm.shape[1]
    width = w_out.shape[1] // groups
    half = width // 2

    def body(xm, xr, w, *outs):
        core = core_index()
        own = pl.ds(pl.multiple_of(core * depth, depth), depth)
        other = pl.ds(pl.multiple_of((1 - core) * depth, depth), depth)
        for (shift, side), out in zip(parts, outs):
            group = lax.rem(lax.axis_index("head") + shift, groups)
            cols = pl.ds(pl.multiple_of(group * width + side * half, half), half)
            got = jnp.dot(xm[...], w[own, cols], preferred_element_type=F32)
            got += jnp.dot(xr[...], w[other, cols], preferred_element_type=F32)
            out[...] = got.astype(dtype)

    return call(
        body, "project_out", (like(ROWS, half, dtype=dtype),) * len(parts), [VMEM] * 3,
        (VMEM,) * len(parts), limit=4,
        flops=2 * ROWS * 2 * depth * half * len(parts), moved=len(parts),
    )(xm, xr, w_out)


def add_body(a, b, p, q, out_a, out_b):
    out_a[...] = (a[...] + p[...].astype(F32)).astype(BF16)
    out_b[...] = (b[...] + q[...].astype(F32)).astype(BF16)


def add_passing(a, b, p, q):
    out = like(*p.shape)
    return call(add_body, "add_passing", (out, out), [VMEM] * 4, (VMEM,) * 2, limit=2)(a, b, p, q)


def total_body(own_a, own_b, left_a, left_b, right_a, right_b, out):
    half = own_a.shape[1]
    for at, pieces in ((0, (own_a, left_a, right_a)), (half, (own_b, left_b, right_b))):
        total = pieces[0][...] + pieces[1][...].astype(F32) + pieces[2][...].astype(F32)
        out[:, at : at + half] = total.astype(BF16)


def add_total(*pieces):
    rows, half = pieces[0].shape
    return call(total_body, "add_total", like(rows, 2 * half), [VMEM] * 6, VMEM, limit=2)(*pieces)


def shards(tokens, w_query, w_key, w_value, w_out, doc_ids):
    ranks = lax.axis_size("ctx")
    groups = lax.axis_size("head")
    table = jnp.asarray(rope_table(ranks * ROWS))

    def swap(value):
        return lax.ppermute(value, "ctx", [(r, r ^ 1) for r in range(ranks)])

    def along(value, even, odd):
        moves = [(r, 2 * (odd if r % 2 else even)(r // 2) + r % 2) for r in range(ranks)]
        return lax.ppermute(value, "ctx", moves)

    def ahead(step):
        return lambda chip: (chip + step) % (ranks // 2)

    def in_row(step):
        return lambda chip: chip // 4 * 4 + (chip + step) % 4

    docs = doc_ids.reshape(1, -1)
    came, docs_came = swap(tokens), swap(docs)
    tokens, w_key, w_value, w_query, table, docs = (
        pltpu.with_memory_space_constraint(a, pltpu.HBM)
        for a in (tokens, w_key, w_value, w_query, table, docs)
    )
    half, tokens, w_kv, docs, table = project_own(tokens, w_key, w_value, docs, table)
    unit = project_unit(half, came, w_kv, docs, docs_came, table)
    r1 = along(unit, ahead(1), ahead(4))
    r2 = along(unit, ahead(2), ahead(8))
    r3 = along(unit, ahead(3), ahead(12))
    r4 = along(unit, ahead(4), in_row(3))
    r1, r2, came = lax.optimization_barrier((r1, r2, came))
    out_b, out_c = bundle_pairs(unit, r1, r2)
    far_b = along(out_b, ahead(8), in_row(2))
    far_c = along(out_c, ahead(12), in_row(3))
    far_a = along(bundle_row(unit, r1, r2, r3, r4), ahead(4), in_row(1))
    qs = project_q(tokens, came, w_query, table)
    state = attend_near(qs, unit, r1, r2)
    state = attend_early(qs, *state, unit, far_b)
    state = attend_middle(qs, *state, unit, r3, r4, far_c)
    xr = swap(attend_last(1, qs, *state, unit, far_a))
    xm = attend_last(0, qs, *state, unit, far_a)

    def shift(value, step):
        return lax.ppermute(value, "head", [(g, (g + step) % groups) for g in range(groups)])

    a2, b2 = project_out(xm, xr, w_out, groups, ((2, 0), (2, 1)), BF16)
    pass_a, pass_b = shift(a2, 1), shift(b2, -1)
    b1, a3 = project_out(xm, xr, w_out, groups, ((1, 1), (3, 0)), BF16)
    left_b, right_a = shift(b1, 1), shift(a3, -1)
    a1, b3, a0, b0 = project_out(xm, xr, w_out, groups, ((1, 0), (3, 1), (0, 0), (0, 1)), F32)
    a1, b3 = add_passing(a1, b3, pass_a, pass_b)
    left_a, right_b = shift(a1, 1), shift(b3, -1)
    return add_total(a0, b0, left_a, left_b, right_a, right_b)


def solution(mesh):
    return jax.shard_map(
        shards,
        mesh=mesh,
        in_specs=(
            P("ctx", None),
            P(None, "head"),
            P(None, "head"),
            P(None, "head"),
            P("head", None),
            P("ctx"),
        ),
        out_specs=P("ctx", "head"),
        check_vma=False,
    )
```

```python
import math

import jax
import jax.numpy as jnp
import numpy as np
from jax import lax
from jax.experimental import pallas as pl
from jax.experimental.pallas import tpu as pltpu
from jax.sharding import PartitionSpec as P

HD = 128
ROWS = 128
UNIT = 264
F32 = jnp.float32
BF16 = jnp.bfloat16
MIB = 1 << 20
SCALE = math.log2(math.e) / math.sqrt(HD)


def rope_table(count):
    half = HD // 2
    freqs = 500000.0 ** (-2.0 * np.arange(half, dtype=np.float64) / HD)
    angles = np.arange(count, dtype=np.float64)[:, None] * freqs[None, :]
    return np.concatenate([np.cos(angles), np.sin(angles)], axis=1).astype(np.float32)


def rotation(table):
    half = HD // 2
    cosine, sine = table[:, :half], table[:, half:]
    cosine = jnp.concatenate([cosine, cosine], axis=1)
    sine = jnp.concatenate([-sine, sine], axis=1)
    return lambda t: t * cosine + pltpu.roll(t, half, 1) * sine


SMEM = pl.BlockSpec(memory_space=pltpu.SMEM)
VMEM = pl.BlockSpec(memory_space=pltpu.VMEM)
HBM = pl.BlockSpec(memory_space=pltpu.HBM)


def like(*dims, dtype=BF16):
    return jax.ShapeDtypeStruct(dims, dtype)


def call(body, name, out, ins, outs, scratch=(), limit=4, flops=0, moved=1, exps=0):
    return pl.pallas_call(
        body,
        out_shape=out,
        in_specs=ins,
        out_specs=outs,
        scratch_shapes=list(scratch),
        name=name,
        cost_estimate=pl.CostEstimate(
            flops=flops, bytes_accessed=moved * MIB, transcendentals=exps
        ),
        compiler_params=pltpu.CompilerParams(vmem_limit_bytes=limit * MIB),
    )


def core_index():
    return lax.rem(lax.axis_index("ctx"), 2)


def table_rows(table):
    return table.at[pl.ds(pl.multiple_of(lax.axis_index("ctx") * ROWS, ROWS), ROWS), :]


def started(copies):
    for copy in copies:
        copy.start()
    return copies


KV_PARTS = 4
CHIP = 2 * ROWS


def halves():
    core = core_index()
    own = pl.ds(pl.multiple_of(core * ROWS, ROWS), ROWS)
    other = pl.ds(pl.multiple_of((1 - core) * ROWS, ROWS), ROWS)
    return own, other


def own_body(tok, wk, wv, docs, table, half, tok_s, w_s, docs_s, table_s, acc, sems):
    part = tok.shape[1] // KV_PARTS
    cols = pl.ds(pl.multiple_of(core_index() * HD, HD), HD)
    copies = []
    for i in range(KV_PARTS):
        cut = pl.ds(i * part, part)
        copies.append(
            started([
                pltpu.make_async_copy(tok.at[:, cut], tok_s.at[:, cut], sems.at[3 * i]),
                pltpu.make_async_copy(
                    wk.at[cut, cols], w_s.at[cut, pl.ds(0, HD)], sems.at[3 * i + 1]
                ),
                pltpu.make_async_copy(
                    wv.at[cut, cols], w_s.at[cut, pl.ds(HD, HD)], sems.at[3 * i + 2]
                ),
            ])
        )
    first = pl.multiple_of(lax.div(lax.axis_index("ctx"), 2) * CHIP, CHIP)
    small = started([
        pltpu.make_async_copy(docs, docs_s, sems.at[3 * KV_PARTS]),
        pltpu.make_async_copy(table.at[pl.ds(first, CHIP), :], table_s, sems.at[3 * KV_PARTS + 1]),
    ])
    for i, group in enumerate(copies):
        for copy in group:
            copy.wait()
        cut = slice(i * part, (i + 1) * part)
        more = jnp.dot(tok_s[:, cut], w_s[cut, :], preferred_element_type=F32)
        if i == 0:
            acc[...] = more
        else:
            acc[...] += more
    for copy in small:
        copy.wait()
    rot = rotation(table_s[halves()[0], :])
    half[:, :HD] = rot(acc[:, :HD]).astype(BF16)
    half[:, HD:] = acc[:, HD:].astype(BF16)


def project_own(tokens, w_key, w_value, docs, table):
    depth = tokens.shape[1]
    return call(
        own_body, "project_own",
        (
            like(ROWS, 2 * HD),
            like(ROWS, depth),
            like(depth, 2 * HD),
            like(1, ROWS, dtype=jnp.int32),
            like(CHIP, HD, dtype=F32),
        ),
        [HBM] * 5, (VMEM,) * 5,
        [pltpu.VMEM((ROWS, 2 * HD), F32), pltpu.SemaphoreType.DMA((3 * KV_PARTS + 2,))],
        limit=6, flops=2 * ROWS * depth * 2 * HD, moved=3,
    )(tokens, w_key, w_value, docs, table)


def unit_body(half, came, w, docs, docs_came, table, unit):
    own, other = halves()
    got = jnp.dot(came[...], w[...], preferred_element_type=F32)
    unit[own, :] = half[...]
    unit[other, :HD] = rotation(table[other, :])(got[:, :HD]).astype(BF16)
    unit[other, HD:] = got[:, HD:].astype(BF16)
    first = core_index() == 0
    a, b = docs[...], docs_came[...]
    tags = jnp.concatenate([jnp.where(first, a, b), jnp.where(first, b, a)], axis=1)
    tags = (tags + 1).astype(F32)
    unit[CHIP:, :] = jnp.broadcast_to(tags, (8, CHIP)).astype(BF16)


def project_unit(half, came, w, docs, docs_came, table):
    return call(
        unit_body, "project_unit", like(UNIT, 2 * HD), [VMEM] * 6, VMEM, limit=2,
        flops=2 * ROWS * w.shape[0] * 2 * HD,
    )(half, came, w, docs, docs_came, table)


Q_PARTS = 4


def q_body(tok, came, wq, table, out, wq_s, sems):
    half = wq.shape[1] // 2
    part = wq.shape[0] // Q_PARTS
    cols = pl.ds(pl.multiple_of(core_index() * half, half), half)
    copies = []
    for i in range(Q_PARTS):
        rows = pl.ds(i * part, part)
        copies += started([
            pltpu.make_async_copy(wq.at[rows, cols], wq_s.at[rows, :], sems.at[i])
        ])
    got = [None, None]
    for i in range(Q_PARTS):
        copies[i].wait()
        rows = slice(i * part, (i + 1) * part)
        for side, src in enumerate((tok, came)):
            more = jnp.dot(src[:, rows], wq_s[rows, :], preferred_element_type=F32)
            got[side] = more if i == 0 else got[side] + more
    for side, span in enumerate(halves()):
        rot = rotation(table[span, :])
        for h in range(half // HD):
            out[h, span, :] = rot(got[side][:, h * HD : (h + 1) * HD]).astype(BF16)


def project_q(tokens, came, w_query, table):
    depth, width = w_query.shape
    return call(
        q_body, "project_q", like(width // 2 // HD, CHIP, HD), [VMEM, VMEM, HBM, VMEM], VMEM,
        [pltpu.VMEM((depth, width // 2), BF16), pltpu.SemaphoreType.DMA((Q_PARTS,))],
        limit=8, flops=2 * CHIP * depth * width // 2, moved=6,
    )(tokens, came, w_query, table)


NONE = 99
NEAR = ((1, 2), (4, 8))
EARLY = ((8, 9), (2, 6))
MIDDLE = ((3, 4), (3, 7))
LAST = ((5, 6, 7), (1, 5, 9))


def fill(out, slots, late, even):
    place = lax.axis_index("ctx")
    column = lax.rem(lax.div(place, 2), 4)
    skip = jnp.where(lax.rem(place, 2) == 0, even, jnp.where(column >= late, 1, 0))
    for i in range(out.shape[0] // UNIT):
        out[i * UNIT : (i + 1) * UNIT, :] = slots[skip + i]


def pairs_body(unit, r1, r2, out_b, out_c, slots):
    for i, src in enumerate((unit, r1, r2)):
        slots[i] = src[...]
    fill(out_b, slots, 2, 0)
    fill(out_c, slots, 1, 0)


def bundle_pairs(unit, r1, r2):
    pair = like(2 * UNIT, 2 * HD)
    return call(
        pairs_body, "bundle_pairs", (pair, pair), [VMEM] * 3, (VMEM,) * 2,
        [pltpu.VMEM((3, UNIT, 2 * HD), BF16)], limit=2,
    )(unit, r1, r2)


def row_body(unit, r1, r2, r3, after, out_a, slots):
    for i, src in enumerate((unit, r1, r2, r3)):
        slots[i] = src[...]
    fill(out_a, slots, 3, 1)


def bundle_row(unit, r1, r2, r3, after):
    return call(
        row_body, "bundle_row", like(3 * UNIT, 2 * HD), [VMEM] * 5, VMEM,
        [pltpu.VMEM((4, UNIT, 2 * HD), BF16)], limit=2,
    )(unit, r1, r2, r3, after)


CONTRACT = (((1,), (1,)), ((), ()))


def tags_of(unit):
    tags = unit[CHIP:UNIT, :].astype(F32)
    return tags, jnp.transpose(tags, (1, 0))[:, 0:1]


def with_ones(values):
    return jnp.concatenate([values, jnp.ones((CHIP, HD), BF16)], axis=1)


def add_units(queries, units, steps, q_tag, before, after):
    place = lax.axis_index("ctx")
    odd = lax.rem(place, 2) == 1
    chip = lax.div(place, 2)
    for i, (block, even_step, odd_step) in enumerate(zip(units, *steps)):
        valid = chip >= jnp.where(odd, odd_step, even_step)
        k_tag = block[CHIP:, :].astype(F32)[0:1, :]
        bias = jnp.where((k_tag == q_tag) & valid, 0.0, -1e30)
        keys = block[:CHIP, :HD]
        values = with_ones(block[:CHIP, HD:])
        for h in range(after[0].shape[0]):
            s = lax.dot_general(queries(h), keys, CONTRACT, preferred_element_type=F32)
            s = s * SCALE + bias
            if i == 0:
                old, old_sum, old_acc = before(h)
            else:
                old, old_sum, old_acc = (ref[h] for ref in after)
            top = jnp.maximum(old, jnp.max(s, axis=1, keepdims=True))
            fade = jnp.exp2(old - top)
            w = jnp.exp2(s - jnp.concatenate([top, top], axis=1)).astype(BF16)
            got = jnp.dot(w, values, preferred_element_type=F32)
            after[0][h] = top
            after[1][h] = fade * old_sum + got[:, HD:]
            after[2][h] = fade * old_acc + got[:, :HD]


def parts(src):
    return [src[i * UNIT : (i + 1) * UNIT, :] for i in range(src.shape[0] // UNIT)]


def near_body(qs, unit, r1, r2, m_s, l_s, acc):
    tags, q_tag = tags_of(unit)
    rows = lax.broadcasted_iota(jnp.int32, (CHIP, CHIP), 0)
    cols = lax.broadcasted_iota(jnp.int32, (CHIP, CHIP), 1)
    bias = jnp.where((tags[0:1, :] == q_tag) & (cols <= rows), 0.0, -1e30)
    keys, values = unit[:CHIP, :HD], with_ones(unit[:CHIP, HD:])
    for h in range(qs.shape[0]):
        s = lax.dot_general(qs[h], keys, CONTRACT, preferred_element_type=F32)
        s = s * SCALE + bias
        top = jnp.max(s, axis=1, keepdims=True)
        got = jnp.dot(jnp.exp2(s - top).astype(BF16), values, preferred_element_type=F32)
        m_s[h] = jnp.broadcast_to(top, (CHIP, HD))
        l_s[h] = got[:, HD:]
        acc[h] = got[:, :HD]
    state = (m_s, l_s, acc)
    units = [src[...] for src in (r1, r2)]
    add_units(lambda h: qs[h], units, NEAR, q_tag, lambda h: [ref[h] for ref in state], state)


def attend_near(qs, unit, r1, r2):
    heads = qs.shape[0]
    state = like(heads, CHIP, HD, dtype=F32)
    return call(
        near_body, "attend_near", (state, state, state), [VMEM] * 4, (VMEM,) * 3, limit=8,
        flops=12 * heads * CHIP * CHIP * HD, exps=3 * heads * CHIP * CHIP,
    )(qs, unit, r1, r2)


def early_body(qs, m_in, l_in, acc_in, unit, far_b, m_s, l_s, acc):
    before = (m_in, l_in, acc_in)
    add_units(
        lambda h: qs[h], parts(far_b), EARLY, tags_of(unit)[1],
        lambda h: [ref[h] for ref in before], (m_s, l_s, acc),
    )


def attend_early(qs, m_in, l_in, acc_in, unit, far_b):
    heads = qs.shape[0]
    state = like(heads, CHIP, HD, dtype=F32)
    return call(
        early_body, "attend_early", (state,) * 3, [VMEM] * 6, (VMEM,) * 3, limit=8,
        flops=64 * heads * CHIP * CHIP * HD, exps=2 * heads * CHIP * CHIP,
    )(qs, m_in, l_in, acc_in, unit, far_b)


def middle_body(qs, m_in, l_in, acc_in, unit, r3, r4, far_c, m_s, l_s, acc):
    before = (m_in, l_in, acc_in)
    even = core_index() == 0
    third, fourth = parts(far_c)
    units = [jnp.where(even, r3[...], third), jnp.where(even, r4[...], fourth)]
    add_units(
        lambda h: qs[h], units, MIDDLE, tags_of(unit)[1],
        lambda h: [ref[h] for ref in before], (m_s, l_s, acc),
    )


def attend_middle(qs, m_in, l_in, acc_in, unit, r3, r4, far_c):
    heads = qs.shape[0]
    state = like(heads, CHIP, HD, dtype=F32)
    return call(
        middle_body, "attend_middle", (state,) * 3, [VMEM] * 8, (VMEM,) * 3, limit=8,
        flops=64 * heads * CHIP * CHIP * HD, exps=2 * heads * CHIP * CHIP,
    )(qs, m_in, l_in, acc_in, unit, r3, r4, far_c)


def attend_last(side, qs, m_in, l_in, acc_in, unit, far_a):
    heads = qs.shape[0]

    def body(qs, m_in, l_in, acc_in, unit, far_a, out, tag_s, m_s, l_s, acc):
        rows = halves()[side]
        before = (m_in, l_in, acc_in)
        tag_s[...] = jnp.broadcast_to(tags_of(unit)[1], (CHIP, HD))
        add_units(
            lambda h: qs[h, rows, :], parts(far_a), LAST, tag_s[rows, :][:, 0:1],
            lambda h: [ref[h, rows, :] for ref in before], (m_s, l_s, acc),
        )
        for h in range(heads):
            out[:, h * HD : (h + 1) * HD] = (acc[h] / l_s[h]).astype(BF16)

    state = pltpu.VMEM((heads, ROWS, HD), F32)
    return call(
        body, "attend_last", like(ROWS, heads * HD), [VMEM] * 6, VMEM,
        [pltpu.VMEM((CHIP, HD), F32), state, state, state],
        limit=8, flops=4 * heads * ROWS * 3 * CHIP * HD, exps=heads * ROWS * 3 * CHIP,
    )(qs, m_in, l_in, acc_in, unit, far_a)


def project_out(xm, xr, w_out, groups, parts, dtype):
    depth = xm.shape[1]
    width = w_out.shape[1] // groups
    half = width // 2

    def body(xm, xr, w, *outs):
        core = core_index()
        own = pl.ds(pl.multiple_of(core * depth, depth), depth)
        other = pl.ds(pl.multiple_of((1 - core) * depth, depth), depth)
        for (shift, side), out in zip(parts, outs):
            group = lax.rem(lax.axis_index("head") + shift, groups)
            cols = pl.ds(pl.multiple_of(group * width + side * half, half), half)
            got = jnp.dot(xm[...], w[own, cols], preferred_element_type=F32)
            got += jnp.dot(xr[...], w[other, cols], preferred_element_type=F32)
            out[...] = got.astype(dtype)

    return call(
        body, "project_out", (like(ROWS, half, dtype=dtype),) * len(parts), [VMEM] * 3,
        (VMEM,) * len(parts), limit=4,
        flops=2 * ROWS * 2 * depth * half * len(parts), moved=len(parts),
    )(xm, xr, w_out)


def add_body(a, b, p, q, out_a, out_b):
    out_a[...] = (a[...] + p[...].astype(F32)).astype(BF16)
    out_b[...] = (b[...] + q[...].astype(F32)).astype(BF16)


def add_passing(a, b, p, q):
    out = like(*p.shape)
    return call(add_body, "add_passing", (out, out), [VMEM] * 4, (VMEM,) * 2, limit=2)(a, b, p, q)


def total_body(own_a, own_b, left_a, left_b, right_a, right_b, out):
    half = own_a.shape[1]
    for at, pieces in ((0, (own_a, left_a, right_a)), (half, (own_b, left_b, right_b))):
        total = pieces[0][...] + pieces[1][...].astype(F32) + pieces[2][...].astype(F32)
        out[:, at : at + half] = total.astype(BF16)


def add_total(*pieces):
    rows, half = pieces[0].shape
    return call(total_body, "add_total", like(rows, 2 * half), [VMEM] * 6, VMEM, limit=2)(*pieces)


def shards(tokens, w_query, w_key, w_value, w_out, doc_ids):
    ranks = lax.axis_size("ctx")
    groups = lax.axis_size("head")
    table = jnp.asarray(rope_table(ranks * ROWS))

    def swap(value):
        return lax.ppermute(value, "ctx", [(r, r ^ 1) for r in range(ranks)])

    def along(value, even, odd):
        moves = []
        for r in range(ranks):
            step = odd if r % 2 else even
            if step is not None:
                moves.append((r, 2 * step(r // 2) + r % 2))
        return lax.ppermute(value, "ctx", moves)

    def ahead(step):
        return lambda chip: (chip + step) % (ranks // 2)

    def in_row(step):
        return lambda chip: chip // 4 * 4 + (chip + step) % 4

    docs = doc_ids.reshape(1, -1)
    came, docs_came = swap(tokens), swap(docs)
    tokens, w_key, w_value, w_query, table, docs = (
        pltpu.with_memory_space_constraint(a, pltpu.HBM)
        for a in (tokens, w_key, w_value, w_query, table, docs)
    )
    half, tokens, w_kv, docs, table = project_own(tokens, w_key, w_value, docs, table)
    unit = project_unit(half, came, w_kv, docs, docs_came, table)
    r1 = along(unit, ahead(1), ahead(4))
    r2 = along(unit, ahead(2), ahead(8))
    r3 = along(unit, ahead(3), ahead(12))
    r4 = along(unit, ahead(4), in_row(3))
    r1, r2, came = lax.optimization_barrier((r1, r2, came))
    out_b, out_c = bundle_pairs(unit, r1, r2)
    far_b = along(out_b, ahead(8), in_row(2))
    far_c = along(out_c, None, in_row(3))
    far_a = along(bundle_row(unit, r1, r2, r3, r4), ahead(4), in_row(1))
    qs = project_q(tokens, came, w_query, table)
    state = attend_near(qs, unit, r1, r2)
    state = attend_early(qs, *state, unit, far_b)
    state = attend_middle(qs, *state, unit, r3, r4, far_c)
    xr = swap(attend_last(1, qs, *state, unit, far_a))
    xm = attend_last(0, qs, *state, unit, far_a)

    def shift(value, step):
        return lax.ppermute(value, "head", [(g, (g + step) % groups) for g in range(groups)])

    a2, b2 = project_out(xm, xr, w_out, groups, ((2, 0), (2, 1)), BF16)
    pass_a, pass_b = shift(a2, 1), shift(b2, -1)
    b1, a3 = project_out(xm, xr, w_out, groups, ((1, 1), (3, 0)), BF16)
    left_b, right_a = shift(b1, 1), shift(a3, -1)
    a1, b3, a0, b0 = project_out(xm, xr, w_out, groups, ((1, 0), (3, 1), (0, 0), (0, 1)), F32)
    a1, b3 = add_passing(a1, b3, pass_a, pass_b)
    left_a, right_b = shift(a1, 1), shift(b3, -1)
    return add_total(a0, b0, left_a, left_b, right_a, right_b)


def solution(mesh):
    return jax.shard_map(
        shards,
        mesh=mesh,
        in_specs=(
            P("ctx", None),
            P(None, "head"),
            P(None, "head"),
            P(None, "head"),
            P("head", None),
            P("ctx"),
        ),
        out_specs=P("ctx", "head"),
        check_vma=False,
    )
```

```python
import math

import jax
import jax.numpy as jnp
import numpy as np
from jax import lax
from jax.experimental import pallas as pl
from jax.experimental.pallas import tpu as pltpu
from jax.sharding import PartitionSpec as P

HD = 128
ROWS = 128
UNIT = 264
F32 = jnp.float32
BF16 = jnp.bfloat16
MIB = 1 << 20
SCALE = math.log2(math.e) / math.sqrt(HD)


def rope_table(count):
    half = HD // 2
    freqs = 500000.0 ** (-2.0 * np.arange(half, dtype=np.float64) / HD)
    angles = np.arange(count, dtype=np.float64)[:, None] * freqs[None, :]
    return np.concatenate([np.cos(angles), np.sin(angles)], axis=1).astype(np.float32)


def rotation(table):
    half = HD // 2
    cosine, sine = table[:, :half], table[:, half:]
    cosine = jnp.concatenate([cosine, cosine], axis=1)
    sine = jnp.concatenate([-sine, sine], axis=1)
    return lambda t: t * cosine + pltpu.roll(t, half, 1) * sine


SMEM = pl.BlockSpec(memory_space=pltpu.SMEM)
VMEM = pl.BlockSpec(memory_space=pltpu.VMEM)
HBM = pl.BlockSpec(memory_space=pltpu.HBM)


def like(*dims, dtype=BF16):
    return jax.ShapeDtypeStruct(dims, dtype)


def call(body, name, out, ins, outs, scratch=(), limit=4, flops=0, moved=1, exps=0):
    return pl.pallas_call(
        body,
        out_shape=out,
        in_specs=ins,
        out_specs=outs,
        scratch_shapes=list(scratch),
        name=name,
        cost_estimate=pl.CostEstimate(
            flops=flops, bytes_accessed=moved * MIB, transcendentals=exps
        ),
        compiler_params=pltpu.CompilerParams(vmem_limit_bytes=limit * MIB),
    )


def core_index():
    return lax.rem(lax.axis_index("ctx"), 2)


def table_rows(table):
    return table.at[pl.ds(pl.multiple_of(lax.axis_index("ctx") * ROWS, ROWS), ROWS), :]


def started(copies):
    for copy in copies:
        copy.start()
    return copies


KV_PARTS = 4
CHIP = 2 * ROWS


def halves():
    core = core_index()
    own = pl.ds(pl.multiple_of(core * ROWS, ROWS), ROWS)
    other = pl.ds(pl.multiple_of((1 - core) * ROWS, ROWS), ROWS)
    return own, other


def own_body(tok, wk, wv, docs, table, half, tok_s, w_s, docs_s, table_s, acc, sems):
    part = tok.shape[1] // KV_PARTS
    cols = pl.ds(pl.multiple_of(core_index() * HD, HD), HD)
    copies = []
    for i in range(KV_PARTS):
        cut = pl.ds(i * part, part)
        copies.append(
            started([
                pltpu.make_async_copy(tok.at[:, cut], tok_s.at[:, cut], sems.at[3 * i]),
                pltpu.make_async_copy(
                    wk.at[cut, cols], w_s.at[cut, pl.ds(0, HD)], sems.at[3 * i + 1]
                ),
                pltpu.make_async_copy(
                    wv.at[cut, cols], w_s.at[cut, pl.ds(HD, HD)], sems.at[3 * i + 2]
                ),
            ])
        )
    first = pl.multiple_of(lax.div(lax.axis_index("ctx"), 2) * CHIP, CHIP)
    small = started([
        pltpu.make_async_copy(docs, docs_s, sems.at[3 * KV_PARTS]),
        pltpu.make_async_copy(table.at[pl.ds(first, CHIP), :], table_s, sems.at[3 * KV_PARTS + 1]),
    ])
    for i, group in enumerate(copies):
        for copy in group:
            copy.wait()
        cut = slice(i * part, (i + 1) * part)
        more = jnp.dot(tok_s[:, cut], w_s[cut, :], preferred_element_type=F32)
        if i == 0:
            acc[...] = more
        else:
            acc[...] += more
    for copy in small:
        copy.wait()
    rot = rotation(table_s[halves()[0], :])
    half[:, :HD] = rot(acc[:, :HD]).astype(BF16)
    half[:, HD:] = acc[:, HD:].astype(BF16)


def project_own(tokens, w_key, w_value, docs, table):
    depth = tokens.shape[1]
    return call(
        own_body, "project_own",
        (
            like(ROWS, 2 * HD),
            like(ROWS, depth),
            like(depth, 2 * HD),
            like(1, ROWS, dtype=jnp.int32),
            like(CHIP, HD, dtype=F32),
        ),
        [HBM] * 5, (VMEM,) * 5,
        [pltpu.VMEM((ROWS, 2 * HD), F32), pltpu.SemaphoreType.DMA((3 * KV_PARTS + 2,))],
        limit=6, flops=2 * ROWS * depth * 2 * HD, moved=3,
    )(tokens, w_key, w_value, docs, table)


def unit_body(half, came, w, docs, docs_came, table, unit):
    own, other = halves()
    got = jnp.dot(came[...], w[...], preferred_element_type=F32)
    unit[own, :] = half[...]
    unit[other, :HD] = rotation(table[other, :])(got[:, :HD]).astype(BF16)
    unit[other, HD:] = got[:, HD:].astype(BF16)
    first = core_index() == 0
    a, b = docs[...], docs_came[...]
    tags = jnp.concatenate([jnp.where(first, a, b), jnp.where(first, b, a)], axis=1)
    tags = (tags + 1).astype(F32)
    unit[CHIP:, :] = jnp.broadcast_to(tags, (8, CHIP)).astype(BF16)


def project_unit(half, came, w, docs, docs_came, table):
    return call(
        unit_body, "project_unit", like(UNIT, 2 * HD), [VMEM] * 6, VMEM, limit=2,
        flops=2 * ROWS * w.shape[0] * 2 * HD,
    )(half, came, w, docs, docs_came, table)


Q_PARTS = 4


def q_body(tok, came, wq, table, out, wq_s, sems):
    half = wq.shape[1] // 2
    part = wq.shape[0] // Q_PARTS
    cols = pl.ds(pl.multiple_of(core_index() * half, half), half)
    copies = []
    for i in range(Q_PARTS):
        rows = pl.ds(i * part, part)
        copies += started([
            pltpu.make_async_copy(wq.at[rows, cols], wq_s.at[rows, :], sems.at[i])
        ])
    got = [None, None]
    for i in range(Q_PARTS):
        copies[i].wait()
        rows = slice(i * part, (i + 1) * part)
        for side, src in enumerate((tok, came)):
            more = jnp.dot(src[:, rows], wq_s[rows, :], preferred_element_type=F32)
            got[side] = more if i == 0 else got[side] + more
    for side, span in enumerate(halves()):
        rot = rotation(table[span, :])
        for h in range(half // HD):
            out[h, span, :] = rot(got[side][:, h * HD : (h + 1) * HD]).astype(BF16)


def project_q(tokens, came, w_query, table):
    depth, width = w_query.shape
    return call(
        q_body, "project_q", like(width // 2 // HD, CHIP, HD), [VMEM, VMEM, HBM, VMEM], VMEM,
        [pltpu.VMEM((depth, width // 2), BF16), pltpu.SemaphoreType.DMA((Q_PARTS,))],
        limit=8, flops=2 * CHIP * depth * width // 2, moved=6,
    )(tokens, came, w_query, table)


NONE = 99
NEAR = ((1, 2), (4, 8))
EARLY = ((8, 9), (2, 6))
MIDDLE = ((3, 4), (3, 7))
LAST = ((5, 6, 7), (1, 5, 9))


def fill(out, slots, late, even):
    place = lax.axis_index("ctx")
    column = lax.rem(lax.div(place, 2), 4)
    skip = jnp.where(lax.rem(place, 2) == 0, even, jnp.where(column >= late, 1, 0))
    for i in range(out.shape[0] // UNIT):
        out[i * UNIT : (i + 1) * UNIT, :] = slots[skip + i]


def pairs_body(unit, r1, r2, out_b, out_c, slots):
    for i, src in enumerate((unit, r1, r2)):
        slots[i] = src[...]
    fill(out_b, slots, 2, 0)
    fill(out_c, slots, 1, 0)


def bundle_pairs(unit, r1, r2):
    pair = like(2 * UNIT, 2 * HD)
    return call(
        pairs_body, "bundle_pairs", (pair, pair), [VMEM] * 3, (VMEM,) * 2,
        [pltpu.VMEM((3, UNIT, 2 * HD), BF16)], limit=2,
    )(unit, r1, r2)


def row_body(unit, r1, r2, r3, after, out_a, slots):
    for i, src in enumerate((unit, r1, r2, r3)):
        slots[i] = src[...]
    fill(out_a, slots, 3, 1)


def bundle_row(unit, r1, r2, r3, after):
    return call(
        row_body, "bundle_row", like(3 * UNIT, 2 * HD), [VMEM] * 5, VMEM,
        [pltpu.VMEM((4, UNIT, 2 * HD), BF16)], limit=2,
    )(unit, r1, r2, r3, after)


CONTRACT = (((1,), (1,)), ((), ()))


def tags_of(unit):
    tags = unit[CHIP:UNIT, :].astype(F32)
    return tags, jnp.transpose(tags, (1, 0))[:, 0:1]


def with_ones(values):
    return jnp.concatenate([values, jnp.ones((CHIP, HD), BF16)], axis=1)


def add_units(queries, units, steps, q_tag, before, after):
    place = lax.axis_index("ctx")
    odd = lax.rem(place, 2) == 1
    chip = lax.div(place, 2)
    for i, (block, even_step, odd_step) in enumerate(zip(units, *steps)):
        valid = chip >= jnp.where(odd, odd_step, even_step)
        k_tag = block[CHIP:, :].astype(F32)[0:1, :]
        bias = jnp.where((k_tag == q_tag) & valid, 0.0, -1e30)
        keys = block[:CHIP, :HD]
        values = with_ones(block[:CHIP, HD:])
        for h in range(after[0].shape[0]):
            s = lax.dot_general(queries(h), keys, CONTRACT, preferred_element_type=F32)
            s = s * SCALE + bias
            if i == 0:
                old, old_sum, old_acc = before(h)
            else:
                old, old_sum, old_acc = (ref[h] for ref in after)
            top = jnp.maximum(old, jnp.max(s, axis=1, keepdims=True))
            fade = jnp.exp2(old - top)
            w = jnp.exp2(s - jnp.concatenate([top, top], axis=1)).astype(BF16)
            got = jnp.dot(w, values, preferred_element_type=F32)
            after[0][h] = top
            after[1][h] = fade * old_sum + got[:, HD:]
            after[2][h] = fade * old_acc + got[:, :HD]


def parts(src):
    return [src[i * UNIT : (i + 1) * UNIT, :] for i in range(src.shape[0] // UNIT)]


def near_body(qs, unit, r1, r2, m_s, l_s, acc):
    tags, q_tag = tags_of(unit)
    rows = lax.broadcasted_iota(jnp.int32, (CHIP, CHIP), 0)
    cols = lax.broadcasted_iota(jnp.int32, (CHIP, CHIP), 1)
    bias = jnp.where((tags[0:1, :] == q_tag) & (cols <= rows), 0.0, -1e30)
    keys, values = unit[:CHIP, :HD], with_ones(unit[:CHIP, HD:])
    for h in range(qs.shape[0]):
        s = lax.dot_general(qs[h], keys, CONTRACT, preferred_element_type=F32)
        s = s * SCALE + bias
        top = jnp.max(s, axis=1, keepdims=True)
        got = jnp.dot(jnp.exp2(s - top).astype(BF16), values, preferred_element_type=F32)
        m_s[h] = jnp.broadcast_to(top, (CHIP, HD))
        l_s[h] = got[:, HD:]
        acc[h] = got[:, :HD]
    state = (m_s, l_s, acc)
    units = [src[...] for src in (r1, r2)]
    add_units(lambda h: qs[h], units, NEAR, q_tag, lambda h: [ref[h] for ref in state], state)


def attend_near(qs, unit, r1, r2):
    heads = qs.shape[0]
    state = like(heads, CHIP, HD, dtype=F32)
    return call(
        near_body, "attend_near", (state, state, state), [VMEM] * 4, (VMEM,) * 3, limit=8,
        flops=12 * heads * CHIP * CHIP * HD, exps=3 * heads * CHIP * CHIP,
    )(qs, unit, r1, r2)


def early_body(qs, m_in, l_in, acc_in, unit, far_b, m_s, l_s, acc):
    before = (m_in, l_in, acc_in)
    add_units(
        lambda h: qs[h], parts(far_b), EARLY, tags_of(unit)[1],
        lambda h: [ref[h] for ref in before], (m_s, l_s, acc),
    )


def attend_early(qs, m_in, l_in, acc_in, unit, far_b):
    heads = qs.shape[0]
    state = like(heads, CHIP, HD, dtype=F32)
    return call(
        early_body, "attend_early", (state,) * 3, [VMEM] * 6, (VMEM,) * 3, limit=8,
        flops=64 * heads * CHIP * CHIP * HD, exps=2 * heads * CHIP * CHIP,
    )(qs, m_in, l_in, acc_in, unit, far_b)


def middle_body(qs, m_in, l_in, acc_in, unit, r3, r4, far_c, m_s, l_s, acc):
    before = (m_in, l_in, acc_in)
    even = core_index() == 0
    third, fourth = parts(far_c)
    units = [jnp.where(even, r3[...], third), jnp.where(even, r4[...], fourth)]
    add_units(
        lambda h: qs[h], units, MIDDLE, tags_of(unit)[1],
        lambda h: [ref[h] for ref in before], (m_s, l_s, acc),
    )


def attend_middle(qs, m_in, l_in, acc_in, unit, r3, r4, far_c):
    heads = qs.shape[0]
    state = like(heads, CHIP, HD, dtype=F32)
    return call(
        middle_body, "attend_middle", (state,) * 3, [VMEM] * 8, (VMEM,) * 3, limit=8,
        flops=64 * heads * CHIP * CHIP * HD, exps=2 * heads * CHIP * CHIP,
    )(qs, m_in, l_in, acc_in, unit, r3, r4, far_c)


def attend_last(side, qs, m_in, l_in, acc_in, unit, far_a):
    heads = qs.shape[0]

    def body(qs, m_in, l_in, acc_in, unit, far_a, out, tag_s, m_s, l_s, acc):
        rows = halves()[side]
        before = (m_in, l_in, acc_in)
        tag_s[...] = jnp.broadcast_to(tags_of(unit)[1], (CHIP, HD))
        add_units(
            lambda h: qs[h, rows, :], parts(far_a), LAST, tag_s[rows, :][:, 0:1],
            lambda h: [ref[h, rows, :] for ref in before], (m_s, l_s, acc),
        )
        for h in range(heads):
            out[:, h * HD : (h + 1) * HD] = (acc[h] / l_s[h]).astype(BF16)

    state = pltpu.VMEM((heads, ROWS, HD), F32)
    return call(
        body, "attend_last", like(ROWS, heads * HD), [VMEM] * 6, VMEM,
        [pltpu.VMEM((CHIP, HD), F32), state, state, state],
        limit=8, flops=4 * heads * ROWS * 3 * CHIP * HD, exps=heads * ROWS * 3 * CHIP,
    )(qs, m_in, l_in, acc_in, unit, far_a)


def project_out(xm, xr, w_out, groups, shifts, dtype):
    depth = xm.shape[1]
    width = w_out.shape[1] // groups

    def body(xm, xr, w, *outs):
        core = core_index()
        own = pl.ds(pl.multiple_of(core * depth, depth), depth)
        other = pl.ds(pl.multiple_of((1 - core) * depth, depth), depth)
        for shift, out in zip(shifts, outs):
            group = lax.rem(lax.axis_index("head") + shift, groups)
            cols = pl.ds(pl.multiple_of(group * width, width), width)
            got = jnp.dot(xm[...], w[own, cols], preferred_element_type=F32)
            got += jnp.dot(xr[...], w[other, cols], preferred_element_type=F32)
            out[...] = got.astype(dtype)

    return call(
        body, "project_out", (like(ROWS, width, dtype=dtype),) * len(shifts), [VMEM] * 3,
        (VMEM,) * len(shifts), limit=4,
        flops=2 * ROWS * 2 * depth * width * len(shifts), moved=2 * len(shifts),
    )(xm, xr, w_out)


def total_body(own, first, second, third, out):
    total = own[...] + first[...].astype(F32)
    total += second[...].astype(F32) + third[...].astype(F32)
    out[...] = total.astype(BF16)


def add_total(own, *came):
    return call(total_body, "add_total", like(*own.shape), [VMEM] * 4, VMEM, limit=2)(own, *came)


def shards(tokens, w_query, w_key, w_value, w_out, doc_ids):
    ranks = lax.axis_size("ctx")
    groups = lax.axis_size("head")
    table = jnp.asarray(rope_table(ranks * ROWS))

    def swap(value):
        return lax.ppermute(value, "ctx", [(r, r ^ 1) for r in range(ranks)])

    def along(value, even, odd):
        moves = [(r, 2 * (odd if r % 2 else even)(r // 2) + r % 2) for r in range(ranks)]
        return lax.ppermute(value, "ctx", moves)

    def ahead(step):
        return lambda chip: (chip + step) % (ranks // 2)

    def in_row(step):
        return lambda chip: chip // 4 * 4 + (chip + step) % 4

    docs = doc_ids.reshape(1, -1)
    came, docs_came = swap(tokens), swap(docs)
    tokens, w_key, w_value, w_query, table, docs = (
        pltpu.with_memory_space_constraint(a, pltpu.HBM)
        for a in (tokens, w_key, w_value, w_query, table, docs)
    )
    half, tokens, w_kv, docs, table = project_own(tokens, w_key, w_value, docs, table)
    unit = project_unit(half, came, w_kv, docs, docs_came, table)
    r1 = along(unit, ahead(1), ahead(4))
    r2 = along(unit, ahead(2), ahead(8))
    r3 = along(unit, ahead(3), ahead(12))
    r4 = along(unit, ahead(4), in_row(3))
    r1, r2, came = lax.optimization_barrier((r1, r2, came))
    out_b, out_c = bundle_pairs(unit, r1, r2)
    far_b = along(out_b, ahead(8), in_row(2))
    far_c = along(out_c, ahead(12), in_row(3))
    far_a = along(bundle_row(unit, r1, r2, r3, r4), ahead(4), in_row(1))
    qs = project_q(tokens, came, w_query, table)
    state = attend_near(qs, unit, r1, r2)
    state = attend_early(qs, *state, unit, far_b)
    state = attend_middle(qs, *state, unit, r3, r4, far_c)
    xr = swap(attend_last(1, qs, *state, unit, far_a))
    xm = attend_last(0, qs, *state, unit, far_a)

    def shift(value, step):
        return lax.ppermute(value, "head", [(g, (g + step) % groups) for g in range(groups)])

    came = []
    for step in (3, 1, 2):
        (partial,) = project_out(xm, xr, w_out, groups, (step,), BF16)
        came.append(shift(partial, step))
    (own,) = project_out(xm, xr, w_out, groups, (0,), F32)
    return add_total(own, *came)


def solution(mesh):
    return jax.shard_map(
        shards,
        mesh=mesh,
        in_specs=(
            P("ctx", None),
            P(None, "head"),
            P(None, "head"),
            P(None, "head"),
            P("head", None),
            P("ctx"),
        ),
        out_specs=P("ctx", "head"),
        check_vma=False,
    )
```

```python
import functools
import math

import jax
import jax.numpy as jnp
import numpy as np
from jax import lax
from jax.experimental import pallas as pl
from jax.experimental.pallas import tpu as pltpu
from jax.sharding import PartitionSpec as P

HD = 128
ROWS = 128
UNIT = 264
F32 = jnp.float32
BF16 = jnp.bfloat16
MIB = 1 << 20
SCALE = math.log2(math.e) / math.sqrt(HD)


def rope_table(count):
    half = HD // 2
    freqs = 500000.0 ** (-2.0 * np.arange(half, dtype=np.float64) / HD)
    angles = np.arange(count, dtype=np.float64)[:, None] * freqs[None, :]
    return np.concatenate([np.cos(angles), np.sin(angles)], axis=1).astype(np.float32)


def rotation(table):
    half = HD // 2
    cosine, sine = table[:, :half], table[:, half:]
    cosine = jnp.concatenate([cosine, cosine], axis=1)
    sine = jnp.concatenate([-sine, sine], axis=1)
    return lambda t: t * cosine + pltpu.roll(t, half, 1) * sine


SMEM = pl.BlockSpec(memory_space=pltpu.SMEM)
VMEM = pl.BlockSpec(memory_space=pltpu.VMEM)
HBM = pl.BlockSpec(memory_space=pltpu.HBM)


def like(*dims, dtype=BF16):
    return jax.ShapeDtypeStruct(dims, dtype)


def call(body, name, out, ins, outs, scratch=(), limit=4, flops=0, moved=1, exps=0):
    return pl.pallas_call(
        body,
        out_shape=out,
        in_specs=ins,
        out_specs=outs,
        scratch_shapes=list(scratch),
        name=name,
        cost_estimate=pl.CostEstimate(
            flops=flops, bytes_accessed=moved * MIB, transcendentals=exps
        ),
        compiler_params=pltpu.CompilerParams(vmem_limit_bytes=limit * MIB),
    )


def core_index():
    return lax.rem(lax.axis_index("ctx"), 2)


def table_rows(table):
    return table.at[pl.ds(pl.multiple_of(lax.axis_index("ctx") * ROWS, ROWS), ROWS), :]


def started(copies):
    for copy in copies:
        copy.start()
    return copies


KV_PARTS = 4
CHIP = 2 * ROWS


def halves():
    core = core_index()
    own = pl.ds(pl.multiple_of(core * ROWS, ROWS), ROWS)
    other = pl.ds(pl.multiple_of((1 - core) * ROWS, ROWS), ROWS)
    return own, other


def own_body(tok, wk, wv, docs, table, half, tok_s, w_s, docs_s, table_s, acc, sems):
    part = tok.shape[1] // KV_PARTS
    cols = pl.ds(pl.multiple_of(core_index() * HD, HD), HD)
    copies = []
    for i in range(KV_PARTS):
        cut = pl.ds(i * part, part)
        copies.append(
            started([
                pltpu.make_async_copy(tok.at[:, cut], tok_s.at[:, cut], sems.at[3 * i]),
                pltpu.make_async_copy(
                    wk.at[cut, cols], w_s.at[cut, pl.ds(0, HD)], sems.at[3 * i + 1]
                ),
                pltpu.make_async_copy(
                    wv.at[cut, cols], w_s.at[cut, pl.ds(HD, HD)], sems.at[3 * i + 2]
                ),
            ])
        )
    first = pl.multiple_of(lax.div(lax.axis_index("ctx"), 2) * CHIP, CHIP)
    small = started([
        pltpu.make_async_copy(docs, docs_s, sems.at[3 * KV_PARTS]),
        pltpu.make_async_copy(table.at[pl.ds(first, CHIP), :], table_s, sems.at[3 * KV_PARTS + 1]),
    ])
    for i, group in enumerate(copies):
        for copy in group:
            copy.wait()
        cut = slice(i * part, (i + 1) * part)
        more = jnp.dot(tok_s[:, cut], w_s[cut, :], preferred_element_type=F32)
        if i == 0:
            acc[...] = more
        else:
            acc[...] += more
    for copy in small:
        copy.wait()
    rot = rotation(table_s[halves()[0], :])
    half[:, :HD] = rot(acc[:, :HD]).astype(BF16)
    half[:, HD:] = acc[:, HD:].astype(BF16)


def project_own(tokens, w_key, w_value, docs, table):
    depth = tokens.shape[1]
    return call(
        own_body, "project_own",
        (
            like(ROWS, 2 * HD),
            like(ROWS, depth),
            like(depth, 2 * HD),
            like(1, ROWS, dtype=jnp.int32),
            like(CHIP, HD, dtype=F32),
        ),
        [HBM] * 5, (VMEM,) * 5,
        [pltpu.VMEM((ROWS, 2 * HD), F32), pltpu.SemaphoreType.DMA((3 * KV_PARTS + 2,))],
        limit=6, flops=2 * ROWS * depth * 2 * HD, moved=3,
    )(tokens, w_key, w_value, docs, table)


def unit_body(half, came, w, docs, docs_came, table, unit):
    own, other = halves()
    got = jnp.dot(came[...], w[...], preferred_element_type=F32)
    unit[own, :] = half[...]
    unit[other, :HD] = rotation(table[other, :])(got[:, :HD]).astype(BF16)
    unit[other, HD:] = got[:, HD:].astype(BF16)
    first = core_index() == 0
    a, b = docs[...], docs_came[...]
    tags = jnp.concatenate([jnp.where(first, a, b), jnp.where(first, b, a)], axis=1)
    tags = (tags + 1).astype(F32)
    unit[CHIP:, :] = jnp.broadcast_to(tags, (8, CHIP)).astype(BF16)


def project_unit(half, came, w, docs, docs_came, table):
    return call(
        unit_body, "project_unit", like(UNIT, 2 * HD), [VMEM] * 6, VMEM, limit=2,
        flops=2 * ROWS * w.shape[0] * 2 * HD,
    )(half, came, w, docs, docs_came, table)


Q_PARTS = 4


def q_body(side, tok, came, wq, table, out, wq_s, sems):
    half = wq_s.shape[1]
    part = wq.shape[0] // Q_PARTS
    cols = pl.ds(pl.multiple_of((2 * core_index() + side) * half, half), half)
    copies = []
    for i in range(Q_PARTS):
        rows = pl.ds(i * part, part)
        copies += started([
            pltpu.make_async_copy(wq.at[rows, cols], wq_s.at[rows, :], sems.at[i])
        ])
    got = [None, None]
    for i in range(Q_PARTS):
        copies[i].wait()
        rows = slice(i * part, (i + 1) * part)
        for side, src in enumerate((tok, came)):
            more = jnp.dot(src[:, rows], wq_s[rows, :], preferred_element_type=F32)
            got[side] = more if i == 0 else got[side] + more
    for side, span in enumerate(halves()):
        rot = rotation(table[span, :])
        for h in range(half // HD):
            out[h, span, :] = rot(got[side][:, h * HD : (h + 1) * HD]).astype(BF16)


def project_q(tokens, came, w_query, table, side):
    depth, width = w_query.shape
    return call(
        functools.partial(q_body, side), "project_q", like(width // 4 // HD, CHIP, HD), [VMEM, VMEM, HBM, VMEM], VMEM,
        [pltpu.VMEM((depth, width // 4), BF16), pltpu.SemaphoreType.DMA((Q_PARTS,))],
        limit=8, flops=2 * CHIP * depth * width // 4, moved=3,
    )(tokens, came, w_query, table)


NONE = 99
NEAR = ((1, 2), (4, 8))
EARLY = ((8, 9), (2, 6))
MIDDLE = ((3, 4), (3, 7))
LAST = ((5, 6, 7), (1, 5, 9))


def fill(out, slots, late, even):
    place = lax.axis_index("ctx")
    column = lax.rem(lax.div(place, 2), 4)
    skip = jnp.where(lax.rem(place, 2) == 0, even, jnp.where(column >= late, 1, 0))
    for i in range(out.shape[0] // UNIT):
        out[i * UNIT : (i + 1) * UNIT, :] = slots[skip + i]


def bundle_pair(unit, r1, r2, late, after):
    def body(unit, r1, r2, after, out, slots):
        for i, src in enumerate((unit, r1, r2)):
            slots[i] = src[...]
        fill(out, slots, late, 0)

    return call(
        body, "bundle_pair", like(2 * UNIT, 2 * HD), [VMEM] * 4, VMEM,
        [pltpu.VMEM((3, UNIT, 2 * HD), BF16)], limit=2,
    )(unit, r1, r2, after)


def row_body(unit, r1, r2, r3, after, out_a, slots):
    for i, src in enumerate((unit, r1, r2, r3)):
        slots[i] = src[...]
    fill(out_a, slots, 3, 1)


def bundle_row(unit, r1, r2, r3, after):
    return call(
        row_body, "bundle_row", like(3 * UNIT, 2 * HD), [VMEM] * 5, VMEM,
        [pltpu.VMEM((4, UNIT, 2 * HD), BF16)], limit=2,
    )(unit, r1, r2, r3, after)


CONTRACT = (((1,), (1,)), ((), ()))


def tags_of(unit):
    tags = unit[CHIP:UNIT, :].astype(F32)
    return tags, jnp.transpose(tags, (1, 0))[:, 0:1]


def with_ones(values):
    return jnp.concatenate([values, jnp.ones((CHIP, HD), BF16)], axis=1)


def add_units(queries, units, steps, q_tag, before, after):
    place = lax.axis_index("ctx")
    odd = lax.rem(place, 2) == 1
    chip = lax.div(place, 2)
    for i, (block, even_step, odd_step) in enumerate(zip(units, *steps)):
        valid = chip >= jnp.where(odd, odd_step, even_step)
        k_tag = block[CHIP:, :].astype(F32)[0:1, :]
        bias = jnp.where((k_tag == q_tag) & valid, 0.0, -1e30)
        keys = block[:CHIP, :HD]
        values = with_ones(block[:CHIP, HD:])
        for h in range(after[0].shape[0]):
            s = lax.dot_general(queries(h), keys, CONTRACT, preferred_element_type=F32)
            s = s * SCALE + bias
            if i == 0:
                old, old_sum, old_acc = before(h)
            else:
                old, old_sum, old_acc = (ref[h] for ref in after)
            top = jnp.maximum(old, jnp.max(s, axis=1, keepdims=True))
            fade = jnp.exp2(old - top)
            w = jnp.exp2(s - jnp.concatenate([top, top], axis=1)).astype(BF16)
            got = jnp.dot(w, values, preferred_element_type=F32)
            after[0][h] = top
            after[1][h] = fade * old_sum + got[:, HD:]
            after[2][h] = fade * old_acc + got[:, :HD]


def parts(src):
    return [src[i * UNIT : (i + 1) * UNIT, :] for i in range(src.shape[0] // UNIT)]


def query_of(halves):
    per = halves[0].shape[0]
    return lambda h: halves[h // per][h % per]


def near_body(qa, qb, unit, r1, r2, m_s, l_s, acc):
    query = query_of((qa, qb))
    tags, q_tag = tags_of(unit)
    rows = lax.broadcasted_iota(jnp.int32, (CHIP, CHIP), 0)
    cols = lax.broadcasted_iota(jnp.int32, (CHIP, CHIP), 1)
    bias = jnp.where((tags[0:1, :] == q_tag) & (cols <= rows), 0.0, -1e30)
    keys, values = unit[:CHIP, :HD], with_ones(unit[:CHIP, HD:])
    for h in range(m_s.shape[0]):
        s = lax.dot_general(query(h), keys, CONTRACT, preferred_element_type=F32)
        s = s * SCALE + bias
        top = jnp.max(s, axis=1, keepdims=True)
        got = jnp.dot(jnp.exp2(s - top).astype(BF16), values, preferred_element_type=F32)
        m_s[h] = jnp.broadcast_to(top, (CHIP, HD))
        l_s[h] = got[:, HD:]
        acc[h] = got[:, :HD]
    state = (m_s, l_s, acc)
    units = [src[...] for src in (r1, r2)]
    add_units(query, units, NEAR, q_tag, lambda h: [ref[h] for ref in state], state)


def attend_near(qs, unit, r1, r2):
    heads = 2 * qs[0].shape[0]
    state = like(heads, CHIP, HD, dtype=F32)
    return call(
        near_body, "attend_near", (state, state, state), [VMEM] * 5, (VMEM,) * 3, limit=8,
        flops=12 * heads * CHIP * CHIP * HD, exps=3 * heads * CHIP * CHIP,
    )(*qs, unit, r1, r2)


def early_body(qa, qb, m_in, l_in, acc_in, unit, far_b, m_s, l_s, acc):
    before = (m_in, l_in, acc_in)
    add_units(
        query_of((qa, qb)), parts(far_b), EARLY, tags_of(unit)[1],
        lambda h: [ref[h] for ref in before], (m_s, l_s, acc),
    )


def attend_early(qs, m_in, l_in, acc_in, unit, far_b):
    heads = 2 * qs[0].shape[0]
    state = like(heads, CHIP, HD, dtype=F32)
    return call(
        early_body, "attend_early", (state,) * 3, [VMEM] * 7, (VMEM,) * 3, limit=8,
        flops=64 * heads * CHIP * CHIP * HD, exps=2 * heads * CHIP * CHIP,
    )(*qs, m_in, l_in, acc_in, unit, far_b)


def middle_body(qa, qb, m_in, l_in, acc_in, unit, r3, r4, far_c, m_s, l_s, acc):
    before = (m_in, l_in, acc_in)
    even = core_index() == 0
    third, fourth = parts(far_c)
    units = [jnp.where(even, r3[...], third), jnp.where(even, r4[...], fourth)]
    add_units(
        query_of((qa, qb)), units, MIDDLE, tags_of(unit)[1],
        lambda h: [ref[h] for ref in before], (m_s, l_s, acc),
    )


def attend_middle(qs, m_in, l_in, acc_in, unit, r3, r4, far_c):
    heads = 2 * qs[0].shape[0]
    state = like(heads, CHIP, HD, dtype=F32)
    return call(
        middle_body, "attend_middle", (state,) * 3, [VMEM] * 9, (VMEM,) * 3, limit=8,
        flops=8 * heads * CHIP * CHIP * HD, exps=2 * heads * CHIP * CHIP,
    )(*qs, m_in, l_in, acc_in, unit, r3, r4, far_c)


def attend_last(side, qs, m_in, l_in, acc_in, unit, far_a):
    heads = 2 * qs[0].shape[0]

    def body(qa, qb, m_in, l_in, acc_in, unit, far_a, out, tag_s, m_s, l_s, acc):
        rows = halves()[side]
        per = qa.shape[0]
        before = (m_in, l_in, acc_in)
        tag_s[...] = jnp.broadcast_to(tags_of(unit)[1], (CHIP, HD))
        add_units(
            lambda h: (qa, qb)[h // per][h % per, rows, :], parts(far_a), LAST, tag_s[rows, :][:, 0:1],
            lambda h: [ref[h, rows, :] for ref in before], (m_s, l_s, acc),
        )
        for h in range(heads):
            out[:, h * HD : (h + 1) * HD] = (acc[h] / l_s[h]).astype(BF16)

    state = pltpu.VMEM((heads, ROWS, HD), F32)
    return call(
        body, "attend_last", like(ROWS, heads * HD), [VMEM] * 7, VMEM,
        [pltpu.VMEM((CHIP, HD), F32), state, state, state],
        limit=8, flops=4 * heads * ROWS * 3 * CHIP * HD, exps=heads * ROWS * 3 * CHIP,
    )(*qs, m_in, l_in, acc_in, unit, far_a)


def project_out(xm, xr, w_out, groups, parts, dtype):
    depth = xm.shape[1]
    width = w_out.shape[1] // groups
    half = width // 2

    def body(xm, xr, w, *outs):
        core = core_index()
        own = pl.ds(pl.multiple_of(core * depth, depth), depth)
        other = pl.ds(pl.multiple_of((1 - core) * depth, depth), depth)
        for (shift, side), out in zip(parts, outs):
            group = lax.rem(lax.axis_index("head") + shift, groups)
            cols = pl.ds(pl.multiple_of(group * width + side * half, half), half)
            got = jnp.dot(xm[...], w[own, cols], preferred_element_type=F32)
            got += jnp.dot(xr[...], w[other, cols], preferred_element_type=F32)
            out[...] = got.astype(dtype)

    return call(
        body, "project_out", (like(ROWS, half, dtype=dtype),) * len(parts), [VMEM] * 3,
        (VMEM,) * len(parts), limit=4,
        flops=2 * ROWS * 2 * depth * half * len(parts), moved=len(parts),
    )(xm, xr, w_out)


def add_body(a, b, p, q, out_a, out_b):
    out_a[...] = (a[...] + p[...].astype(F32)).astype(BF16)
    out_b[...] = (b[...] + q[...].astype(F32)).astype(BF16)


def add_passing(a, b, p, q):
    out = like(*p.shape)
    return call(add_body, "add_passing", (out, out), [VMEM] * 4, (VMEM,) * 2, limit=2)(a, b, p, q)


def total_body(own_a, own_b, left_a, left_b, right_a, right_b, out):
    half = own_a.shape[1]
    for at, pieces in ((0, (own_a, left_a, right_a)), (half, (own_b, left_b, right_b))):
        total = pieces[0][...] + pieces[1][...].astype(F32) + pieces[2][...].astype(F32)
        out[:, at : at + half] = total.astype(BF16)


def add_total(*pieces):
    rows, half = pieces[0].shape
    return call(total_body, "add_total", like(rows, 2 * half), [VMEM] * 6, VMEM, limit=2)(*pieces)


def shards(tokens, w_query, w_key, w_value, w_out, doc_ids):
    ranks = lax.axis_size("ctx")
    groups = lax.axis_size("head")
    table = jnp.asarray(rope_table(ranks * ROWS))

    def swap(value):
        return lax.ppermute(value, "ctx", [(r, r ^ 1) for r in range(ranks)])

    def along(value, even, odd):
        moves = [(r, 2 * (odd if r % 2 else even)(r // 2) + r % 2) for r in range(ranks)]
        return lax.ppermute(value, "ctx", moves)

    def ahead(step):
        return lambda chip: (chip + step) % (ranks // 2)

    def in_row(step):
        return lambda chip: chip // 4 * 4 + (chip + step) % 4

    docs = doc_ids.reshape(1, -1)
    came, docs_came = swap(tokens), swap(docs)
    tokens, w_key, w_value, w_query, table, docs = (
        pltpu.with_memory_space_constraint(a, pltpu.HBM)
        for a in (tokens, w_key, w_value, w_query, table, docs)
    )
    half, tokens, w_kv, docs, table = project_own(tokens, w_key, w_value, docs, table)
    unit = project_unit(half, came, w_kv, docs, docs_came, table)
    r1 = along(unit, ahead(1), ahead(4))
    r2 = along(unit, ahead(2), ahead(8))
    r3 = along(unit, ahead(3), ahead(12))
    r4 = along(unit, ahead(4), in_row(3))
    qs = project_q(tokens, came, w_query, table, 0)
    r1, r2, came, qs = lax.optimization_barrier((r1, r2, came, qs))
    far_b = along(bundle_pair(unit, r1, r2, 2, unit), ahead(8), in_row(2))
    out_a = bundle_row(unit, r1, r2, r3, r4)
    far_a = along(out_a, ahead(4), in_row(1))
    far_c = along(bundle_pair(unit, r1, r2, 1, out_a), ahead(12), in_row(3))
    qs = (qs, project_q(tokens, came, w_query, table, 1))
    state = attend_near(qs, unit, r1, r2)
    state = attend_early(qs, *state, unit, far_b)
    state = attend_middle(qs, *state, unit, r3, r4, far_c)
    xr = swap(attend_last(1, qs, *state, unit, far_a))
    xm = attend_last(0, qs, *state, unit, far_a)

    def shift(value, step):
        return lax.ppermute(value, "head", [(g, (g + step) % groups) for g in range(groups)])

    a2, b2 = project_out(xm, xr, w_out, groups, ((2, 0), (2, 1)), BF16)
    pass_a, pass_b = shift(a2, 1), shift(b2, -1)
    b1, a3 = project_out(xm, xr, w_out, groups, ((1, 1), (3, 0)), BF16)
    left_b, right_a = shift(b1, 1), shift(a3, -1)
    a1, b3, a0, b0 = project_out(xm, xr, w_out, groups, ((1, 0), (3, 1), (0, 0), (0, 1)), F32)
    a1, b3 = add_passing(a1, b3, pass_a, pass_b)
    left_a, right_b = shift(a1, 1), shift(b3, -1)
    return add_total(a0, b0, left_a, left_b, right_a, right_b)


def solution(mesh):
    return jax.shard_map(
        shards,
        mesh=mesh,
        in_specs=(
            P("ctx", None),
            P(None, "head"),
            P(None, "head"),
            P(None, "head"),
            P("head", None),
            P("ctx"),
        ),
        out_specs=P("ctx", "head"),
        check_vma=False,
    )
```

```python
import math

import jax
import jax.numpy as jnp
import numpy as np
from jax import lax
from jax.experimental import pallas as pl
from jax.experimental.pallas import tpu as pltpu
from jax.sharding import PartitionSpec as P

HD = 128
ROWS = 128
UNIT = 264
F32 = jnp.float32
BF16 = jnp.bfloat16
MIB = 1 << 20
SCALE = math.log2(math.e) / math.sqrt(HD)


def rope_table(count):
    half = HD // 2
    freqs = 500000.0 ** (-2.0 * np.arange(half, dtype=np.float64) / HD)
    angles = np.arange(count, dtype=np.float64)[:, None] * freqs[None, :]
    return np.concatenate([np.cos(angles), np.sin(angles)], axis=1).astype(np.float32)


def rotation(table):
    half = HD // 2
    cosine, sine = table[:, :half], table[:, half:]
    cosine = jnp.concatenate([cosine, cosine], axis=1)
    sine = jnp.concatenate([-sine, sine], axis=1)
    return lambda t: t * cosine + pltpu.roll(t, half, 1) * sine


SMEM = pl.BlockSpec(memory_space=pltpu.SMEM)
VMEM = pl.BlockSpec(memory_space=pltpu.VMEM)
HBM = pl.BlockSpec(memory_space=pltpu.HBM)


def like(*dims, dtype=BF16):
    return jax.ShapeDtypeStruct(dims, dtype)


def call(body, name, out, ins, outs, scratch=(), limit=4, flops=0, moved=1, exps=0):
    return pl.pallas_call(
        body,
        out_shape=out,
        in_specs=ins,
        out_specs=outs,
        scratch_shapes=list(scratch),
        name=name,
        cost_estimate=pl.CostEstimate(
            flops=flops, bytes_accessed=moved * MIB, transcendentals=exps
        ),
        compiler_params=pltpu.CompilerParams(vmem_limit_bytes=limit * MIB),
    )


def core_index():
    return lax.rem(lax.axis_index("ctx"), 2)


def table_rows(table):
    return table.at[pl.ds(pl.multiple_of(lax.axis_index("ctx") * ROWS, ROWS), ROWS), :]


def started(copies):
    for copy in copies:
        copy.start()
    return copies


KV_PARTS = 4
CHIP = 2 * ROWS


def halves():
    core = core_index()
    own = pl.ds(pl.multiple_of(core * ROWS, ROWS), ROWS)
    other = pl.ds(pl.multiple_of((1 - core) * ROWS, ROWS), ROWS)
    return own, other


def own_body(tok, wk, wv, docs, table, half, tok_s, w_s, docs_s, table_s, acc, sems):
    part = tok.shape[1] // KV_PARTS
    cols = pl.ds(pl.multiple_of(core_index() * HD, HD), HD)
    copies = []
    for i in range(KV_PARTS):
        cut = pl.ds(i * part, part)
        copies.append(
            started([
                pltpu.make_async_copy(tok.at[:, cut], tok_s.at[:, cut], sems.at[3 * i]),
                pltpu.make_async_copy(
                    wk.at[cut, cols], w_s.at[cut, pl.ds(0, HD)], sems.at[3 * i + 1]
                ),
                pltpu.make_async_copy(
                    wv.at[cut, cols], w_s.at[cut, pl.ds(HD, HD)], sems.at[3 * i + 2]
                ),
            ])
        )
    first = pl.multiple_of(lax.div(lax.axis_index("ctx"), 2) * CHIP, CHIP)
    small = started([
        pltpu.make_async_copy(docs, docs_s, sems.at[3 * KV_PARTS]),
        pltpu.make_async_copy(table.at[pl.ds(first, CHIP), :], table_s, sems.at[3 * KV_PARTS + 1]),
    ])
    for i, group in enumerate(copies):
        for copy in group:
            copy.wait()
        cut = slice(i * part, (i + 1) * part)
        more = jnp.dot(tok_s[:, cut], w_s[cut, :], preferred_element_type=F32)
        if i == 0:
            acc[...] = more
        else:
            acc[...] += more
    for copy in small:
        copy.wait()
    rot = rotation(table_s[halves()[0], :])
    half[:, :HD] = rot(acc[:, :HD]).astype(BF16)
    half[:, HD:] = acc[:, HD:].astype(BF16)


def project_own(tokens, w_key, w_value, docs, table):
    depth = tokens.shape[1]
    return call(
        own_body, "project_own",
        (
            like(ROWS, 2 * HD),
            like(ROWS, depth),
            like(depth, 2 * HD),
            like(1, ROWS, dtype=jnp.int32),
            like(CHIP, HD, dtype=F32),
        ),
        [HBM] * 5, (VMEM,) * 5,
        [pltpu.VMEM((ROWS, 2 * HD), F32), pltpu.SemaphoreType.DMA((3 * KV_PARTS + 2,))],
        limit=6, flops=2 * ROWS * depth * 2 * HD, moved=3,
    )(tokens, w_key, w_value, docs, table)


def unit_body(half, came, w, docs, docs_came, table, unit):
    own, other = halves()
    got = jnp.dot(came[...], w[...], preferred_element_type=F32)
    unit[own, :] = half[...]
    unit[other, :HD] = rotation(table[other, :])(got[:, :HD]).astype(BF16)
    unit[other, HD:] = got[:, HD:].astype(BF16)
    first = core_index() == 0
    a, b = docs[...], docs_came[...]
    tags = jnp.concatenate([jnp.where(first, a, b), jnp.where(first, b, a)], axis=1)
    tags = (tags + 1).astype(F32)
    unit[CHIP:, :] = jnp.broadcast_to(tags, (8, CHIP)).astype(BF16)


def project_unit(half, came, w, docs, docs_came, table):
    return call(
        unit_body, "project_unit", like(UNIT, 2 * HD), [VMEM] * 6, VMEM, limit=2,
        flops=2 * ROWS * w.shape[0] * 2 * HD,
    )(half, came, w, docs, docs_came, table)


def q_body(tok, came, wq, table, out):
    half = wq.shape[1] // 2
    cols = pl.ds(pl.multiple_of(core_index() * half, half), half)
    for span, src in zip(halves(), (tok, came)):
        got = jnp.dot(src[...], wq[:, cols], preferred_element_type=F32)
        rot = rotation(table[span, :])
        for h in range(half // HD):
            out[h, span, :] = rot(got[:, h * HD : (h + 1) * HD]).astype(BF16)


def project_q(tokens, came, w_query, table):
    depth, width = w_query.shape
    return call(
        q_body, "project_q", like(width // 2 // HD, CHIP, HD), [VMEM] * 4, VMEM,
        limit=4, flops=2 * CHIP * depth * width // 2, moved=6,
    )(tokens, came, w_query, table)


NONE = 99
NEAR = ((1, 2), (4, 8))
EARLY = ((8, 9), (2, 6))
MIDDLE = ((3, 4), (3, 7))
LAST = ((5, 6, 7), (1, 5, 9))


def fill(out, slots, late, even):
    place = lax.axis_index("ctx")
    column = lax.rem(lax.div(place, 2), 4)
    skip = jnp.where(lax.rem(place, 2) == 0, even, jnp.where(column >= late, 1, 0))
    for i in range(out.shape[0] // UNIT):
        out[i * UNIT : (i + 1) * UNIT, :] = slots[skip + i]


def bundle_pair(unit, r1, r2, late, after):
    def body(unit, r1, r2, after, out, slots):
        for i, src in enumerate((unit, r1, r2)):
            slots[i] = src[...]
        fill(out, slots, late, 0)

    return call(
        body, "bundle_pair", like(2 * UNIT, 2 * HD), [VMEM] * 4, VMEM,
        [pltpu.VMEM((3, UNIT, 2 * HD), BF16)], limit=2,
    )(unit, r1, r2, after)


def row_body(unit, r1, r2, r3, after, out_a, slots):
    for i, src in enumerate((unit, r1, r2, r3)):
        slots[i] = src[...]
    fill(out_a, slots, 3, 1)


def bundle_row(unit, r1, r2, r3, after):
    return call(
        row_body, "bundle_row", like(3 * UNIT, 2 * HD), [VMEM] * 5, VMEM,
        [pltpu.VMEM((4, UNIT, 2 * HD), BF16)], limit=2,
    )(unit, r1, r2, r3, after)


CONTRACT = (((1,), (1,)), ((), ()))


def tags_of(unit):
    tags = unit[CHIP:UNIT, :].astype(F32)
    return tags, jnp.transpose(tags, (1, 0))[:, 0:1]


def with_ones(values):
    return jnp.concatenate([values, jnp.ones((CHIP, HD), BF16)], axis=1)


def add_units(queries, units, steps, q_tag, before, after):
    place = lax.axis_index("ctx")
    odd = lax.rem(place, 2) == 1
    chip = lax.div(place, 2)
    for i, (block, even_step, odd_step) in enumerate(zip(units, *steps)):
        valid = chip >= jnp.where(odd, odd_step, even_step)
        k_tag = block[CHIP:, :].astype(F32)[0:1, :]
        bias = jnp.where((k_tag == q_tag) & valid, 0.0, -1e30)
        keys = block[:CHIP, :HD]
        values = with_ones(block[:CHIP, HD:])
        for h in range(after[0].shape[0]):
            s = lax.dot_general(queries(h), keys, CONTRACT, preferred_element_type=F32)
            s = s * SCALE + bias
            if i == 0:
                old, old_sum, old_acc = before(h)
            else:
                old, old_sum, old_acc = (ref[h] for ref in after)
            top = jnp.maximum(old, jnp.max(s, axis=1, keepdims=True))
            fade = jnp.exp2(old - top)
            w = jnp.exp2(s - jnp.concatenate([top, top], axis=1)).astype(BF16)
            got = jnp.dot(w, values, preferred_element_type=F32)
            after[0][h] = top
            after[1][h] = fade * old_sum + got[:, HD:]
            after[2][h] = fade * old_acc + got[:, :HD]


def parts(src):
    return [src[i * UNIT : (i + 1) * UNIT, :] for i in range(src.shape[0] // UNIT)]


def near_body(qs, unit, r1, r2, m_s, l_s, acc):
    tags, q_tag = tags_of(unit)
    rows = lax.broadcasted_iota(jnp.int32, (CHIP, CHIP), 0)
    cols = lax.broadcasted_iota(jnp.int32, (CHIP, CHIP), 1)
    bias = jnp.where((tags[0:1, :] == q_tag) & (cols <= rows), 0.0, -1e30)
    keys, values = unit[:CHIP, :HD], with_ones(unit[:CHIP, HD:])
    for h in range(qs.shape[0]):
        s = lax.dot_general(qs[h], keys, CONTRACT, preferred_element_type=F32)
        s = s * SCALE + bias
        top = jnp.max(s, axis=1, keepdims=True)
        got = jnp.dot(jnp.exp2(s - top).astype(BF16), values, preferred_element_type=F32)
        m_s[h] = jnp.broadcast_to(top, (CHIP, HD))
        l_s[h] = got[:, HD:]
        acc[h] = got[:, :HD]
    state = (m_s, l_s, acc)
    units = [src[...] for src in (r1, r2)]
    add_units(lambda h: qs[h], units, NEAR, q_tag, lambda h: [ref[h] for ref in state], state)


def attend_near(qs, unit, r1, r2):
    heads = qs.shape[0]
    state = like(heads, CHIP, HD, dtype=F32)
    return call(
        near_body, "attend_near", (state, state, state), [VMEM] * 4, (VMEM,) * 3, limit=8,
        flops=12 * heads * CHIP * CHIP * HD, exps=3 * heads * CHIP * CHIP,
    )(qs, unit, r1, r2)


def early_body(qs, m_in, l_in, acc_in, unit, far_b, m_s, l_s, acc):
    before = (m_in, l_in, acc_in)
    add_units(
        lambda h: qs[h], parts(far_b), EARLY, tags_of(unit)[1],
        lambda h: [ref[h] for ref in before], (m_s, l_s, acc),
    )


def attend_early(qs, m_in, l_in, acc_in, unit, far_b):
    heads = qs.shape[0]
    state = like(heads, CHIP, HD, dtype=F32)
    return call(
        early_body, "attend_early", (state,) * 3, [VMEM] * 6, (VMEM,) * 3, limit=8,
        flops=64 * heads * CHIP * CHIP * HD, exps=2 * heads * CHIP * CHIP,
    )(qs, m_in, l_in, acc_in, unit, far_b)


def middle_body(qs, m_in, l_in, acc_in, unit, r3, r4, far_c, m_s, l_s, acc):
    before = (m_in, l_in, acc_in)
    even = core_index() == 0
    third, fourth = parts(far_c)
    units = [jnp.where(even, r3[...], third), jnp.where(even, r4[...], fourth)]
    add_units(
        lambda h: qs[h], units, MIDDLE, tags_of(unit)[1],
        lambda h: [ref[h] for ref in before], (m_s, l_s, acc),
    )


def attend_middle(qs, m_in, l_in, acc_in, unit, r3, r4, far_c):
    heads = qs.shape[0]
    state = like(heads, CHIP, HD, dtype=F32)
    return call(
        middle_body, "attend_middle", (state,) * 3, [VMEM] * 8, (VMEM,) * 3, limit=8,
        flops=8 * heads * CHIP * CHIP * HD, exps=2 * heads * CHIP * CHIP,
    )(qs, m_in, l_in, acc_in, unit, r3, r4, far_c)


def attend_last(side, qs, m_in, l_in, acc_in, unit, far_a):
    heads = qs.shape[0]

    def body(qs, m_in, l_in, acc_in, unit, far_a, out, tag_s, m_s, l_s, acc):
        rows = halves()[side]
        before = (m_in, l_in, acc_in)
        tag_s[...] = jnp.broadcast_to(tags_of(unit)[1], (CHIP, HD))
        add_units(
            lambda h: qs[h, rows, :], parts(far_a), LAST, tag_s[rows, :][:, 0:1],
            lambda h: [ref[h, rows, :] for ref in before], (m_s, l_s, acc),
        )
        for h in range(heads):
            out[:, h * HD : (h + 1) * HD] = (acc[h] / l_s[h]).astype(BF16)

    state = pltpu.VMEM((heads, ROWS, HD), F32)
    return call(
        body, "attend_last", like(ROWS, heads * HD), [VMEM] * 6, VMEM,
        [pltpu.VMEM((CHIP, HD), F32), state, state, state],
        limit=8, flops=4 * heads * ROWS * 3 * CHIP * HD, exps=heads * ROWS * 3 * CHIP,
    )(qs, m_in, l_in, acc_in, unit, far_a)


def project_out(xm, xr, w_out, groups, parts, dtype):
    depth = xm.shape[1]
    width = w_out.shape[1] // groups
    half = width // 2

    def body(xm, xr, w, *outs):
        core = core_index()
        own = pl.ds(pl.multiple_of(core * depth, depth), depth)
        other = pl.ds(pl.multiple_of((1 - core) * depth, depth), depth)
        for (shift, side), out in zip(parts, outs):
            group = lax.rem(lax.axis_index("head") + shift, groups)
            cols = pl.ds(pl.multiple_of(group * width + side * half, half), half)
            got = jnp.dot(xm[...], w[own, cols], preferred_element_type=F32)
            got += jnp.dot(xr[...], w[other, cols], preferred_element_type=F32)
            out[...] = got.astype(dtype)

    return call(
        body, "project_out", (like(ROWS, half, dtype=dtype),) * len(parts), [VMEM] * 3,
        (VMEM,) * len(parts), limit=4,
        flops=2 * ROWS * 2 * depth * half * len(parts), moved=len(parts),
    )(xm, xr, w_out)


def add_body(a, b, p, q, out_a, out_b):
    out_a[...] = (a[...] + p[...].astype(F32)).astype(BF16)
    out_b[...] = (b[...] + q[...].astype(F32)).astype(BF16)


def add_passing(a, b, p, q):
    out = like(*p.shape)
    return call(add_body, "add_passing", (out, out), [VMEM] * 4, (VMEM,) * 2, limit=2)(a, b, p, q)


def total_body(own_a, own_b, left_a, left_b, right_a, right_b, out):
    half = own_a.shape[1]
    for at, pieces in ((0, (own_a, left_a, right_a)), (half, (own_b, left_b, right_b))):
        total = pieces[0][...] + pieces[1][...].astype(F32) + pieces[2][...].astype(F32)
        out[:, at : at + half] = total.astype(BF16)


def add_total(*pieces):
    rows, half = pieces[0].shape
    return call(total_body, "add_total", like(rows, 2 * half), [VMEM] * 6, VMEM, limit=2)(*pieces)


def shards(tokens, w_query, w_key, w_value, w_out, doc_ids):
    ranks = lax.axis_size("ctx")
    groups = lax.axis_size("head")
    table = jnp.asarray(rope_table(ranks * ROWS))

    def swap(value):
        return lax.ppermute(value, "ctx", [(r, r ^ 1) for r in range(ranks)])

    def along(value, even, odd):
        moves = [(r, 2 * (odd if r % 2 else even)(r // 2) + r % 2) for r in range(ranks)]
        return lax.ppermute(value, "ctx", moves)

    def ahead(step):
        return lambda chip: (chip + step) % (ranks // 2)

    def in_row(step):
        return lambda chip: chip // 4 * 4 + (chip + step) % 4

    docs = doc_ids.reshape(1, -1)
    came, docs_came = swap(tokens), swap(docs)
    tokens, w_key, w_value, table, docs = (
        pltpu.with_memory_space_constraint(a, pltpu.HBM)
        for a in (tokens, w_key, w_value, table, docs)
    )
    half, tokens, w_kv, docs, table = project_own(tokens, w_key, w_value, docs, table)
    unit = project_unit(half, came, w_kv, docs, docs_came, table)
    r1 = along(unit, ahead(1), ahead(4))
    r2 = along(unit, ahead(2), ahead(8))
    r3 = along(unit, ahead(3), ahead(12))
    r4 = along(unit, ahead(4), in_row(3))
    r1, r2, came = lax.optimization_barrier((r1, r2, came))
    far_b = along(bundle_pair(unit, r1, r2, 2, unit), ahead(8), in_row(2))
    out_a = bundle_row(unit, r1, r2, r3, r4)
    far_a = along(out_a, ahead(4), in_row(1))
    far_c = along(bundle_pair(unit, r1, r2, 1, out_a), ahead(12), in_row(3))
    qs = project_q(tokens, came, w_query, table)
    state = attend_near(qs, unit, r1, r2)
    state = attend_early(qs, *state, unit, far_b)
    state = attend_middle(qs, *state, unit, r3, r4, far_c)
    xr = swap(attend_last(1, qs, *state, unit, far_a))
    xm = attend_last(0, qs, *state, unit, far_a)

    def shift(value, step):
        return lax.ppermute(value, "head", [(g, (g + step) % groups) for g in range(groups)])

    a2, b2 = project_out(xm, xr, w_out, groups, ((2, 0), (2, 1)), BF16)
    pass_a, pass_b = shift(a2, 1), shift(b2, -1)
    b1, a3 = project_out(xm, xr, w_out, groups, ((1, 1), (3, 0)), BF16)
    left_b, right_a = shift(b1, 1), shift(a3, -1)
    a1, b3, a0, b0 = project_out(xm, xr, w_out, groups, ((1, 0), (3, 1), (0, 0), (0, 1)), F32)
    a1, b3 = add_passing(a1, b3, pass_a, pass_b)
    left_a, right_b = shift(a1, 1), shift(b3, -1)
    return add_total(a0, b0, left_a, left_b, right_a, right_b)


def solution(mesh):
    return jax.shard_map(
        shards,
        mesh=mesh,
        in_specs=(
            P("ctx", None),
            P(None, "head"),
            P(None, "head"),
            P(None, "head"),
            P("head", None),
            P("ctx"),
        ),
        out_specs=P("ctx", "head"),
        check_vma=False,
    )
```

```python
import math

import jax
import jax.numpy as jnp
import numpy as np
from jax import lax
from jax.experimental import pallas as pl
from jax.experimental.pallas import tpu as pltpu
from jax.sharding import PartitionSpec as P

HD = 128
ROWS = 128
UNIT = 264
F32 = jnp.float32
BF16 = jnp.bfloat16
MIB = 1 << 20
SCALE = math.log2(math.e) / math.sqrt(HD)


def rope_table(count):
    half = HD // 2
    freqs = 500000.0 ** (-2.0 * np.arange(half, dtype=np.float64) / HD)
    angles = np.arange(count, dtype=np.float64)[:, None] * freqs[None, :]
    return np.concatenate([np.cos(angles), np.sin(angles)], axis=1).astype(np.float32)


def rotation(table):
    half = HD // 2
    cosine, sine = table[:, :half], table[:, half:]
    cosine = jnp.concatenate([cosine, cosine], axis=1)
    sine = jnp.concatenate([-sine, sine], axis=1)
    return lambda t: t * cosine + pltpu.roll(t, half, 1) * sine


SMEM = pl.BlockSpec(memory_space=pltpu.SMEM)
VMEM = pl.BlockSpec(memory_space=pltpu.VMEM)
HBM = pl.BlockSpec(memory_space=pltpu.HBM)


def like(*dims, dtype=BF16):
    return jax.ShapeDtypeStruct(dims, dtype)


def call(body, name, out, ins, outs, scratch=(), limit=4, flops=0, moved=1, exps=0):
    return pl.pallas_call(
        body,
        out_shape=out,
        in_specs=ins,
        out_specs=outs,
        scratch_shapes=list(scratch),
        name=name,
        cost_estimate=pl.CostEstimate(
            flops=flops, bytes_accessed=moved * MIB, transcendentals=exps
        ),
        compiler_params=pltpu.CompilerParams(vmem_limit_bytes=limit * MIB),
    )


def core_index():
    return lax.rem(lax.axis_index("ctx"), 2)


def table_rows(table):
    return table.at[pl.ds(pl.multiple_of(lax.axis_index("ctx") * ROWS, ROWS), ROWS), :]


def started(copies):
    for copy in copies:
        copy.start()
    return copies


KV_PARTS = 4
CHIP = 2 * ROWS


def halves():
    core = core_index()
    own = pl.ds(pl.multiple_of(core * ROWS, ROWS), ROWS)
    other = pl.ds(pl.multiple_of((1 - core) * ROWS, ROWS), ROWS)
    return own, other


def own_body(tok, wk, wv, docs, table, half, tok_s, w_s, docs_s, table_s, acc, sems):
    part = tok.shape[1] // KV_PARTS
    cols = pl.ds(pl.multiple_of(core_index() * HD, HD), HD)
    copies = []
    for i in range(KV_PARTS):
        cut = pl.ds(i * part, part)
        copies.append(
            started([
                pltpu.make_async_copy(tok.at[:, cut], tok_s.at[:, cut], sems.at[3 * i]),
                pltpu.make_async_copy(
                    wk.at[cut, cols], w_s.at[cut, pl.ds(0, HD)], sems.at[3 * i + 1]
                ),
                pltpu.make_async_copy(
                    wv.at[cut, cols], w_s.at[cut, pl.ds(HD, HD)], sems.at[3 * i + 2]
                ),
            ])
        )
    first = pl.multiple_of(lax.div(lax.axis_index("ctx"), 2) * CHIP, CHIP)
    small = started([
        pltpu.make_async_copy(docs, docs_s, sems.at[3 * KV_PARTS]),
        pltpu.make_async_copy(table.at[pl.ds(first, CHIP), :], table_s, sems.at[3 * KV_PARTS + 1]),
    ])
    for i, group in enumerate(copies):
        for copy in group:
            copy.wait()
        cut = slice(i * part, (i + 1) * part)
        more = jnp.dot(tok_s[:, cut], w_s[cut, :], preferred_element_type=F32)
        if i == 0:
            acc[...] = more
        else:
            acc[...] += more
    for copy in small:
        copy.wait()
    rot = rotation(table_s[halves()[0], :])
    half[:, :HD] = rot(acc[:, :HD]).astype(BF16)
    half[:, HD:] = acc[:, HD:].astype(BF16)


def project_own(tokens, w_key, w_value, docs, table):
    depth = tokens.shape[1]
    return call(
        own_body, "project_own",
        (
            like(ROWS, 2 * HD),
            like(ROWS, depth),
            like(depth, 2 * HD),
            like(1, ROWS, dtype=jnp.int32),
            like(CHIP, HD, dtype=F32),
        ),
        [HBM] * 5, (VMEM,) * 5,
        [pltpu.VMEM((ROWS, 2 * HD), F32), pltpu.SemaphoreType.DMA((3 * KV_PARTS + 2,))],
        limit=6, flops=2 * ROWS * depth * 2 * HD, moved=3,
    )(tokens, w_key, w_value, docs, table)


def unit_body(half, came, w, docs, docs_came, table, unit):
    own, other = halves()
    got = jnp.dot(came[...], w[...], preferred_element_type=F32)
    unit[own, :] = half[...]
    unit[other, :HD] = rotation(table[other, :])(got[:, :HD]).astype(BF16)
    unit[other, HD:] = got[:, HD:].astype(BF16)
    first = core_index() == 0
    a, b = docs[...], docs_came[...]
    tags = jnp.concatenate([jnp.where(first, a, b), jnp.where(first, b, a)], axis=1)
    tags = (tags + 1).astype(F32)
    unit[CHIP:, :] = jnp.broadcast_to(tags, (8, CHIP)).astype(BF16)


def project_unit(half, came, w, docs, docs_came, table):
    return call(
        unit_body, "project_unit", like(UNIT, 2 * HD), [VMEM] * 6, VMEM, limit=2,
        flops=2 * ROWS * w.shape[0] * 2 * HD,
    )(half, came, w, docs, docs_came, table)


def q_body(tok, came, wq, table, out):
    half = wq.shape[1] // 2
    cols = pl.ds(pl.multiple_of(core_index() * half, half), half)
    for span, src in zip(halves(), (tok, came)):
        got = jnp.dot(src[...], wq[:, cols], preferred_element_type=F32)
        rot = rotation(table[span, :])
        for h in range(half // HD):
            out[h, span, :] = rot(got[:, h * HD : (h + 1) * HD]).astype(BF16)


def project_q(tokens, came, w_query, table):
    depth, width = w_query.shape
    return call(
        q_body, "project_q", like(width // 2 // HD, CHIP, HD), [VMEM] * 4, VMEM,
        limit=4, flops=2 * CHIP * depth * width // 2, moved=6,
    )(tokens, came, w_query, table)


NONE = 99
NEAR = ((1, 2), (4, 8))
EARLY = ((8, 9), (2, 6))
MIDDLE = ((3, 4), (3, 7))
LAST = ((5, 6, 7), (1, 5, 9))


def fill(out, slots, late, even):
    place = lax.axis_index("ctx")
    column = lax.rem(lax.div(place, 2), 4)
    skip = jnp.where(lax.rem(place, 2) == 0, even, jnp.where(column >= late, 1, 0))
    for i in range(out.shape[0] // UNIT):
        out[i * UNIT : (i + 1) * UNIT, :] = slots[skip + i]


def bundle_pair(unit, r1, r2, late, after):
    def body(unit, r1, r2, after, out, slots):
        for i, src in enumerate((unit, r1, r2)):
            slots[i] = src[...]
        fill(out, slots, late, 0)

    return call(
        body, "bundle_pair", like(2 * UNIT, 2 * HD), [VMEM] * 4, VMEM,
        [pltpu.VMEM((3, UNIT, 2 * HD), BF16)], limit=2,
    )(unit, r1, r2, after)


def row_body(unit, r1, r2, r3, after, out_a, slots):
    for i, src in enumerate((unit, r1, r2, r3)):
        slots[i] = src[...]
    fill(out_a, slots, 3, 1)


def bundle_row(unit, r1, r2, r3, after):
    return call(
        row_body, "bundle_row", like(3 * UNIT, 2 * HD), [VMEM] * 5, VMEM,
        [pltpu.VMEM((4, UNIT, 2 * HD), BF16)], limit=2,
    )(unit, r1, r2, r3, after)


CONTRACT = (((1,), (1,)), ((), ()))


def tags_of(unit):
    tags = unit[CHIP:UNIT, :].astype(F32)
    return tags, jnp.transpose(tags, (1, 0))[:, 0:1]


def with_ones(values):
    return jnp.concatenate([values, jnp.ones((CHIP, HD), BF16)], axis=1)


def add_units(queries, units, steps, q_tag, before, after):
    place = lax.axis_index("ctx")
    odd = lax.rem(place, 2) == 1
    chip = lax.div(place, 2)
    for i, (block, even_step, odd_step) in enumerate(zip(units, *steps)):
        valid = chip >= jnp.where(odd, odd_step, even_step)
        k_tag = block[CHIP:, :].astype(F32)[0:1, :]
        bias = jnp.where((k_tag == q_tag) & valid, 0.0, -1e30)
        keys = block[:CHIP, :HD]
        values = with_ones(block[:CHIP, HD:])
        for h in range(after[0].shape[0]):
            s = lax.dot_general(queries(h), keys, CONTRACT, preferred_element_type=F32)
            s = s * SCALE + bias
            if i == 0:
                old, old_sum, old_acc = before(h)
            else:
                old, old_sum, old_acc = (ref[h] for ref in after)
            top = jnp.maximum(old, jnp.max(s, axis=1, keepdims=True))
            fade = jnp.exp2(old - top)
            w = jnp.exp2(s - jnp.concatenate([top, top], axis=1)).astype(BF16)
            got = jnp.dot(w, values, preferred_element_type=F32)
            after[0][h] = top
            after[1][h] = fade * old_sum + got[:, HD:]
            after[2][h] = fade * old_acc + got[:, :HD]


def parts(src):
    return [src[i * UNIT : (i + 1) * UNIT, :] for i in range(src.shape[0] // UNIT)]


def near_body(qs, unit, r1, r2, m_s, l_s, acc):
    tags, q_tag = tags_of(unit)
    rows = lax.broadcasted_iota(jnp.int32, (CHIP, CHIP), 0)
    cols = lax.broadcasted_iota(jnp.int32, (CHIP, CHIP), 1)
    bias = jnp.where((tags[0:1, :] == q_tag) & (cols <= rows), 0.0, -1e30)
    keys, values = unit[:CHIP, :HD], with_ones(unit[:CHIP, HD:])
    for h in range(qs.shape[0]):
        s = lax.dot_general(qs[h], keys, CONTRACT, preferred_element_type=F32)
        s = s * SCALE + bias
        top = jnp.max(s, axis=1, keepdims=True)
        got = jnp.dot(jnp.exp2(s - top).astype(BF16), values, preferred_element_type=F32)
        m_s[h] = jnp.broadcast_to(top, (CHIP, HD))
        l_s[h] = got[:, HD:]
        acc[h] = got[:, :HD]
    state = (m_s, l_s, acc)
    units = [src[...] for src in (r1, r2)]
    add_units(lambda h: qs[h], units, NEAR, q_tag, lambda h: [ref[h] for ref in state], state)


def attend_near(qs, unit, r1, r2):
    heads = qs.shape[0]
    state = like(heads, CHIP, HD, dtype=F32)
    return call(
        near_body, "attend_near", (state, state, state), [VMEM] * 4, (VMEM,) * 3, limit=8,
        flops=12 * heads * CHIP * CHIP * HD, exps=3 * heads * CHIP * CHIP,
    )(qs, unit, r1, r2)


def early_body(qs, m_in, l_in, acc_in, unit, far_b, m_s, l_s, acc):
    before = (m_in, l_in, acc_in)
    add_units(
        lambda h: qs[h], parts(far_b), EARLY, tags_of(unit)[1],
        lambda h: [ref[h] for ref in before], (m_s, l_s, acc),
    )


def attend_early(qs, m_in, l_in, acc_in, unit, far_b):
    heads = qs.shape[0]
    state = like(heads, CHIP, HD, dtype=F32)
    return call(
        early_body, "attend_early", (state,) * 3, [VMEM] * 6, (VMEM,) * 3, limit=8,
        flops=64 * heads * CHIP * CHIP * HD, exps=2 * heads * CHIP * CHIP,
    )(qs, m_in, l_in, acc_in, unit, far_b)


def middle_body(qs, m_in, l_in, acc_in, unit, r3, r4, far_c, m_s, l_s, acc):
    before = (m_in, l_in, acc_in)
    even = core_index() == 0
    third, fourth = parts(far_c)
    units = [jnp.where(even, r3[...], third), jnp.where(even, r4[...], fourth)]
    add_units(
        lambda h: qs[h], units, MIDDLE, tags_of(unit)[1],
        lambda h: [ref[h] for ref in before], (m_s, l_s, acc),
    )


def attend_middle(qs, m_in, l_in, acc_in, unit, r3, r4, far_c):
    heads = qs.shape[0]
    state = like(heads, CHIP, HD, dtype=F32)
    return call(
        middle_body, "attend_middle", (state,) * 3, [VMEM] * 8, (VMEM,) * 3, limit=8,
        flops=8 * heads * CHIP * CHIP * HD, exps=2 * heads * CHIP * CHIP,
    )(qs, m_in, l_in, acc_in, unit, r3, r4, far_c)


def attend_last(side, qs, m_in, l_in, acc_in, unit, far_a):
    heads = qs.shape[0]

    def body(qs, m_in, l_in, acc_in, unit, far_a, out, tag_s, m_s, l_s, acc):
        rows = halves()[side]
        before = (m_in, l_in, acc_in)
        tag_s[...] = jnp.broadcast_to(tags_of(unit)[1], (CHIP, HD))
        add_units(
            lambda h: qs[h, rows, :], parts(far_a), LAST, tag_s[rows, :][:, 0:1],
            lambda h: [ref[h, rows, :] for ref in before], (m_s, l_s, acc),
        )
        for h in range(heads):
            out[:, h * HD : (h + 1) * HD] = (acc[h] / l_s[h]).astype(BF16)

    state = pltpu.VMEM((heads, ROWS, HD), F32)
    return call(
        body, "attend_last", like(ROWS, heads * HD), [VMEM] * 6, VMEM,
        [pltpu.VMEM((CHIP, HD), F32), state, state, state],
        limit=8, flops=4 * heads * ROWS * 3 * CHIP * HD, exps=heads * ROWS * 3 * CHIP,
    )(qs, m_in, l_in, acc_in, unit, far_a)


def project_out(xm, xr, w_out, groups, parts, dtype):
    depth = xm.shape[1]
    width = w_out.shape[1] // groups
    half = width // 2

    def body(xm, xr, w, *outs):
        core = core_index()
        own = pl.ds(pl.multiple_of(core * depth, depth), depth)
        other = pl.ds(pl.multiple_of((1 - core) * depth, depth), depth)
        for (shift, side), out in zip(parts, outs):
            group = lax.rem(lax.axis_index("head") + shift, groups)
            cols = pl.ds(pl.multiple_of(group * width + side * half, half), half)
            got = jnp.dot(xm[...], w[own, cols], preferred_element_type=F32)
            got += jnp.dot(xr[...], w[other, cols], preferred_element_type=F32)
            out[...] = got.astype(dtype)

    return call(
        body, "project_out", (like(ROWS, half, dtype=dtype),) * len(parts), [VMEM] * 3,
        (VMEM,) * len(parts), limit=4,
        flops=2 * ROWS * 2 * depth * half * len(parts), moved=len(parts),
    )(xm, xr, w_out)


def add_body(a, b, p, q, out_a, out_b):
    out_a[...] = (a[...] + p[...].astype(F32)).astype(BF16)
    out_b[...] = (b[...] + q[...].astype(F32)).astype(BF16)


def add_passing(a, b, p, q):
    out = like(*p.shape)
    return call(add_body, "add_passing", (out, out), [VMEM] * 4, (VMEM,) * 2, limit=2)(a, b, p, q)


def total_body(own_a, own_b, left_a, left_b, right_a, right_b, out):
    half = own_a.shape[1]
    for at, pieces in ((0, (own_a, left_a, right_a)), (half, (own_b, left_b, right_b))):
        total = pieces[0][...] + pieces[1][...].astype(F32) + pieces[2][...].astype(F32)
        out[:, at : at + half] = total.astype(BF16)


def add_total(*pieces):
    rows, half = pieces[0].shape
    return call(total_body, "add_total", like(rows, 2 * half), [VMEM] * 6, VMEM, limit=2)(*pieces)


def shards(tokens, w_query, w_key, w_value, w_out, doc_ids):
    ranks = lax.axis_size("ctx")
    groups = lax.axis_size("head")
    table = jnp.asarray(rope_table(ranks * ROWS))

    def swap(value):
        return lax.ppermute(value, "ctx", [(r, r ^ 1) for r in range(ranks)])

    def along(value, even, odd):
        moves = []
        for r in range(ranks):
            step = odd if r % 2 else even
            if step is not None:
                moves.append((r, 2 * step(r // 2) + r % 2))
        return lax.ppermute(value, "ctx", moves)

    def ahead(step):
        return lambda chip: (chip + step) % (ranks // 2)

    def in_row(step):
        return lambda chip: chip // 4 * 4 + (chip + step) % 4

    docs = doc_ids.reshape(1, -1)
    came, docs_came = swap(tokens), swap(docs)
    tokens, w_key, w_value, table, docs = (
        pltpu.with_memory_space_constraint(a, pltpu.HBM)
        for a in (tokens, w_key, w_value, table, docs)
    )
    half, tokens, w_kv, docs, table = project_own(tokens, w_key, w_value, docs, table)
    unit = project_unit(half, came, w_kv, docs, docs_came, table)
    r1 = along(unit, ahead(1), ahead(4))
    r2 = along(unit, ahead(2), ahead(8))
    r3 = along(unit, ahead(3), ahead(12))
    r4 = along(unit, ahead(4), in_row(3))
    r1, r2, came = lax.optimization_barrier((r1, r2, came))
    far_b = along(bundle_pair(unit, r1, r2, 2, unit), ahead(8), in_row(2))
    out_a = bundle_row(unit, r1, r2, r3, r4)
    far_a = along(out_a, ahead(4), in_row(1))
    far_c = along(bundle_pair(unit, r1, r2, 1, out_a), None, in_row(3))
    qs = project_q(tokens, came, w_query, table)
    state = attend_near(qs, unit, r1, r2)
    state = attend_early(qs, *state, unit, far_b)
    state = attend_middle(qs, *state, unit, r3, r4, far_c)
    xr = swap(attend_last(1, qs, *state, unit, far_a))
    xm = attend_last(0, qs, *state, unit, far_a)

    def shift(value, step):
        return lax.ppermute(value, "head", [(g, (g + step) % groups) for g in range(groups)])

    a2, b2 = project_out(xm, xr, w_out, groups, ((2, 0), (2, 1)), BF16)
    pass_a, pass_b = shift(a2, 1), shift(b2, -1)
    b1, a3 = project_out(xm, xr, w_out, groups, ((1, 1), (3, 0)), BF16)
    left_b, right_a = shift(b1, 1), shift(a3, -1)
    a1, b3, a0, b0 = project_out(xm, xr, w_out, groups, ((1, 0), (3, 1), (0, 0), (0, 1)), F32)
    a1, b3 = add_passing(a1, b3, pass_a, pass_b)
    left_a, right_b = shift(a1, 1), shift(b3, -1)
    return add_total(a0, b0, left_a, left_b, right_a, right_b)


def solution(mesh):
    return jax.shard_map(
        shards,
        mesh=mesh,
        in_specs=(
            P("ctx", None),
            P(None, "head"),
            P(None, "head"),
            P(None, "head"),
            P("head", None),
            P("ctx"),
        ),
        out_specs=P("ctx", "head"),
        check_vma=False,
    )
```

```python
import math

import jax
import jax.numpy as jnp
import numpy as np
from jax import lax
from jax.experimental import pallas as pl
from jax.experimental.pallas import tpu as pltpu
from jax.sharding import PartitionSpec as P

HD = 128
ROWS = 128
UNIT = 264
F32 = jnp.float32
BF16 = jnp.bfloat16
MIB = 1 << 20
SCALE = math.log2(math.e) / math.sqrt(HD)


def rope_table(count):
    half = HD // 2
    freqs = 500000.0 ** (-2.0 * np.arange(half, dtype=np.float64) / HD)
    angles = np.arange(count, dtype=np.float64)[:, None] * freqs[None, :]
    return np.concatenate([np.cos(angles), np.sin(angles)], axis=1).astype(np.float32)


def rotation(table):
    half = HD // 2
    cosine, sine = table[:, :half], table[:, half:]
    cosine = jnp.concatenate([cosine, cosine], axis=1)
    sine = jnp.concatenate([-sine, sine], axis=1)
    return lambda t: t * cosine + pltpu.roll(t, half, 1) * sine


SMEM = pl.BlockSpec(memory_space=pltpu.SMEM)
VMEM = pl.BlockSpec(memory_space=pltpu.VMEM)
HBM = pl.BlockSpec(memory_space=pltpu.HBM)


def like(*dims, dtype=BF16):
    return jax.ShapeDtypeStruct(dims, dtype)


def call(body, name, out, ins, outs, scratch=(), limit=4, flops=0, moved=1, exps=0):
    return pl.pallas_call(
        body,
        out_shape=out,
        in_specs=ins,
        out_specs=outs,
        scratch_shapes=list(scratch),
        name=name,
        cost_estimate=pl.CostEstimate(
            flops=flops, bytes_accessed=moved * MIB, transcendentals=exps
        ),
        compiler_params=pltpu.CompilerParams(vmem_limit_bytes=limit * MIB),
    )


def core_index():
    return lax.rem(lax.axis_index("ctx"), 2)


def table_rows(table):
    return table.at[pl.ds(pl.multiple_of(lax.axis_index("ctx") * ROWS, ROWS), ROWS), :]


def started(copies):
    for copy in copies:
        copy.start()
    return copies


KV_PARTS = 4
CHIP = 2 * ROWS


def halves():
    core = core_index()
    own = pl.ds(pl.multiple_of(core * ROWS, ROWS), ROWS)
    other = pl.ds(pl.multiple_of((1 - core) * ROWS, ROWS), ROWS)
    return own, other


def own_body(tok, wk, wv, docs, table, half, tok_s, w_s, docs_s, table_s, acc, sems):
    part = tok.shape[1] // KV_PARTS
    cols = pl.ds(pl.multiple_of(core_index() * HD, HD), HD)
    copies = []
    for i in range(KV_PARTS):
        cut = pl.ds(i * part, part)
        copies.append(
            started([
                pltpu.make_async_copy(tok.at[:, cut], tok_s.at[:, cut], sems.at[3 * i]),
                pltpu.make_async_copy(
                    wk.at[cut, cols], w_s.at[cut, pl.ds(0, HD)], sems.at[3 * i + 1]
                ),
                pltpu.make_async_copy(
                    wv.at[cut, cols], w_s.at[cut, pl.ds(HD, HD)], sems.at[3 * i + 2]
                ),
            ])
        )
    first = pl.multiple_of(lax.div(lax.axis_index("ctx"), 2) * CHIP, CHIP)
    small = started([
        pltpu.make_async_copy(docs, docs_s, sems.at[3 * KV_PARTS]),
        pltpu.make_async_copy(table.at[pl.ds(first, CHIP), :], table_s, sems.at[3 * KV_PARTS + 1]),
    ])
    for i, group in enumerate(copies):
        for copy in group:
            copy.wait()
        cut = slice(i * part, (i + 1) * part)
        more = jnp.dot(tok_s[:, cut], w_s[cut, :], preferred_element_type=F32)
        if i == 0:
            acc[...] = more
        else:
            acc[...] += more
    for copy in small:
        copy.wait()
    rot = rotation(table_s[halves()[0], :])
    half[:, :HD] = rot(acc[:, :HD]).astype(BF16)
    half[:, HD:] = acc[:, HD:].astype(BF16)


def project_own(tokens, w_key, w_value, docs, table):
    depth = tokens.shape[1]
    return call(
        own_body, "project_own",
        (
            like(ROWS, 2 * HD),
            like(ROWS, depth),
            like(depth, 2 * HD),
            like(1, ROWS, dtype=jnp.int32),
            like(CHIP, HD, dtype=F32),
        ),
        [HBM] * 5, (VMEM,) * 5,
        [pltpu.VMEM((ROWS, 2 * HD), F32), pltpu.SemaphoreType.DMA((3 * KV_PARTS + 2,))],
        limit=6, flops=2 * ROWS * depth * 2 * HD, moved=3,
    )(tokens, w_key, w_value, docs, table)


def unit_body(half, came, w, docs, docs_came, table, unit):
    own, other = halves()
    got = jnp.dot(came[...], w[...], preferred_element_type=F32)
    unit[own, :] = half[...]
    unit[other, :HD] = rotation(table[other, :])(got[:, :HD]).astype(BF16)
    unit[other, HD:] = got[:, HD:].astype(BF16)
    first = core_index() == 0
    a, b = docs[...], docs_came[...]
    tags = jnp.concatenate([jnp.where(first, a, b), jnp.where(first, b, a)], axis=1)
    tags = (tags + 1).astype(F32)
    unit[CHIP:, :] = jnp.broadcast_to(tags, (8, CHIP)).astype(BF16)


def project_unit(half, came, w, docs, docs_came, table):
    return call(
        unit_body, "project_unit", like(UNIT, 2 * HD), [VMEM] * 6, VMEM, limit=2,
        flops=2 * ROWS * w.shape[0] * 2 * HD,
    )(half, came, w, docs, docs_came, table)


def q_body(tok, came, wq, table, out):
    half = wq.shape[1] // 2
    cols = pl.ds(pl.multiple_of(core_index() * half, half), half)
    for span, src in zip(halves(), (tok, came)):
        got = jnp.dot(src[...], wq[:, cols], preferred_element_type=F32)
        rot = rotation(table[span, :])
        for h in range(half // HD):
            out[h, span, :] = rot(got[:, h * HD : (h + 1) * HD]).astype(BF16)


def project_q(tokens, came, w_query, table):
    depth, width = w_query.shape
    return call(
        q_body, "project_q", like(width // 2 // HD, CHIP, HD), [VMEM] * 4, VMEM,
        limit=4, flops=2 * CHIP * depth * width // 2, moved=6,
    )(tokens, came, w_query, table)


NONE = 99
NEAR = ((1, 2), (4, 8))
EARLY = ((5, 6, 7), (1, 5, 9))
MIDDLE = ((3, 4), (3, 7))
LAST = ((8, 9), (2, 6))


def fill(out, slots, late, even):
    place = lax.axis_index("ctx")
    column = lax.rem(lax.div(place, 2), 4)
    skip = jnp.where(lax.rem(place, 2) == 0, even, jnp.where(column >= late, 1, 0))
    for i in range(out.shape[0] // UNIT):
        out[i * UNIT : (i + 1) * UNIT, :] = slots[skip + i]


def bundle_pair(unit, r1, r2, late, after):
    def body(unit, r1, r2, after, out, slots):
        for i, src in enumerate((unit, r1, r2)):
            slots[i] = src[...]
        fill(out, slots, late, 0)

    return call(
        body, "bundle_pair", like(2 * UNIT, 2 * HD), [VMEM] * 4, VMEM,
        [pltpu.VMEM((3, UNIT, 2 * HD), BF16)], limit=2,
    )(unit, r1, r2, after)


def row_body(unit, r1, r2, r3, after, out_a, slots):
    for i, src in enumerate((unit, r1, r2, r3)):
        slots[i] = src[...]
    fill(out_a, slots, 3, 1)


def bundle_row(unit, r1, r2, r3, after):
    return call(
        row_body, "bundle_row", like(3 * UNIT, 2 * HD), [VMEM] * 5, VMEM,
        [pltpu.VMEM((4, UNIT, 2 * HD), BF16)], limit=2,
    )(unit, r1, r2, r3, after)


CONTRACT = (((1,), (1,)), ((), ()))


def tags_of(unit):
    tags = unit[CHIP:UNIT, :].astype(F32)
    return tags, jnp.transpose(tags, (1, 0))[:, 0:1]


def with_ones(values):
    return jnp.concatenate([values, jnp.ones((CHIP, HD), BF16)], axis=1)


def add_units(queries, units, steps, q_tag, before, after):
    place = lax.axis_index("ctx")
    odd = lax.rem(place, 2) == 1
    chip = lax.div(place, 2)
    for i, (block, even_step, odd_step) in enumerate(zip(units, *steps)):
        valid = chip >= jnp.where(odd, odd_step, even_step)
        k_tag = block[CHIP:, :].astype(F32)[0:1, :]
        bias = jnp.where((k_tag == q_tag) & valid, 0.0, -1e30)
        keys = block[:CHIP, :HD]
        values = with_ones(block[:CHIP, HD:])
        for h in range(after[0].shape[0]):
            s = lax.dot_general(queries(h), keys, CONTRACT, preferred_element_type=F32)
            s = s * SCALE + bias
            if i == 0:
                old, old_sum, old_acc = before(h)
            else:
                old, old_sum, old_acc = (ref[h] for ref in after)
            top = jnp.maximum(old, jnp.max(s, axis=1, keepdims=True))
            fade = jnp.exp2(old - top)
            w = jnp.exp2(s - jnp.concatenate([top, top], axis=1)).astype(BF16)
            got = jnp.dot(w, values, preferred_element_type=F32)
            after[0][h] = top
            after[1][h] = fade * old_sum + got[:, HD:]
            after[2][h] = fade * old_acc + got[:, :HD]


def parts(src):
    return [src[i * UNIT : (i + 1) * UNIT, :] for i in range(src.shape[0] // UNIT)]


def near_body(qs, unit, r1, r2, m_s, l_s, acc):
    tags, q_tag = tags_of(unit)
    rows = lax.broadcasted_iota(jnp.int32, (CHIP, CHIP), 0)
    cols = lax.broadcasted_iota(jnp.int32, (CHIP, CHIP), 1)
    bias = jnp.where((tags[0:1, :] == q_tag) & (cols <= rows), 0.0, -1e30)
    keys, values = unit[:CHIP, :HD], with_ones(unit[:CHIP, HD:])
    for h in range(qs.shape[0]):
        s = lax.dot_general(qs[h], keys, CONTRACT, preferred_element_type=F32)
        s = s * SCALE + bias
        top = jnp.max(s, axis=1, keepdims=True)
        got = jnp.dot(jnp.exp2(s - top).astype(BF16), values, preferred_element_type=F32)
        m_s[h] = jnp.broadcast_to(top, (CHIP, HD))
        l_s[h] = got[:, HD:]
        acc[h] = got[:, :HD]
    state = (m_s, l_s, acc)
    units = [src[...] for src in (r1, r2)]
    add_units(lambda h: qs[h], units, NEAR, q_tag, lambda h: [ref[h] for ref in state], state)


def attend_near(qs, unit, r1, r2):
    heads = qs.shape[0]
    state = like(heads, CHIP, HD, dtype=F32)
    return call(
        near_body, "attend_near", (state, state, state), [VMEM] * 4, (VMEM,) * 3, limit=8,
        flops=12 * heads * CHIP * CHIP * HD, exps=3 * heads * CHIP * CHIP,
    )(qs, unit, r1, r2)


def early_body(qs, m_in, l_in, acc_in, unit, far_b, m_s, l_s, acc):
    before = (m_in, l_in, acc_in)
    add_units(
        lambda h: qs[h], parts(far_b), EARLY, tags_of(unit)[1],
        lambda h: [ref[h] for ref in before], (m_s, l_s, acc),
    )


def attend_early(qs, m_in, l_in, acc_in, unit, far_b):
    heads = qs.shape[0]
    state = like(heads, CHIP, HD, dtype=F32)
    return call(
        early_body, "attend_early", (state,) * 3, [VMEM] * 6, (VMEM,) * 3, limit=8,
        flops=64 * heads * CHIP * CHIP * HD, exps=2 * heads * CHIP * CHIP,
    )(qs, m_in, l_in, acc_in, unit, far_b)


def middle_body(qs, m_in, l_in, acc_in, unit, r3, r4, far_c, m_s, l_s, acc):
    before = (m_in, l_in, acc_in)
    even = core_index() == 0
    third, fourth = parts(far_c)
    units = [jnp.where(even, r3[...], third), jnp.where(even, r4[...], fourth)]
    add_units(
        lambda h: qs[h], units, MIDDLE, tags_of(unit)[1],
        lambda h: [ref[h] for ref in before], (m_s, l_s, acc),
    )


def attend_middle(qs, m_in, l_in, acc_in, unit, r3, r4, far_c):
    heads = qs.shape[0]
    state = like(heads, CHIP, HD, dtype=F32)
    return call(
        middle_body, "attend_middle", (state,) * 3, [VMEM] * 8, (VMEM,) * 3, limit=8,
        flops=8 * heads * CHIP * CHIP * HD, exps=2 * heads * CHIP * CHIP,
    )(qs, m_in, l_in, acc_in, unit, r3, r4, far_c)


def attend_last(side, qs, m_in, l_in, acc_in, unit, far_a):
    heads = qs.shape[0]

    def body(qs, m_in, l_in, acc_in, unit, far_a, out, tag_s, m_s, l_s, acc):
        rows = halves()[side]
        before = (m_in, l_in, acc_in)
        tag_s[...] = jnp.broadcast_to(tags_of(unit)[1], (CHIP, HD))
        add_units(
            lambda h: qs[h, rows, :], parts(far_a), LAST, tag_s[rows, :][:, 0:1],
            lambda h: [ref[h, rows, :] for ref in before], (m_s, l_s, acc),
        )
        for h in range(heads):
            out[:, h * HD : (h + 1) * HD] = (acc[h] / l_s[h]).astype(BF16)

    state = pltpu.VMEM((heads, ROWS, HD), F32)
    return call(
        body, "attend_last", like(ROWS, heads * HD), [VMEM] * 6, VMEM,
        [pltpu.VMEM((CHIP, HD), F32), state, state, state],
        limit=8, flops=4 * heads * ROWS * 3 * CHIP * HD, exps=heads * ROWS * 3 * CHIP,
    )(qs, m_in, l_in, acc_in, unit, far_a)


def project_out(xm, xr, w_out, groups, parts, dtype):
    depth = xm.shape[1]
    width = w_out.shape[1] // groups
    half = width // 2

    def body(xm, xr, w, *outs):
        core = core_index()
        own = pl.ds(pl.multiple_of(core * depth, depth), depth)
        other = pl.ds(pl.multiple_of((1 - core) * depth, depth), depth)
        for (shift, side), out in zip(parts, outs):
            group = lax.rem(lax.axis_index("head") + shift, groups)
            cols = pl.ds(pl.multiple_of(group * width + side * half, half), half)
            got = jnp.dot(xm[...], w[own, cols], preferred_element_type=F32)
            got += jnp.dot(xr[...], w[other, cols], preferred_element_type=F32)
            out[...] = got.astype(dtype)

    return call(
        body, "project_out", (like(ROWS, half, dtype=dtype),) * len(parts), [VMEM] * 3,
        (VMEM,) * len(parts), limit=4,
        flops=2 * ROWS * 2 * depth * half * len(parts), moved=len(parts),
    )(xm, xr, w_out)


def add_body(a, b, p, q, out_a, out_b):
    out_a[...] = (a[...] + p[...].astype(F32)).astype(BF16)
    out_b[...] = (b[...] + q[...].astype(F32)).astype(BF16)


def add_passing(a, b, p, q):
    out = like(*p.shape)
    return call(add_body, "add_passing", (out, out), [VMEM] * 4, (VMEM,) * 2, limit=2)(a, b, p, q)


def total_body(own_a, own_b, left_a, left_b, right_a, right_b, out):
    half = own_a.shape[1]
    for at, pieces in ((0, (own_a, left_a, right_a)), (half, (own_b, left_b, right_b))):
        total = pieces[0][...] + pieces[1][...].astype(F32) + pieces[2][...].astype(F32)
        out[:, at : at + half] = total.astype(BF16)


def add_total(*pieces):
    rows, half = pieces[0].shape
    return call(total_body, "add_total", like(rows, 2 * half), [VMEM] * 6, VMEM, limit=2)(*pieces)


def shards(tokens, w_query, w_key, w_value, w_out, doc_ids):
    ranks = lax.axis_size("ctx")
    groups = lax.axis_size("head")
    table = jnp.asarray(rope_table(ranks * ROWS))

    def swap(value):
        return lax.ppermute(value, "ctx", [(r, r ^ 1) for r in range(ranks)])

    def along(value, even, odd):
        moves = []
        for r in range(ranks):
            step = odd if r % 2 else even
            if step is not None:
                moves.append((r, 2 * step(r // 2) + r % 2))
        return lax.ppermute(value, "ctx", moves)

    def ahead(step):
        return lambda chip: (chip + step) % (ranks // 2)

    def in_row(step):
        return lambda chip: chip // 4 * 4 + (chip + step) % 4

    docs = doc_ids.reshape(1, -1)
    came, docs_came = swap(tokens), swap(docs)
    tokens, w_key, w_value, table, docs = (
        pltpu.with_memory_space_constraint(a, pltpu.HBM)
        for a in (tokens, w_key, w_value, table, docs)
    )
    half, tokens, w_kv, docs, table = project_own(tokens, w_key, w_value, docs, table)
    unit = project_unit(half, came, w_kv, docs, docs_came, table)
    r1 = along(unit, ahead(1), ahead(4))
    r2 = along(unit, ahead(2), ahead(8))
    r3 = along(unit, ahead(3), ahead(12))
    r4 = along(unit, ahead(4), in_row(3))
    r1, r2, came = lax.optimization_barrier((r1, r2, came))
    out_a = bundle_row(unit, r1, r2, r3, r4)
    far_b = along(bundle_pair(unit, r1, r2, 2, out_a), ahead(8), in_row(2))
    far_a = along(out_a, ahead(4), in_row(1))
    far_c = along(bundle_pair(unit, r1, r2, 1, out_a), None, in_row(3))
    qs = project_q(tokens, came, w_query, table)
    state = attend_near(qs, unit, r1, r2)
    state = attend_middle(qs, *state, unit, r3, r4, far_c)
    state = attend_early(qs, *state, unit, far_a)
    xr = swap(attend_last(1, qs, *state, unit, far_b))
    xm = attend_last(0, qs, *state, unit, far_b)

    def shift(value, step):
        return lax.ppermute(value, "head", [(g, (g + step) % groups) for g in range(groups)])

    a2, b2 = project_out(xm, xr, w_out, groups, ((2, 0), (2, 1)), BF16)
    pass_a, pass_b = shift(a2, 1), shift(b2, -1)
    b1, a3 = project_out(xm, xr, w_out, groups, ((1, 1), (3, 0)), BF16)
    left_b, right_a = shift(b1, 1), shift(a3, -1)
    a1, b3, a0, b0 = project_out(xm, xr, w_out, groups, ((1, 0), (3, 1), (0, 0), (0, 1)), F32)
    a1, b3 = add_passing(a1, b3, pass_a, pass_b)
    left_a, right_b = shift(a1, 1), shift(b3, -1)
    return add_total(a0, b0, left_a, left_b, right_a, right_b)


def solution(mesh):
    return jax.shard_map(
        shards,
        mesh=mesh,
        in_specs=(
            P("ctx", None),
            P(None, "head"),
            P(None, "head"),
            P(None, "head"),
            P("head", None),
            P("ctx"),
        ),
        out_specs=P("ctx", "head"),
        check_vma=False,
    )
```

```python
import math

import jax
import jax.numpy as jnp
import numpy as np
from jax import lax
from jax.experimental import pallas as pl
from jax.experimental.pallas import tpu as pltpu
from jax.sharding import PartitionSpec as P

HD = 128
ROWS = 128
UNIT = 264
F32 = jnp.float32
BF16 = jnp.bfloat16
MIB = 1 << 20
SCALE = math.log2(math.e) / math.sqrt(HD)


def rope_table(count):
    half = HD // 2
    freqs = 500000.0 ** (-2.0 * np.arange(half, dtype=np.float64) / HD)
    angles = np.arange(count, dtype=np.float64)[:, None] * freqs[None, :]
    return np.concatenate([np.cos(angles), np.sin(angles)], axis=1).astype(np.float32)


def rotation(table):
    half = HD // 2
    cosine, sine = table[:, :half], table[:, half:]
    cosine = jnp.concatenate([cosine, cosine], axis=1)
    sine = jnp.concatenate([-sine, sine], axis=1)
    return lambda t: t * cosine + pltpu.roll(t, half, 1) * sine


SMEM = pl.BlockSpec(memory_space=pltpu.SMEM)
VMEM = pl.BlockSpec(memory_space=pltpu.VMEM)
HBM = pl.BlockSpec(memory_space=pltpu.HBM)


def like(*dims, dtype=BF16):
    return jax.ShapeDtypeStruct(dims, dtype)


def call(body, name, out, ins, outs, scratch=(), limit=4, flops=0, moved=1, exps=0):
    return pl.pallas_call(
        body,
        out_shape=out,
        in_specs=ins,
        out_specs=outs,
        scratch_shapes=list(scratch),
        name=name,
        cost_estimate=pl.CostEstimate(
            flops=flops, bytes_accessed=moved * MIB, transcendentals=exps
        ),
        compiler_params=pltpu.CompilerParams(vmem_limit_bytes=limit * MIB),
    )


def core_index():
    return lax.rem(lax.axis_index("ctx"), 2)


def table_rows(table):
    return table.at[pl.ds(pl.multiple_of(lax.axis_index("ctx") * ROWS, ROWS), ROWS), :]


def started(copies):
    for copy in copies:
        copy.start()
    return copies


KV_PARTS = 4
CHIP = 2 * ROWS


def halves():
    core = core_index()
    own = pl.ds(pl.multiple_of(core * ROWS, ROWS), ROWS)
    other = pl.ds(pl.multiple_of((1 - core) * ROWS, ROWS), ROWS)
    return own, other


def own_body(tok, wk, wv, docs, table, half, tok_s, w_s, docs_s, table_s, acc, sems):
    part = tok.shape[1] // KV_PARTS
    cols = pl.ds(pl.multiple_of(core_index() * HD, HD), HD)
    copies = []
    for i in range(KV_PARTS):
        cut = pl.ds(i * part, part)
        copies.append(
            started([
                pltpu.make_async_copy(tok.at[:, cut], tok_s.at[:, cut], sems.at[3 * i]),
                pltpu.make_async_copy(
                    wk.at[cut, cols], w_s.at[cut, pl.ds(0, HD)], sems.at[3 * i + 1]
                ),
                pltpu.make_async_copy(
                    wv.at[cut, cols], w_s.at[cut, pl.ds(HD, HD)], sems.at[3 * i + 2]
                ),
            ])
        )
    first = pl.multiple_of(lax.div(lax.axis_index("ctx"), 2) * CHIP, CHIP)
    small = started([
        pltpu.make_async_copy(docs, docs_s, sems.at[3 * KV_PARTS]),
        pltpu.make_async_copy(table.at[pl.ds(first, CHIP), :], table_s, sems.at[3 * KV_PARTS + 1]),
    ])
    for i, group in enumerate(copies):
        for copy in group:
            copy.wait()
        cut = slice(i * part, (i + 1) * part)
        more = jnp.dot(tok_s[:, cut], w_s[cut, :], preferred_element_type=F32)
        if i == 0:
            acc[...] = more
        else:
            acc[...] += more
    for copy in small:
        copy.wait()
    rot = rotation(table_s[halves()[0], :])
    half[:, :HD] = rot(acc[:, :HD]).astype(BF16)
    half[:, HD:] = acc[:, HD:].astype(BF16)


def project_own(tokens, w_key, w_value, docs, table):
    depth = tokens.shape[1]
    return call(
        own_body, "project_own",
        (
            like(ROWS, 2 * HD),
            like(ROWS, depth),
            like(depth, 2 * HD),
            like(1, ROWS, dtype=jnp.int32),
            like(CHIP, HD, dtype=F32),
        ),
        [HBM] * 5, (VMEM,) * 5,
        [pltpu.VMEM((ROWS, 2 * HD), F32), pltpu.SemaphoreType.DMA((3 * KV_PARTS + 2,))],
        limit=6, flops=2 * ROWS * depth * 2 * HD, moved=3,
    )(tokens, w_key, w_value, docs, table)


def unit_body(half, came, w, docs, docs_came, table, unit):
    own, other = halves()
    got = jnp.dot(came[...], w[...], preferred_element_type=F32)
    unit[own, :] = half[...]
    unit[other, :HD] = rotation(table[other, :])(got[:, :HD]).astype(BF16)
    unit[other, HD:] = got[:, HD:].astype(BF16)
    first = core_index() == 0
    a, b = docs[...], docs_came[...]
    tags = jnp.concatenate([jnp.where(first, a, b), jnp.where(first, b, a)], axis=1)
    tags = (tags + 1).astype(F32)
    unit[CHIP:, :] = jnp.broadcast_to(tags, (8, CHIP)).astype(BF16)


def project_unit(half, came, w, docs, docs_came, table):
    return call(
        unit_body, "project_unit", like(UNIT, 2 * HD), [VMEM] * 6, VMEM, limit=2,
        flops=2 * ROWS * w.shape[0] * 2 * HD,
    )(half, came, w, docs, docs_came, table)


def q_body(tok, came, wq, table, out):
    half = wq.shape[1] // 2
    cols = pl.ds(pl.multiple_of(core_index() * half, half), half)
    for span, src in zip(halves(), (tok, came)):
        got = jnp.dot(src[...], wq[:, cols], preferred_element_type=F32)
        rot = rotation(table[span, :])
        for h in range(half // HD):
            out[h, span, :] = rot(got[:, h * HD : (h + 1) * HD]).astype(BF16)


def project_q(tokens, came, w_query, table):
    depth, width = w_query.shape
    return call(
        q_body, "project_q", like(width // 2 // HD, CHIP, HD), [VMEM] * 4, VMEM,
        limit=4, flops=2 * CHIP * depth * width // 2, moved=6,
    )(tokens, came, w_query, table)


NONE = 99
NEAR = ((1, 2), (4, 8))
EARLY = ((8, 9), (2, 6))
MIDDLE = ((3, 4), (3, 7))
LAST = ((5, 6, 7), (1, 5, 9))


def fill(out, slots, late, even):
    place = lax.axis_index("ctx")
    column = lax.rem(lax.div(place, 2), 4)
    skip = jnp.where(lax.rem(place, 2) == 0, even, jnp.where(column >= late, 1, 0))
    for i in range(out.shape[0] // UNIT):
        out[i * UNIT : (i + 1) * UNIT, :] = slots[skip + i]


def pairs_body(unit, r1, r2, out_b, out_c, slots):
    for i, src in enumerate((unit, r1, r2)):
        slots[i] = src[...]
    fill(out_b, slots, 2, 0)
    fill(out_c, slots, 1, 0)


def bundle_pairs(unit, r1, r2):
    pair = like(2 * UNIT, 2 * HD)
    return call(
        pairs_body, "bundle_pairs", (pair, pair), [VMEM] * 3, (VMEM,) * 2,
        [pltpu.VMEM((3, UNIT, 2 * HD), BF16)], limit=2,
    )(unit, r1, r2)


def row_body(unit, r1, r2, r3, after, out_a, slots):
    for i, src in enumerate((unit, r1, r2, r3)):
        slots[i] = src[...]
    fill(out_a, slots, 3, 1)


def bundle_row(unit, r1, r2, r3, after):
    return call(
        row_body, "bundle_row", like(3 * UNIT, 2 * HD), [VMEM] * 5, VMEM,
        [pltpu.VMEM((4, UNIT, 2 * HD), BF16)], limit=2,
    )(unit, r1, r2, r3, after)


CONTRACT = (((1,), (1,)), ((), ()))


def tags_of(unit):
    tags = unit[CHIP:UNIT, :].astype(F32)
    return tags, jnp.transpose(tags, (1, 0))[:, 0:1]


def with_ones(values):
    return jnp.concatenate([values, jnp.ones((CHIP, HD), BF16)], axis=1)


def add_units(queries, units, steps, q_tag, before, after):
    place = lax.axis_index("ctx")
    odd = lax.rem(place, 2) == 1
    chip = lax.div(place, 2)
    for i, (block, even_step, odd_step) in enumerate(zip(units, *steps)):
        valid = chip >= jnp.where(odd, odd_step, even_step)
        k_tag = block[CHIP:, :].astype(F32)[0:1, :]
        bias = jnp.where((k_tag == q_tag) & valid, 0.0, -1e30)
        keys = block[:CHIP, :HD]
        values = with_ones(block[:CHIP, HD:])
        for h in range(after[0].shape[0]):
            s = lax.dot_general(queries(h), keys, CONTRACT, preferred_element_type=F32)
            s = s * SCALE + bias
            if i == 0:
                old, old_sum, old_acc = before(h)
            else:
                old, old_sum, old_acc = (ref[h] for ref in after)
            top = jnp.maximum(old, jnp.max(s, axis=1, keepdims=True))
            fade = jnp.exp2(old - top)
            w = jnp.exp2(s - jnp.concatenate([top, top], axis=1)).astype(BF16)
            got = jnp.dot(w, values, preferred_element_type=F32)
            after[0][h] = top
            after[1][h] = fade * old_sum + got[:, HD:]
            after[2][h] = fade * old_acc + got[:, :HD]


def parts(src):
    return [src[i * UNIT : (i + 1) * UNIT, :] for i in range(src.shape[0] // UNIT)]


def near_body(qs, unit, r1, r2, m_s, l_s, acc):
    tags, q_tag = tags_of(unit)
    rows = lax.broadcasted_iota(jnp.int32, (CHIP, CHIP), 0)
    cols = lax.broadcasted_iota(jnp.int32, (CHIP, CHIP), 1)
    bias = jnp.where((tags[0:1, :] == q_tag) & (cols <= rows), 0.0, -1e30)
    keys, values = unit[:CHIP, :HD], with_ones(unit[:CHIP, HD:])
    for h in range(qs.shape[0]):
        s = lax.dot_general(qs[h], keys, CONTRACT, preferred_element_type=F32)
        s = s * SCALE + bias
        top = jnp.max(s, axis=1, keepdims=True)
        got = jnp.dot(jnp.exp2(s - top).astype(BF16), values, preferred_element_type=F32)
        m_s[h] = jnp.broadcast_to(top, (CHIP, HD))
        l_s[h] = got[:, HD:]
        acc[h] = got[:, :HD]
    state = (m_s, l_s, acc)
    units = [src[...] for src in (r1, r2)]
    add_units(lambda h: qs[h], units, NEAR, q_tag, lambda h: [ref[h] for ref in state], state)


def attend_near(qs, unit, r1, r2):
    heads = qs.shape[0]
    state = like(heads, CHIP, HD, dtype=F32)
    return call(
        near_body, "attend_near", (state, state, state), [VMEM] * 4, (VMEM,) * 3, limit=8,
        flops=12 * heads * CHIP * CHIP * HD, exps=3 * heads * CHIP * CHIP,
    )(qs, unit, r1, r2)


def early_body(qs, m_in, l_in, acc_in, unit, far_b, m_s, l_s, acc):
    before = (m_in, l_in, acc_in)
    add_units(
        lambda h: qs[h], parts(far_b), EARLY, tags_of(unit)[1],
        lambda h: [ref[h] for ref in before], (m_s, l_s, acc),
    )


def attend_early(qs, m_in, l_in, acc_in, unit, far_b):
    heads = qs.shape[0]
    state = like(heads, CHIP, HD, dtype=F32)
    return call(
        early_body, "attend_early", (state,) * 3, [VMEM] * 6, (VMEM,) * 3, limit=8,
        flops=64 * heads * CHIP * CHIP * HD, exps=2 * heads * CHIP * CHIP,
    )(qs, m_in, l_in, acc_in, unit, far_b)


def middle_body(qs, m_in, l_in, acc_in, unit, r3, r4, far_c, m_s, l_s, acc):
    before = (m_in, l_in, acc_in)
    even = core_index() == 0
    third, fourth = parts(far_c)
    units = [jnp.where(even, r3[...], third), jnp.where(even, r4[...], fourth)]
    add_units(
        lambda h: qs[h], units, MIDDLE, tags_of(unit)[1],
        lambda h: [ref[h] for ref in before], (m_s, l_s, acc),
    )


def attend_middle(qs, m_in, l_in, acc_in, unit, r3, r4, far_c):
    heads = qs.shape[0]
    state = like(heads, CHIP, HD, dtype=F32)
    return call(
        middle_body, "attend_middle", (state,) * 3, [VMEM] * 8, (VMEM,) * 3, limit=8,
        flops=64 * heads * CHIP * CHIP * HD, exps=2 * heads * CHIP * CHIP,
    )(qs, m_in, l_in, acc_in, unit, r3, r4, far_c)


def attend_last(side, qs, m_in, l_in, acc_in, unit, far_a):
    heads = qs.shape[0]

    def body(qs, m_in, l_in, acc_in, unit, far_a, out, tag_s, m_s, l_s, acc):
        rows = halves()[side]
        before = (m_in, l_in, acc_in)
        tag_s[...] = jnp.broadcast_to(tags_of(unit)[1], (CHIP, HD))
        add_units(
            lambda h: qs[h, rows, :], parts(far_a), LAST, tag_s[rows, :][:, 0:1],
            lambda h: [ref[h, rows, :] for ref in before], (m_s, l_s, acc),
        )
        for h in range(heads):
            out[:, h * HD : (h + 1) * HD] = (acc[h] / l_s[h]).astype(BF16)

    state = pltpu.VMEM((heads, ROWS, HD), F32)
    return call(
        body, "attend_last", like(ROWS, heads * HD), [VMEM] * 6, VMEM,
        [pltpu.VMEM((CHIP, HD), F32), state, state, state],
        limit=8, flops=4 * heads * ROWS * 3 * CHIP * HD, exps=heads * ROWS * 3 * CHIP,
    )(qs, m_in, l_in, acc_in, unit, far_a)


def project_out(xm, xr, w_out, groups, parts, dtype):
    depth = xm.shape[1]
    width = w_out.shape[1] // groups
    half = width // 2

    def body(xm, xr, w, *outs):
        core = core_index()
        own = pl.ds(pl.multiple_of(core * depth, depth), depth)
        other = pl.ds(pl.multiple_of((1 - core) * depth, depth), depth)
        for (shift, side), out in zip(parts, outs):
            group = lax.rem(lax.axis_index("head") + shift, groups)
            cols = pl.ds(pl.multiple_of(group * width + side * half, half), half)
            got = jnp.dot(xm[...], w[own, cols], preferred_element_type=F32)
            got += jnp.dot(xr[...], w[other, cols], preferred_element_type=F32)
            out[...] = got.astype(dtype)

    return call(
        body, "project_out", (like(ROWS, half, dtype=dtype),) * len(parts), [VMEM] * 3,
        (VMEM,) * len(parts), limit=4,
        flops=2 * ROWS * 2 * depth * half * len(parts), moved=len(parts),
    )(xm, xr, w_out)


def add_body(a, b, p, q, out_a, out_b):
    out_a[...] = (a[...] + p[...].astype(F32)).astype(BF16)
    out_b[...] = (b[...] + q[...].astype(F32)).astype(BF16)


def add_passing(a, b, p, q):
    out = like(*p.shape)
    return call(add_body, "add_passing", (out, out), [VMEM] * 4, (VMEM,) * 2, limit=2)(a, b, p, q)


def total_body(own_a, own_b, left_a, left_b, right_a, right_b, out):
    half = own_a.shape[1]
    for at, pieces in ((0, (own_a, left_a, right_a)), (half, (own_b, left_b, right_b))):
        total = pieces[0][...] + pieces[1][...].astype(F32) + pieces[2][...].astype(F32)
        out[:, at : at + half] = total.astype(BF16)


def add_total(*pieces):
    rows, half = pieces[0].shape
    return call(total_body, "add_total", like(rows, 2 * half), [VMEM] * 6, VMEM, limit=2)(*pieces)


def shards(tokens, w_query, w_key, w_value, w_out, doc_ids):
    ranks = lax.axis_size("ctx")
    groups = lax.axis_size("head")
    table = jnp.asarray(rope_table(ranks * ROWS))

    def swap(value):
        return lax.ppermute(value, "ctx", [(r, r ^ 1) for r in range(ranks)])

    def along(value, even, odd):
        moves = [(r, 2 * (odd if r % 2 else even)(r // 2) + r % 2) for r in range(ranks)]
        return lax.ppermute(value, "ctx", moves)

    def ahead(step):
        return lambda chip: (chip + step) % (ranks // 2)

    def in_row(step):
        return lambda chip: chip // 4 * 4 + (chip + step) % 4

    docs = doc_ids.reshape(1, -1)
    came, docs_came = swap(tokens), swap(docs)
    tokens, w_key, w_value, table, docs = (
        pltpu.with_memory_space_constraint(a, pltpu.HBM)
        for a in (tokens, w_key, w_value, table, docs)
    )
    half, tokens, w_kv, docs, table = project_own(tokens, w_key, w_value, docs, table)
    unit = project_unit(half, came, w_kv, docs, docs_came, table)
    r1 = along(unit, ahead(1), ahead(4))
    r2 = along(unit, ahead(2), ahead(8))
    r3 = along(unit, ahead(3), ahead(12))
    r4 = along(unit, ahead(4), in_row(3))
    r1, r2, came = lax.optimization_barrier((r1, r2, came))
    out_b, out_c = bundle_pairs(unit, r1, r2)
    far_b = along(out_b, ahead(8), in_row(2))
    far_c = along(out_c, ahead(12), in_row(3))
    far_a = along(bundle_row(unit, r1, r2, r3, r4), ahead(4), in_row(1))
    qs = project_q(tokens, came, w_query, table)
    state = attend_near(qs, unit, r1, r2)
    state = attend_early(qs, *state, unit, far_b)
    state = attend_middle(qs, *state, unit, r3, r4, far_c)
    xr = swap(attend_last(1, qs, *state, unit, far_a))
    xm = attend_last(0, qs, *state, unit, far_a)

    def shift(value, step):
        return lax.ppermute(value, "head", [(g, (g + step) % groups) for g in range(groups)])

    a2, b2 = project_out(xm, xr, w_out, groups, ((2, 0), (2, 1)), BF16)
    pass_a, pass_b = shift(a2, 1), shift(b2, -1)
    b1, a3 = project_out(xm, xr, w_out, groups, ((1, 1), (3, 0)), BF16)
    left_b, right_a = shift(b1, 1), shift(a3, -1)
    a1, b3, a0, b0 = project_out(xm, xr, w_out, groups, ((1, 0), (3, 1), (0, 0), (0, 1)), F32)
    a1, b3 = add_passing(a1, b3, pass_a, pass_b)
    left_a, right_b = shift(a1, 1), shift(b3, -1)
    return add_total(a0, b0, left_a, left_b, right_a, right_b)


def solution(mesh):
    return jax.shard_map(
        shards,
        mesh=mesh,
        in_specs=(
            P("ctx", None),
            P(None, "head"),
            P(None, "head"),
            P(None, "head"),
            P("head", None),
            P("ctx"),
        ),
        out_specs=P("ctx", "head"),
        check_vma=False,
    )
```
